32 devices in a mesh: dp: 8 (over z, x), seq: 4 (over y, core).
Axes of the slice: x: 2, y: 2, z: 4, core: 2. Of those that a mesh axis runs over, the one named last changes fastest.
Arguments:
- tokens: bfloat16 [32, 512, 768], P('dp', 'seq'), may hold values from -6 to 6
- memory_init: bfloat16 [768, 10], replicated, may hold values from -6 to 6
- query_weight: bfloat16 [768, 768], replicated, may hold values from -0.21875 to 0.21875
- query_bias: bfloat16 [768], replicated, may hold values from -3 to 3
- key_weight: bfloat16 [768, 768], replicated, may hold values from -0.21875 to 0.21875
- value_weight: bfloat16 [768, 768], replicated, may hold values from -0.21875 to 0.21875
- value_bias: bfloat16 [768], replicated, may hold values from -3 to 3
- output_weight: bfloat16 [768, 768], replicated, may hold values from -1.75 to 1.75
- output_bias: bfloat16 [768], replicated, may hold values from -3 to 3
- attn_gain: bfloat16 [768], replicated, may hold values from 0.5 to 1.5
- attn_shift: bfloat16 [768], replicated, may hold values from -3 to 3
- inner_weight: bfloat16 [768, 3072], replicated, may hold values from -0.21875 to 0.21875
- inner_bias: bfloat16 [3072], replicated, may hold values from -3 to 3
- outer_weight: bfloat16 [3072, 768], replicated, may hold values from -0.109375 to 0.109375
- outer_bias: bfloat16 [768], replicated, may hold values from -3 to 3
- ffn_gain: bfloat16 [768], replicated, may hold values from 0.5 to 1.5
- ffn_shift: bfloat16 [768], replicated, may hold values from -3 to 3
- out_grad: bfloat16 [32, 512, 768], P('dp', 'seq'), may hold values from -6 to 6
- lm_mask: int32 [32, 512], P('dp', 'seq'), may hold values from 0 to 1, as said below
- doc_segments: int32 [8], replicated, may hold values from 1 to 8, 32 in all
Outputs:
- layer_out: bfloat16 [32, 512, 768], P('dp', 'seq')
- tokens_grad: float32 [32, 512, 768], P('dp', 'seq')
- query_weight_grad: float32 [768, 768], P('dp')
- query_bias_grad: float32 [768], P('dp')
- key_weight_grad: float32 [768, 768], P('dp')
- value_weight_grad: float32 [768, 768], P('dp')
- value_bias_grad: float32 [768], P('dp')
- output_weight_grad: float32 [768, 768], P('dp')
- output_bias_grad: float32 [768], P('dp')
- attn_gain_grad: float32 [768], P('dp')
- attn_shift_grad: float32 [768], P('dp')
- inner_weight_grad: float32 [768, 3072], P('dp')
- inner_bias_grad: float32 [3072], P('dp')
- outer_weight_grad: float32 [3072, 768], P('dp')
- outer_bias_grad: float32 [768], P('dp')
- ffn_gain_grad: float32 [768], P('dp')
- ffn_shift_grad: float32 [768], P('dp')
- memory_init_grad: float32 [768, 10], P('dp')
The draws below stay inside these ranges and needn't reach their ends.
Inputs may be any that keep to these rules, and one draw needn't show every extreme that they name: `lm_mask`: 1 marks a masked position; the share of ones rises along the segments; some whole segments have no ones.
All inputs are finite; a program needn't handle non-finite values.
Results may differ from the reference program's by a relative error of at most 0.014.
Values may be sent and summed in bfloat16 or wider, within the bound.
No kernel may reach another device: no remote copies, remote signals or barrier semaphores. Data moves between devices by JAX's collectives and lax.ppermute only.
A program may use at most 192 MiB of HBM per device.

```python
import math
import jax
import jax.numpy as jnp
import numpy as np
from jax import lax

D = 768
HEADS = 12
HEAD_DIM = 64
FF = 3072
MEM = 10
ROWS = 512
SEGS = 32
DOCS = 8


def draw_lm_mask(key, part):
    key_ticket = jax.random.fold_in(key, 11)
    key_skip = jax.random.fold_in(key, 23)
    segment = jnp.arange(SEGS, dtype=jnp.int32)[:, None]
    threshold = 80 + 160 * segment // max(SEGS - 1, 1)
    ticket = jax.random.randint(key_ticket, (SEGS, ROWS), 0, 1000, dtype=jnp.int32)
    offset = jax.random.randint(key_skip, (), 0, 8, dtype=jnp.int32)
    keep = ((segment + offset) % 8 != 0).astype(jnp.int32)
    return (ticket < threshold).astype(jnp.int32) * keep


def shard_levels(stream_key, dims, cuts, low, top_value):
    level = 1.0
    for dim, parts in cuts:
        heights = jax.random.uniform(jax.random.fold_in(jax.random.fold_in(stream_key, 6), dim), (parts,), jnp.float32, low / len(cuts), top_value / len(cuts))
        level = level * jnp.repeat(jnp.exp(heights), dims[dim] // parts).reshape((-1,) + (1,) * (len(dims) - 1 - dim))
    return level


def length_profile(amount, total, limit, lean):
    loads = [(1 << 20) // math.isqrt(grade ** lean) + 1 for grade in range(2, amount + 1)]
    surplus, holding = total - limit - (amount - 1), [1] * (amount - 1)
    while surplus > 0:
        candidates = [i for i in range(amount - 1) if holding[i] < limit]
        whole, remaining = sum([loads[i] for i in candidates]), surplus
        for i in candidates:
            addition = min(limit - holding[i], max(1, remaining * loads[i] // whole), surplus)
            holding[i] = holding[i] + addition
            surplus = surplus - addition
    return np.array([limit] + holding)


def uneven_parts(rng, amount, total, bound, skew):
    if amount == 2:
        one = jax.random.randint(rng, (), max(1, total - bound), min(bound, total - 1) + 1)
        return jnp.stack([one, total - one])
    lengths = jnp.asarray(length_profile(amount, total, bound, skew), jnp.int32)
    couples = (amount - 1) // 2
    source_of, receiver = lengths[1:1 + 2 * couples:2], lengths[2:2 + 2 * couples:2]
    slack = jnp.minimum(source_of - 1, bound - receiver)
    passed = jax.random.randint(jax.random.fold_in(rng, 1), (couples,), 0, 1 << 20) % (slack + 1)
    lengths = lengths.at[1:1 + 2 * couples:2].set(source_of - passed).at[2:2 + 2 * couples:2].set(receiver + passed)
    return lengths[jax.random.permutation(jax.random.fold_in(rng, 2), amount)]


def scatter_about(own_key, shape, scale, reach, split=(), kind=jnp.bfloat16):
    array = scale * jax.random.normal(own_key, shape, jnp.float32)
    if split:
        array = array * shard_levels(own_key, shape, split, -0.22, 0.18)
    return jnp.clip(array, -reach, reach).astype(kind)


def setup_inputs(seed: int = 0) -> dict:
    streams_of = jax.random.split(jax.random.key(seed), 21)
    return {
        "tokens": scatter_about(streams_of[0], (SEGS, ROWS, D), 1.0, 6.0, ((0, 8), (1, 4))),
        "memory_init": scatter_about(streams_of[1], (D, MEM), 1.0, 6.0),
        "query_weight": scatter_about(streams_of[2], (D, D), D ** -0.5, 0.21875),
        "query_bias": scatter_about(streams_of[3], (D,), 0.5, 3.0),
        "key_weight": scatter_about(streams_of[4], (D, D), D ** -0.5, 0.21875),
        "value_weight": scatter_about(streams_of[5], (D, D), D ** -0.5, 0.21875),
        "value_bias": scatter_about(streams_of[6], (D,), 0.5, 3.0),
        "output_weight": scatter_about(streams_of[7], (D, D), (max(D // 64, 1)) ** -0.5, 1.75),
        "output_bias": scatter_about(streams_of[8], (D,), 0.5, 3.0),
        "attn_gain": jnp.clip(1.0 + 0.1 * jax.random.normal(streams_of[9], (D,), jnp.float32), 0.5, 1.5).astype(jnp.bfloat16),
        "attn_shift": scatter_about(streams_of[10], (D,), 0.5, 3.0),
        "inner_weight": scatter_about(streams_of[11], (D, FF), D ** -0.5, 0.21875),
        "inner_bias": scatter_about(streams_of[12], (FF,), 0.5, 3.0),
        "outer_weight": scatter_about(streams_of[13], (FF, D), FF ** -0.5, 0.109375),
        "outer_bias": scatter_about(streams_of[14], (D,), 0.5, 3.0),
        "ffn_gain": jnp.clip(1.0 + 0.1 * jax.random.normal(streams_of[15], (D,), jnp.float32), 0.5, 1.5).astype(jnp.bfloat16),
        "ffn_shift": scatter_about(streams_of[16], (D,), 0.5, 3.0),
        "out_grad": scatter_about(streams_of[17], (SEGS, ROWS, D), 1.0, 6.0, ((0, 8), (1, 4))),
        "lm_mask": draw_lm_mask(jax.random.fold_in(streams_of[20], 71), 0),
        "doc_segments": uneven_parts(streams_of[19], DOCS, SEGS, min(8, SEGS // 2), 2).astype(jnp.int32),
    }


@jax.custom_vjp
def low(v):
    return lax.optimization_barrier(v.astype(jnp.bfloat16)).astype(jnp.float32)

@jax.custom_vjp
def low_back(v):
    return v

def low_keep(v):
    return (low(v), None)

def low_pass(kept, grad):
    return (grad,)

def back_keep(v):
    return (v, None)

def back_low(kept, grad):
    return (low(grad),)
low.defvjp(low_keep, low_pass)
low_back.defvjp(back_keep, back_low)
epsilon = 1e-06
highest = lax.Precision.HIGHEST

def layer_norm(values, gain, shift):
    center = values - lax.optimization_barrier(jnp.mean(values, axis=-1, keepdims=True))
    spread = lax.optimization_barrier(jnp.mean(center * center, axis=-1, keepdims=True))
    return center * lax.rsqrt(spread + epsilon) * gain + shift

def rounded_both(values):
    return low_back(low(values))

def project(left, right):
    return jnp.einsum('srd,de->sre', left, right, precision=highest)

def forward(params, group_tokens, select):
    query_weight, query_bias, key_weight, value_weight, value_bias, output_weight, output_bias, attn_gain, attn_shift, inner_weight, inner_bias, outer_weight, outer_bias, ffn_gain, ffn_shift, memory_init = params
    count = group_tokens.shape[0]
    memory_table = jnp.concatenate([memory_init.T, jnp.zeros((ROWS - MEM, D), memory_init.dtype)], axis=0)
    inputs = jnp.where(select[..., None], memory_table[None], group_tokens)
    queries = rounded_both(project(inputs, query_weight) + query_bias)
    keys = rounded_both(project(inputs, key_weight))
    values = rounded_both(project(inputs, value_weight) + value_bias)
    shape4 = (count, ROWS, HEADS, HEAD_DIM)
    scores = low_back(jnp.einsum('sqhd,skhd->shqk', queries.reshape(shape4), keys.reshape(shape4), precision=highest) * HEAD_DIM ** (-0.5))
    probs = jax.nn.softmax(scores, axis=-1)
    context = rounded_both(jnp.einsum('shqk,skhd->sqhd', low(probs), values.reshape(shape4), precision=highest)).reshape(count, ROWS, D)
    attended = low_back(project(context, output_weight) + output_bias)
    normed1 = layer_norm(inputs + attended, attn_gain, attn_shift)
    inner = low_back(project(low(normed1), inner_weight) + inner_bias)
    active = low(jax.nn.gelu(inner, approximate=False))
    outer = low_back(project(active, outer_weight) + outer_bias)
    return layer_norm(normed1 + outer, ffn_gain, ffn_shift)

def reference(tokens, memory_init, query_weight, query_bias, key_weight, value_weight, value_bias, output_weight, output_bias, attn_gain, attn_shift, inner_weight, inner_bias, outer_weight, outer_bias, ffn_gain, ffn_shift, out_grad, lm_mask, doc_segments):
    row_index = jnp.arange(ROWS, dtype=jnp.int32)
    valid = lm_mask * (row_index >= MEM).astype(jnp.int32)[None, :]
    seg_counts = lax.optimization_barrier(jnp.sum(valid, axis=1))
    total = jnp.sum(seg_counts)
    weight = total.astype(jnp.float32) / SEGS / jnp.maximum(seg_counts, 1).astype(jnp.float32)
    cotangent = out_grad.astype(jnp.float32) * valid.astype(jnp.float32)[..., None] * weight[:, None, None]
    starts = jnp.cumsum(doc_segments) - doc_segments
    is_first = jnp.any(starts[None, :] == jnp.arange(SEGS, dtype=jnp.int32)[:, None], axis=1)
    select = is_first[:, None] & (row_index < MEM)[None, :]
    params = tuple((item.astype(jnp.float32) for item in (query_weight, query_bias, key_weight, value_weight, value_bias, output_weight, output_bias, attn_gain, attn_shift, inner_weight, inner_bias, outer_weight, outer_bias, ffn_gain, ffn_shift, memory_init)))
    group = 8 if SEGS % 8 == 0 else 1
    steps_count = SEGS // group
    token_groups = tokens.astype(jnp.float32).reshape(steps_count, group, ROWS, D)
    cot_groups = cotangent.reshape(steps_count, group, ROWS, D)
    select_groups = select.reshape(steps_count, group, ROWS)

    def one_group(totals, pieces):
        group_tokens, group_cot, group_select = pieces
        result, pullback = jax.vjp(lambda prm, inp: forward(prm, inp, group_select), params, group_tokens)
        param_grads, token_grads = pullback(group_cot)
        totals = jax.tree.map(lambda left, right: left + right, totals, param_grads)
        return (totals, (result.astype(jnp.bfloat16), token_grads))
    zeros = jax.tree.map(jnp.zeros_like, params)
    grads, (outputs, token_grads) = lax.scan(one_group, zeros, (token_groups, cot_groups, select_groups))
    layer_out = outputs.reshape(SEGS, ROWS, D)
    tokens_grad = token_grads.reshape(SEGS, ROWS, D)
    return (layer_out, tokens_grad, grads[0], grads[1], grads[2], grads[3], grads[4], grads[5], grads[6], grads[7], grads[8], grads[9], grads[10], grads[11], grads[12], grads[13], grads[14], grads[15])
```

```python
import jax
import jax.numpy as jnp
from jax import lax
from jax.experimental import pallas as pl
from jax.experimental.pallas import tpu as pltpu
from jax.sharding import PartitionSpec as P

HEADS = 12
HEAD_DIM = 64
EPS = 1e-06
LOG2E = 1.4426950408889634
f32 = jnp.float32
bf16 = jnp.bfloat16


def dot(a, b, ca, cb):
    return lax.dot_general(a, b, (((ca,), (cb,)), ((), ())), preferred_element_type=f32)


def attn_fwd_kernel(q_ref, k_ref, v_ref, ctx_ref, p_ref):
    q = q_ref[...]
    k = k_ref[...]
    v = v_ref[...]
    lanes = lax.broadcasted_iota(jnp.int32, (1, 2 * HEAD_DIM), 1)
    ctx = None
    for h in range(2):
        mask = (lanes // HEAD_DIM) == h
        kh = jnp.where(mask, k, jnp.zeros_like(k))
        vh = jnp.where(mask, v, jnp.zeros_like(v))
        s = dot(q, kh, 1, 1) * (HEAD_DIM ** (-0.5) * LOG2E)
        e = jnp.exp2(s - jnp.max(s, axis=-1, keepdims=True))
        p = (e * (1.0 / jnp.sum(e, axis=-1, keepdims=True))).astype(bf16)
        p_ref[h] = p
        c = dot(p, vh, 1, 0)
        ctx = c if ctx is None else ctx + c
    ctx_ref[...] = ctx.astype(bf16)


def attn_bwd_kernel(q_ref, k_ref, v_ref, ctx_ref, dctx_ref, p_ref, dq_ref, dk_ref, dv_ref):
    q = q_ref[...]
    k = k_ref[...]
    v = v_ref[...]
    dctx = dctx_ref[...]
    prod = dctx.astype(f32) * ctx_ref[...].astype(f32)
    lanes = lax.broadcasted_iota(jnp.int32, (1, 2 * HEAD_DIM), 1)
    scale = HEAD_DIM ** (-0.5)
    dq = None
    dk = None
    dv = None
    for h in range(2):
        mask = (lanes // HEAD_DIM) == h
        zero = jnp.zeros_like(k)
        vh = jnp.where(mask, v, zero)
        kh = jnp.where(mask, k, zero)
        qh = jnp.where(mask, q, zero)
        dh = jnp.where(mask, dctx, zero)
        delta = jnp.sum(jnp.where(mask, prod, 0.0), axis=-1, keepdims=True)
        p = p_ref[h]
        dp = dot(dctx, vh, 1, 1)
        ds = (p.astype(f32) * (dp - delta)).astype(bf16)
        dqh = dot(ds, kh, 1, 0)
        dkh = dot(ds, qh, 0, 0)
        dvh = dot(p, dh, 0, 0)
        dq = dqh if dq is None else dq + dqh
        dk = dkh if dk is None else dk + dkh
        dv = dvh if dv is None else dv + dvh
    dq_ref[...] = (dq * scale).astype(bf16)
    dk_ref[...] = (dk * scale).astype(bf16)
    dv_ref[...] = dv.astype(bf16)


def attention_forward(q, k, v, segs, rows):
    width = q.shape[1]
    block = 2 * HEAD_DIM
    pairs = width // block
    spec = pl.BlockSpec((rows, block), lambda s, h: (s, h))
    pspec = pl.BlockSpec((2, rows, rows), lambda s, h: (s * pairs + h, 0, 0))
    return pl.pallas_call(
        attn_fwd_kernel,
        grid=(segs, pairs),
        in_specs=[spec, spec, spec],
        out_specs=[spec, pspec],
        out_shape=[
            jax.ShapeDtypeStruct(q.shape, bf16),
            jax.ShapeDtypeStruct((segs * 2 * pairs, rows, rows), bf16),
        ],
        name="attn_fwd",
    )(q, k, v)


def attention_backward(q, k, v, ctx, dctx, p, segs, rows):
    width = q.shape[1]
    block = 2 * HEAD_DIM
    pairs = width // block
    spec = pl.BlockSpec((rows, block), lambda s, h: (s, h))
    pspec = pl.BlockSpec((2, rows, rows), lambda s, h: (s * pairs + h, 0, 0))
    shape = jax.ShapeDtypeStruct(q.shape, bf16)
    return pl.pallas_call(
        attn_bwd_kernel,
        grid=(segs, pairs),
        in_specs=[spec] * 5 + [pspec],
        out_specs=[spec] * 3,
        out_shape=[shape] * 3,
        name="attn_bwd",
    )(q, k, v, ctx, dctx, p)


def xor_perm(size, mask):
    return [(i, i ^ mask) for i in range(size)]


def bits_of(size):
    count = size.bit_length() - 1
    assert 1 << count == size
    return count


class Reducer:
    def __init__(self, mesh):
        self.size = {name: mesh.shape[name] for name in ("dp", "seq")}
        self.count = {name: bits_of(size) for name, size in self.size.items()}
        self.index = {name: lax.axis_index(name) for name in ("dp", "seq")}

    def bit(self, axis, b):
        return (self.index[axis] >> b) & 1

    def swap(self, x, axis, b):
        return lax.ppermute(x, axis, xor_perm(self.size[axis], 1 << b))

    def exchange_all(self, x, order):
        for axis, b in order:
            x = x + self.swap(x, axis, b)
        return x

    def reduce_matrix(self, grad, order, split):
        rows, cols = grad.shape
        ndp, nseq = self.count["dp"], self.count["seq"]
        part = rows // self.size["dp"]
        lead = (2,) * ndp
        if split == 0:
            piece = (part // self.size["seq"], cols)
            terms = [grad.reshape(lead + (2,) * nseq + piece)]
            base = ndp
        else:
            piece = (part, cols // self.size["seq"])
            terms = [grad.reshape(lead + (part, cols))]
        dims = [("dp", b) for b in reversed(range(ndp))]
        if split == 0:
            dims += [("seq", b) for b in reversed(range(nseq))]
        for axis, b in order:
            mine = self.bit(axis, b)
            if split == 1 and axis == "seq":
                half = terms[0].shape[-1] // 2
                take = lambda t, i: lax.dynamic_slice_in_dim(t, i * half, half, axis=t.ndim - 1)
            else:
                at = dims.index((axis, b))
                dims.pop(at)
                take = lambda t, i, at=at: lax.dynamic_index_in_dim(t, i, axis=at, keepdims=False)
            send = take(terms[0], 1 - mine).astype(f32)
            for t in terms[1:]:
                send = send + take(t, 1 - mine).astype(f32)
            got = self.swap(send.astype(bf16), axis, b)
            terms = [take(t, mine) for t in terms] + [got]
        total = terms[0].astype(f32)
        for t in terms[1:]:
            total = total + t.astype(f32)
        total = total.astype(bf16)
        seq_order = [b for axis, b in order if axis == "seq"]
        for b in reversed(seq_order):
            other = self.swap(total, "seq", b)
            mine = self.bit("seq", b)
            if split == 1:
                pair = jnp.where(mine == 0, jnp.concatenate([total, other], -1), jnp.concatenate([other, total], -1))
                total = pair
            else:
                total = jnp.where(mine == 0, jnp.stack([total, other]), jnp.stack([other, total]))
        if split == 0:
            perm = [seq_order.index(b) for b in reversed(range(nseq))]
            n = len(perm)
            total = total.transpose(perm + [n + i for i in range(total.ndim - n)])
        return total.reshape(part, cols).astype(f32)


def layer_stats(values):
    center = values - jnp.mean(values, axis=-1, keepdims=True)
    inv = lax.rsqrt(jnp.mean(center * center, axis=-1, keepdims=True) + EPS)
    return center * inv, inv


def layer_norm_back(hat, inv, gain, cot):
    g = cot * gain
    a = jnp.mean(g, axis=-1, keepdims=True)
    b = jnp.mean(g * hat, axis=-1, keepdims=True)
    return inv * (g - a - hat * b)


def make_per_device(mesh):
    def per_device(
        tokens,
        memory_init,
        query_weight,
        query_bias,
        key_weight,
        value_weight,
        value_bias,
        output_weight,
        output_bias,
        attn_gain,
        attn_shift,
        inner_weight,
        inner_bias,
        outer_weight,
        outer_bias,
        ffn_gain,
        ffn_shift,
        out_grad,
        lm_mask,
        doc_segments,
    ):
        red = Reducer(mesh)
        nseq = red.size["seq"]
        ndp = red.size["dp"]
        seg_dev, rows_dev, width = tokens.shape
        own = seg_dev // nseq
        assert own * nseq == seg_dev
        rows = rows_dev * nseq
        flat_rows = own * rows
        mem_rows = memory_init.shape[1]
        seq_index = red.index["seq"]
        dp_index = red.index["dp"]
        segs_total = ndp * seg_dev

        def to_segments(x):
            x = x.reshape((nseq, own) + x.shape[1:])
            pieces = []
            for k in range(nseq):
                piece = lax.dynamic_index_in_dim(x, seq_index ^ k, axis=0, keepdims=False)
                if k:
                    piece = lax.ppermute(piece, "seq", xor_perm(nseq, k))
                pieces.append(piece)
            return jnp.stack(pieces, axis=1)

        def to_rows(x):
            out = jnp.zeros((nseq,) + (x.shape[0],) + x.shape[2:], x.dtype)
            for k in range(nseq):
                piece = x[:, k]
                if k:
                    piece = lax.ppermute(piece, "seq", xor_perm(nseq, k))
                out = lax.dynamic_update_index_in_dim(out, piece, seq_index ^ k, axis=0)
            return out.reshape((seg_dev,) + x.shape[2:])

        source = seq_index ^ jnp.arange(nseq, dtype=jnp.int32)
        position = source[:, None] * rows_dev + jnp.arange(rows_dev, dtype=jnp.int32)[None, :]
        is_mem = (position < mem_rows).reshape(1, rows)
        raw = to_segments(tokens)
        mask = to_segments(lm_mask).reshape(own, rows)
        cot_raw = to_segments(out_grad)

        valid = jnp.where(is_mem, 0, mask)
        seg_counts = jnp.sum(valid, axis=1)
        everyone = [("seq", b) for b in range(red.count["seq"])] + [("dp", b) for b in range(red.count["dp"])]
        total = red.exchange_all(jnp.broadcast_to(jnp.sum(seg_counts), (8, 128)), everyone)[0, 0]
        seg_weight = total.astype(f32) / segs_total / jnp.maximum(seg_counts, 1).astype(f32)
        row_scale = (valid.astype(f32) * seg_weight[:, None]).reshape(flat_rows, 1)

        seg_global = dp_index * seg_dev + seq_index * own + jnp.arange(own, dtype=jnp.int32)
        starts = jnp.cumsum(doc_segments) - doc_segments
        is_first = jnp.any(starts[None, :] == seg_global[:, None], axis=1)
        select = (is_first[:, None] & is_mem).reshape(flat_rows, 1)
        table = jnp.concatenate([memory_init.T, jnp.zeros((rows_dev - mem_rows, width), bf16)], axis=0)
        table = jnp.broadcast_to(table[None, None], (own, nseq, rows_dev, width)).reshape(flat_rows, width)
        flat = jnp.where(select, table, raw.reshape(flat_rows, width))

        queries = (dot(flat, query_weight, 1, 0) + query_bias.astype(f32)).astype(bf16)
        keys = dot(flat, key_weight, 1, 0).astype(bf16)
        values = (dot(flat, value_weight, 1, 0) + value_bias.astype(f32)).astype(bf16)
        context, probs = attention_forward(queries, keys, values, own, rows)
        resid1 = flat.astype(f32) + dot(context, output_weight, 1, 0) + output_bias.astype(f32)
        gain1 = attn_gain.astype(f32)
        hat1, inv1 = layer_stats(resid1)
        normed1 = hat1 * gain1 + attn_shift.astype(f32)
        normed_low = normed1.astype(bf16)
        inner = dot(normed_low, inner_weight, 1, 0) + inner_bias.astype(f32)
        cdf = 0.5 * lax.erfc(-inner * (0.5 ** 0.5))
        active = (inner * cdf).astype(bf16)
        slope = (cdf + inner * jnp.exp(-0.5 * inner * inner) * 0.3989422804014327).astype(bf16)
        resid2 = normed1 + dot(active, outer_weight, 1, 0) + outer_bias.astype(f32)
        gain2 = ffn_gain.astype(f32)
        hat2, inv2 = layer_stats(resid2)
        result = hat2 * gain2 + ffn_shift.astype(f32)
        layer_out = to_rows(result.astype(bf16).reshape(own, nseq, rows_dev, width))

        cot = cot_raw.reshape(flat_rows, width).astype(f32) * row_scale
        d_gain2 = jnp.sum(cot * hat2, axis=0)
        d_shift2 = jnp.sum(cot, axis=0)
        d_resid2 = layer_norm_back(hat2, inv2, gain2, cot)
        d_outer = d_resid2.astype(bf16)
        d_outer_bias = jnp.sum(d_outer.astype(f32), axis=0)
        seq_order = [("seq", b) for b in range(red.count["seq"])]
        dp_order = [("dp", b) for b in range(red.count["dp"])]
        order_y = seq_order + dp_order
        order_x = seq_order[:1] + dp_order[:1] + seq_order[1:] + dp_order[1:]
        d_outer_weight = dot(active, d_outer, 0, 0).astype(bf16)
        g_outer = red.reduce_matrix(d_outer_weight, order_y, 0)
        d_active = dot(d_outer, outer_weight, 1, 1)
        d_inner = (d_active * slope.astype(f32)).astype(bf16)
        d_inner_bias = jnp.sum(d_inner.astype(f32), axis=0)
        d_inner_weight = dot(normed_low, d_inner, 0, 0).astype(bf16)
        g_inner = red.reduce_matrix(d_inner_weight, order_x, 1)
        d_normed1 = dot(d_inner, inner_weight, 1, 1) + d_resid2
        d_gain1 = jnp.sum(d_normed1 * hat1, axis=0)
        d_shift1 = jnp.sum(d_normed1, axis=0)
        d_resid1 = layer_norm_back(hat1, inv1, gain1, d_normed1)
        d_attn = d_resid1.astype(bf16)
        d_output_bias = jnp.sum(d_attn.astype(f32), axis=0)
        g_output = red.reduce_matrix(dot(context, d_attn, 0, 0).astype(bf16), order_y, 0)
        d_context = dot(d_attn, output_weight, 1, 1).astype(bf16)
        d_queries, d_keys, d_values = attention_backward(
            queries, keys, values, context, d_context, probs, own, rows
        )
        d_query_bias = jnp.sum(d_queries.astype(f32), axis=0)
        d_value_bias = jnp.sum(d_values.astype(f32), axis=0)
        g_query = red.reduce_matrix(dot(flat, d_queries, 0, 0).astype(bf16), order_x, 0)
        g_key = red.reduce_matrix(dot(flat, d_keys, 0, 0).astype(bf16), order_y, 0)
        g_value = red.reduce_matrix(dot(flat, d_values, 0, 0).astype(bf16), order_x, 0)
        d_inputs = (
            dot(d_queries, query_weight, 1, 1)
            + dot(d_keys, key_weight, 1, 1)
            + dot(d_values, value_weight, 1, 1)
            + d_resid1
        )
        cut = jnp.where(select, 0.0, d_inputs).astype(bf16)
        tokens_grad = to_rows(cut.reshape(own, nseq, rows_dev, width)).astype(f32)
        at_mem = lax.dynamic_index_in_dim(
            d_inputs.reshape(own, nseq, rows_dev, width), seq_index, axis=1, keepdims=False
        )[:, :mem_rows]
        d_memory = jnp.sum(jnp.where(is_first[:, None, None], at_mem, 0.0), axis=0)

        small = jnp.concatenate(
            [
                jnp.stack(
                    [
                        d_query_bias,
                        d_value_bias,
                        d_output_bias,
                        d_gain1,
                        d_shift1,
                        d_outer_bias,
                        d_gain2,
                        d_shift2,
                    ]
                ),
                d_inner_bias.reshape(-1, width),
                d_memory,
            ],
            axis=0,
        )
        small = red.exchange_all(small, everyone)
        part = width // ndp
        mine = lax.dynamic_slice_in_dim(small, dp_index * part, part, axis=1)
        inner_rows = d_inner_bias.shape[0] // width
        inner_part = d_inner_bias.shape[0] // ndp
        g_inner_bias = lax.dynamic_slice_in_dim(
            small[8 : 8 + inner_rows].reshape(-1), dp_index * inner_part, inner_part, axis=0
        )
        g_memory = mine[8 + inner_rows :].T
        return (
            layer_out,
            tokens_grad,
            g_query,
            mine[0],
            g_key,
            g_value,
            mine[1],
            g_output,
            mine[2],
            mine[3],
            mine[4],
            g_inner,
            g_inner_bias,
            g_outer,
            mine[5],
            mine[6],
            mine[7],
            g_memory,
        )

    return per_device


def solution(mesh):
    rows = P("dp", "seq", None)
    in_specs = (rows,) + (P(),) * 16 + (rows, P("dp", "seq"), P())
    out_specs = (
        rows,
        rows,
        P("dp", None),
        P("dp"),
        P("dp", None),
        P("dp", None),
        P("dp"),
        P("dp", None),
        P("dp"),
        P("dp"),
        P("dp"),
        P("dp", None),
        P("dp"),
        P("dp", None),
        P("dp"),
        P("dp"),
        P("dp"),
        P("dp", None),
    )
    return jax.shard_map(
        make_per_device(mesh), mesh=mesh, in_specs=in_specs, out_specs=out_specs, check_vma=False
    )
```

```python
import jax
import jax.numpy as jnp
from jax import lax
from jax.experimental import pallas as pl
from jax.experimental.pallas import tpu as pltpu
from jax.sharding import PartitionSpec as P


HEAD_DIM = 64
EPS = 1e-06
LOG2E = 1.4426950408889634
BLOCK = 768
DIGITS = 16
EXTRA = 16
f32 = jnp.float32
bf16 = jnp.bfloat16


def dot(a, b, ca, cb):
    return lax.dot_general(a, b, (((ca,), (cb,)), ((), ())), preferred_element_type=f32)


def attn_fwd_kernel(q_ref, k_ref, v_ref, ctx_ref, p_ref):
    q = q_ref[...]
    k = k_ref[...]
    v = v_ref[...]
    lanes = lax.broadcasted_iota(jnp.int32, (1, 2 * HEAD_DIM), 1)
    ctx = None
    for h in range(2):
        mask = (lanes // HEAD_DIM) == h
        kh = jnp.where(mask, k, jnp.zeros_like(k))
        vh = jnp.where(mask, v, jnp.zeros_like(v))
        s = dot(q, kh, 1, 1) * (HEAD_DIM ** (-0.5) * LOG2E)
        e = jnp.exp2(s - jnp.max(s, axis=-1, keepdims=True))
        p = (e * (1.0 / jnp.sum(e, axis=-1, keepdims=True))).astype(bf16)
        p_ref[h] = p
        c = dot(p, vh, 1, 0)
        ctx = c if ctx is None else ctx + c
    ctx_ref[...] = ctx.astype(bf16)


def attn_bwd_kernel(q_ref, k_ref, v_ref, ctx_ref, dctx_ref, p_ref, dq_ref, dk_ref, dv_ref):
    q = q_ref[...]
    k = k_ref[...]
    v = v_ref[...]
    dctx = dctx_ref[...]
    prod = dctx.astype(f32) * ctx_ref[...].astype(f32)
    lanes = lax.broadcasted_iota(jnp.int32, (1, 2 * HEAD_DIM), 1)
    scale = HEAD_DIM ** (-0.5)
    dq = None
    dk = None
    dv = None
    for h in range(2):
        mask = (lanes // HEAD_DIM) == h
        zero = jnp.zeros_like(k)
        vh = jnp.where(mask, v, zero)
        kh = jnp.where(mask, k, zero)
        qh = jnp.where(mask, q, zero)
        dh = jnp.where(mask, dctx, zero)
        delta = jnp.sum(jnp.where(mask, prod, 0.0), axis=-1, keepdims=True)
        p = p_ref[h]
        dp = dot(dctx, vh, 1, 1)
        ds = (p.astype(f32) * (dp - delta)).astype(bf16)
        dqh = dot(ds, kh, 1, 0)
        dkh = dot(ds, qh, 0, 0)
        dvh = dot(p, dh, 0, 0)
        dq = dqh if dq is None else dq + dqh
        dk = dkh if dk is None else dk + dkh
        dv = dvh if dv is None else dv + dvh
    dq_ref[...] = (dq * scale).astype(bf16)
    dk_ref[...] = (dk * scale).astype(bf16)
    dv_ref[...] = dv.astype(bf16)


def attention_forward(q, k, v, segs, rows):
    block = 2 * HEAD_DIM
    pairs = q.shape[1] // block
    spec = pl.BlockSpec((rows, block), lambda s, h: (s, h))
    pspec = pl.BlockSpec((2, rows, rows), lambda s, h: (s * pairs + h, 0, 0))
    return pl.pallas_call(
        attn_fwd_kernel,
        grid=(segs, pairs),
        in_specs=[spec, spec, spec],
        out_specs=[spec, pspec],
        out_shape=[
            jax.ShapeDtypeStruct(q.shape, bf16),
            jax.ShapeDtypeStruct((segs * 2 * pairs, rows, rows), bf16),
        ],
        name="attn_fwd",
    )(q, k, v)


def attention_backward(q, k, v, ctx, dctx, p, segs, rows):
    block = 2 * HEAD_DIM
    pairs = q.shape[1] // block
    spec = pl.BlockSpec((rows, block), lambda s, h: (s, h))
    pspec = pl.BlockSpec((2, rows, rows), lambda s, h: (s * pairs + h, 0, 0))
    shape = jax.ShapeDtypeStruct(q.shape, bf16)
    return pl.pallas_call(
        attn_bwd_kernel,
        grid=(segs, pairs),
        in_specs=[spec] * 5 + [pspec],
        out_specs=[spec] * 3,
        out_shape=[shape] * 3,
        name="attn_bwd",
    )(q, k, v, ctx, dctx, p)


def upper_tail(x):
    z = jnp.abs(x) * (0.5 ** 0.5)
    t = 1.0 / (1.0 + 0.5 * z)
    poly = 0.17087277
    for c in (
        -0.82215223,
        1.48851587,
        -1.13520398,
        0.27886807,
        -0.18628806,
        0.09678418,
        0.37409196,
        1.00002368,
        -1.26551223,
    ):
        poly = poly * t + c
    bell = jnp.exp(-0.5 * x * x)
    half = 0.5 * t * bell * jnp.exp(poly)
    return jnp.where(x >= 0, 1.0 - half, half), bell


def normalize(values):
    center = values - jnp.mean(values, axis=-1, keepdims=True)
    inv = lax.rsqrt(jnp.mean(center * center, axis=-1, keepdims=True) + EPS)
    return center * inv, inv


def normalize_back(hat, inv, g):
    a = jnp.mean(g, axis=-1, keepdims=True)
    b = jnp.mean(g * hat, axis=-1, keepdims=True)
    return inv * (g - a - hat * b)


def rows_of(*vectors):
    lines = [jnp.sum(v, axis=0, keepdims=True) for v in vectors]
    pad = 8 - len(lines)
    return jnp.concatenate(lines + [jnp.zeros((pad, lines[0].shape[1]), f32)], axis=0)


def ffn_forward(flat, ctx, wout, vecs, wi, ib, wo, cot_pieces, rows_dev):
    n, width = flat.shape
    inner = wi.shape[1]
    count = len(cot_pieces)

    def kernel(flat_ref, ctx_ref, wout_ref, vec_ref, wi_ref, ib_ref, wo_ref, *refs):
        cot_refs = refs[:count]
        hat1_ref, inv1_ref, n1t_ref, active_ref, slope_ref = refs[count : count + 5]
        out_refs = refs[count + 5 : 2 * count + 5]
        dres_ref, douter_ref, small_ref, low, acc = refs[2 * count + 5 :]
        j = pl.program_id(0)

        @pl.when(j == 0)
        def _():
            resid = flat_ref[...].astype(f32) + dot(ctx_ref[...], wout_ref[...], 1, 0) + vec_ref[0:1]
            hat, inv = normalize(resid)
            hat1_ref[...] = hat
            inv1_ref[...] = jnp.broadcast_to(inv, inv1_ref.shape)
            normed = hat * vec_ref[1:2] + vec_ref[2:3]
            low[...] = normed.astype(bf16)
            n1t_ref[...] = normed.astype(bf16).T
            acc[...] = normed + vec_ref[3:4]

        inner = dot(low[...], wi_ref[...], 1, 0) + ib_ref[...]
        cdf, bell = upper_tail(inner)
        active = (inner * cdf).astype(bf16)
        active_ref[...] = active
        slope_ref[...] = (cdf + inner * bell * 0.3989422804014327).astype(bf16)
        acc[...] += dot(active, wo_ref[...], 1, 0)

        @pl.when(j == pl.num_programs(0) - 1)
        def _():
            valid_rows = cot_refs[0][rows_dev : rows_dev + EXTRA].astype(f32)[0:1]
            for r in cot_refs[1:]:
                valid_rows = valid_rows + r[rows_dev : rows_dev + EXTRA].astype(f32)[0:1]
            scale = 1.0 / jnp.maximum(valid_rows, 1.0)
            lines = [valid_rows * 0.0] * 3
            for k in range(count):
                part = slice(k * rows_dev, (k + 1) * rows_dev)
                hat, inv = normalize(acc[part])
                out_refs[k][...] = (hat * vec_ref[4:5] + vec_ref[5:6]).astype(bf16)
                cot = cot_refs[k][0:rows_dev].astype(f32) * scale
                dres = normalize_back(hat, inv, cot * vec_ref[4:5])
                dres_ref[part] = dres
                low_d = dres.astype(bf16)
                douter_ref[part] = low_d
                for i, v in enumerate((cot * hat, cot, low_d.astype(f32))):
                    lines[i] = lines[i] + jnp.sum(v, axis=0, keepdims=True)
            for i, v in enumerate(lines + [valid_rows]):
                small_ref[i : i + 1] = v

    full = lambda a: pl.BlockSpec(a.shape, lambda j: (0,) * a.ndim)
    whole = lambda shape: pl.BlockSpec(shape, lambda j: (0,) * len(shape))
    cols = pl.BlockSpec((n, BLOCK), lambda j: (0, j))
    outs = [
        (whole, (n, width), f32),
        (whole, (n, 128), f32),
        (whole, (width, n), bf16),
        (None, (n, inner), bf16),
        (None, (n, inner), bf16),
    ]
    outs += [(whole, (rows_dev, width), bf16)] * count
    outs += [(whole, (n, width), f32), (whole, (n, width), bf16), (whole, (8, width), f32)]
    got = pl.pallas_call(
        kernel,
        grid=(inner // BLOCK,),
        in_specs=[
            full(flat),
            full(ctx),
            full(wout),
            full(vecs),
            pl.BlockSpec((width, BLOCK), lambda j: (0, j)),
            pl.BlockSpec((1, BLOCK), lambda j: (0, j)),
            pl.BlockSpec((BLOCK, width), lambda j: (j, 0)),
        ]
        + [full(c) for c in cot_pieces],
        out_specs=[spec(shape) if spec else cols for spec, shape, _ in outs],
        out_shape=[jax.ShapeDtypeStruct(shape, kind) for _, shape, kind in outs],
        scratch_shapes=[pltpu.VMEM((n, width), bf16), pltpu.VMEM((n, width), f32)],
        name="ffn_fwd",
    )(flat, ctx, wout, vecs, wi, ib, wo, *cot_pieces)
    return got[:5], got[5 : 5 + count], got[5 + count :]


def inputs_backward(me, grads, weights, d_resid1, small1, small2, d_inner_bias, rows_dev, nseq, mem_rows):
    _, width = d_resid1.shape
    ib_rows = d_inner_bias.shape[1] // width

    def kernel(me_ref, dq_ref, dk_ref, dv_ref, wq_ref, wk_ref, wv_ref, dres_ref, s1_ref, s2_ref, ib_ref, *outs):
        pieces, small_ref = outs[:nseq], outs[nseq]
        seq_me = me_ref[1]
        first = me_ref[2]
        small_ref[...] = jnp.zeros_like(small_ref)
        d = dres_ref[...]
        for g, w in ((dq_ref, wq_ref), (dk_ref, wk_ref), (dv_ref, wv_ref)):
            d = d + dot(g[...], w[...], 1, 1)
        row = lax.broadcasted_iota(jnp.int32, (rows_dev, 1), 0)
        memory = jnp.zeros((EXTRA, width), f32)
        for k in range(nseq):
            part = d[k * rows_dev : (k + 1) * rows_dev]
            is_mem = jnp.logical_and(row < mem_rows, jnp.logical_and(seq_me == k, first != 0))
            pieces[k][...] = jnp.where(is_mem, 0.0, part).astype(bf16)
            memory = memory + jnp.where(is_mem[:EXTRA], part[:EXTRA], 0.0)
        small_ref[0, 0:1] = jnp.sum(dq_ref[...].astype(f32), axis=0, keepdims=True)
        small_ref[0, 1:2] = jnp.sum(dv_ref[...].astype(f32), axis=0, keepdims=True)
        small_ref[0, 2:5] = s1_ref[0:3]
        small_ref[0, 5:8] = s2_ref[0:3]
        for r in range(ib_rows):
            small_ref[1, r : r + 1] = ib_ref[0:1, r * width : (r + 1) * width]
        lane = lax.broadcasted_iota(jnp.int32, (1, width), 1)
        bits = (s2_ref[3:4].astype(jnp.int32) >> jnp.minimum(lane, DIGITS)) & 1
        small_ref[1, ib_rows : ib_rows + 1] = bits.astype(f32)
        small_ref[2] = memory

    vmem = pl.BlockSpec(memory_space=pltpu.VMEM)
    got = pl.pallas_call(
        kernel,
        in_specs=[pl.BlockSpec(memory_space=pltpu.SMEM)] + [vmem] * 10,
        out_specs=[vmem] * (nseq + 1),
        out_shape=[jax.ShapeDtypeStruct((rows_dev, width), bf16)] * nseq
        + [jax.ShapeDtypeStruct((nseq, EXTRA, width), f32)],
        name="inputs_bwd",
    )(me, *grads, *weights, d_resid1, small1, small2, d_inner_bias)
    return got[:nseq], got[nseq]


class Plan:
    def __init__(self, mesh):
        self.ndp, self.nseq = mesh.shape["dp"], mesh.shape["seq"]
        bits = [("seq", b) for b in range(self.nseq.bit_length() - 1)]
        dp_bits = [("dp", b) for b in range(self.ndp.bit_length() - 1)]
        assert 2 ** len(bits) == self.nseq and 2 ** len(dp_bits) == self.ndp
        rest = bits[2:] + dp_bits[1:]
        self.first = bits[0]
        self.orders = [[bits[1], dp_bits[0]] + rest, [dp_bits[0], bits[1]] + rest]
        self.steps = len(self.orders[0])
        self.places = 1 << self.steps

    def flip(self, device, which):
        axis, b = which
        return device ^ ((1 << b) * (self.nseq if axis == "dp" else 1))

    def perm(self, step):
        devices = range(self.ndp * self.nseq)
        if step < 0:
            return [(d, self.flip(d, self.first)) for d in devices]
        return [(d, self.flip(d, self.orders[d & 1][step])) for d in devices]

    def place(self, dp_diff, seq_diff, half):
        value = {"dp": dp_diff, "seq": seq_diff}
        places = []
        for order in self.orders:
            p = 0
            for axis, b in order:
                p = p * 2 + ((value[axis] >> b) & 1)
            places.append(p)
        return jnp.where(half == 0, places[0], places[1])


def scatter_pieces(plan, me_ref, result, pieces, keep_ref, send_ref, rows, offset=0):
    dp_me = me_ref[0]
    seq_me = me_ref[1]
    for i, (dp, seq) in enumerate(pieces):
        tile = result[i * rows : (i + 1) * rows].astype(bf16)
        half = seq & 1
        at = plan.place(dp ^ dp_me, seq ^ seq_me, half)
        stay = half == (seq_me & 1)

        @pl.when(stay)
        def _(tile=tile, at=at):
            keep_ref[at, offset : offset + rows] = tile

        @pl.when(jnp.logical_not(stay))
        def _(tile=tile, at=at):
            send_ref[at, offset : offset + rows] = tile


def ffn_outer_grad(plan, me, active, d_outer):
    n, inner = active.shape
    width = d_outer.shape[1]
    rows = inner // (plan.ndp * plan.nseq)
    per = BLOCK // rows

    def kernel(me_ref, active_ref, d_ref, keep_ref, send_ref):
        j = pl.program_id(0)
        result = dot(active_ref[...], d_ref[...], 0, 0)
        pieces = [((j * per + i) // plan.nseq, (j * per + i) % plan.nseq) for i in range(per)]
        scatter_pieces(plan, me_ref, result, pieces, keep_ref, send_ref, rows)

    shape = jax.ShapeDtypeStruct((plan.places, rows, width), bf16)
    spec = pl.BlockSpec(shape.shape, lambda j, m: (0, 0, 0))
    return pl.pallas_call(
        kernel,
        grid_spec=pltpu.PrefetchScalarGridSpec(
            num_scalar_prefetch=1,
            grid=(inner // BLOCK,),
            in_specs=[
                pl.BlockSpec((n, BLOCK), lambda j, m: (0, j)),
                pl.BlockSpec((n, width), lambda j, m: (0, 0)),
            ],
            out_specs=[spec, spec],
        ),
        out_shape=[shape, shape],
        name="outer_grad",
    )(me, active, d_outer)


def ffn_backward(plan, me, slope, d_outer, wo, wi, n1t, d_resid2, hat1, inv1, gain1, wout):
    n, inner = slope.shape
    width = d_outer.shape[1]
    rows = width // plan.ndp
    cols = inner // plan.nseq

    def kernel(
        me_ref, slope_ref, douter_ref, wo_ref, wi_ref, n1t_ref, dres2_ref, hat1_ref, inv1_ref, gain_ref, wout_ref,
        keep_ref, send_ref, dres1_ref, dattn_ref, dctx_ref, ib_ref, small_ref, acc,
    ):
        j = pl.program_id(0)
        d_active = dot(douter_ref[...], wo_ref[...], 1, 1)
        d_inner = (d_active * slope_ref[...].astype(f32)).astype(bf16)
        ib_ref[...] = jnp.broadcast_to(jnp.sum(d_inner.astype(f32), axis=0, keepdims=True), ib_ref.shape)
        result = dot(n1t_ref[...], d_inner, 1, 0)
        scatter_pieces(plan, me_ref, result, [(i, j) for i in range(plan.ndp)], keep_ref, send_ref, rows)
        back = dot(d_inner, wi_ref[...], 1, 1)

        @pl.when(j == 0)
        def _():
            acc[...] = dres2_ref[...] + back

        @pl.when(j > 0)
        def _():
            acc[...] += back

        @pl.when(j == pl.num_programs(0) - 1)
        def _():
            d_normed = acc[...]
            hat = hat1_ref[...]
            dres = normalize_back(hat, inv1_ref[:, 0:1], d_normed * gain_ref[...])
            dres1_ref[...] = dres
            low = dres.astype(bf16)
            dattn_ref[...] = low
            dctx_ref[...] = dot(low, wout_ref[...], 1, 1).astype(bf16)
            small_ref[...] = rows_of(d_normed * hat, d_normed, low.astype(f32))

    full = lambda a: pl.BlockSpec(a.shape, lambda j, m: (0,) * a.ndim)
    whole = lambda shape: pl.BlockSpec(shape, lambda j, m: (0,) * len(shape))
    chunk = jax.ShapeDtypeStruct((plan.places, rows, cols), bf16)
    return pl.pallas_call(
        kernel,
        grid_spec=pltpu.PrefetchScalarGridSpec(
            num_scalar_prefetch=1,
            grid=(plan.nseq,),
            in_specs=[
                pl.BlockSpec((n, cols), lambda j, m: (0, j)),
                full(d_outer),
                pl.BlockSpec((cols, width), lambda j, m: (j, 0)),
                pl.BlockSpec((width, cols), lambda j, m: (0, j)),
                full(n1t),
                full(d_resid2),
                full(hat1),
                full(inv1),
                full(gain1),
                full(wout),
            ],
            out_specs=[
                whole(chunk.shape),
                whole(chunk.shape),
                whole((n, width)),
                whole((n, width)),
                whole((n, width)),
                pl.BlockSpec((8, cols), lambda j, m: (0, j)),
                whole((8, width)),
            ],
            scratch_shapes=[pltpu.VMEM((n, width), f32)],
        ),
        out_shape=[
            chunk,
            chunk,
            jax.ShapeDtypeStruct((n, width), f32),
            jax.ShapeDtypeStruct((n, width), bf16),
            jax.ShapeDtypeStruct((n, width), bf16),
            jax.ShapeDtypeStruct((8, inner), f32),
            jax.ShapeDtypeStruct((8, width), f32),
        ],
        name="ffn_bwd",
    )(me, slope, d_outer, wo, wi, n1t, d_resid2, hat1, inv1, gain1, wout)


def attn_weight_grads(plan, me, flat, ctx, grads, small):
    n, width = flat.shape
    rows = width // plan.ndp

    def kernel(me_ref, flat_ref, ctx_ref, d0_ref, d1_ref, d2_ref, d3_ref, small_ref, keep_ref, send_ref, flat_t, ctx_t):
        flat_t[...] = flat_ref[...].T
        ctx_t[...] = ctx_ref[...].T
        for s, d_ref in enumerate((d0_ref, d1_ref, d2_ref, d3_ref)):
            left = ctx_t if s == 3 else flat_t
            result = dot(left[...], d_ref[...], 1, 0)
            pieces = [(i, s) for i in range(plan.ndp)]
            scatter_pieces(plan, me_ref, result, pieces, keep_ref, send_ref, rows)
            below = jnp.concatenate([small_ref[s].astype(bf16)] * plan.ndp, axis=0)
            scatter_pieces(plan, me_ref, below, pieces, keep_ref, send_ref, EXTRA, rows)

    shape = jax.ShapeDtypeStruct((plan.places, rows + EXTRA, width), bf16)
    return pl.pallas_call(
        kernel,
        in_specs=[pl.BlockSpec(memory_space=pltpu.SMEM)] + [pl.BlockSpec(memory_space=pltpu.VMEM)] * 7,
        out_specs=[pl.BlockSpec(memory_space=pltpu.VMEM)] * 2,
        out_shape=[shape, shape],
        scratch_shapes=[pltpu.VMEM((width, n), bf16), pltpu.VMEM((width, n), bf16)],
        name="attn_grad",
    )(me, flat, ctx, *grads, small)


def place_pieces(plan, me, blocks):
    dp = jnp.repeat(jnp.arange(plan.ndp), plan.nseq)
    seq = jnp.tile(jnp.arange(plan.nseq), plan.ndp)
    half = seq & 1
    place = plan.place(dp ^ me[0], seq ^ me[1], half)
    away = half ^ (me[1] & 1)
    flat = blocks.reshape((plan.ndp * plan.nseq,) + blocks.shape[2:])
    order = jnp.zeros((2 * plan.places,), jnp.int32).at[away * plan.places + place].set(jnp.arange(dp.shape[0]))
    both = jnp.take(flat, order, axis=0)
    return both[: plan.places], both[plan.places :]


def make_per_device(mesh):
    plan = Plan(mesh)
    ndp, nseq = plan.ndp, plan.nseq
    devices = ("dp", "seq")

    def total_of(terms):
        total = terms[0].astype(f32)
        for t in terms[1:]:
            total = total + t.astype(f32)
        return total

    def start_chunk(keep, send):
        return [keep, lax.ppermute(send, devices, plan.perm(-1))]

    def step_chunk(terms, step):
        half = terms[0].shape[0] // 2
        send = total_of([t[half:] for t in terms]).astype(bf16)
        got = lax.ppermute(send, devices, plan.perm(step))
        return [t[:half] for t in terms] + [got]

    def swap_seq(x, k):
        return lax.ppermute(x, "seq", [(i, i ^ k) for i in range(nseq)])

    def gather_seq(x):
        x = x[None]
        for b in reversed(range(nseq.bit_length() - 1)):
            x = jnp.concatenate([x, lax.ppermute(x, "seq", [(i, i ^ (1 << b)) for i in range(nseq)])], axis=0)
        count = nseq.bit_length() - 1
        order = []
        for k in range(nseq):
            pos = 0
            for b in range(count):
                pos |= ((k >> b) & 1) << (count - 1 - b)
            order.append(pos)
        return [x[p] for p in order]

    def per_device(
        tokens,
        memory_init,
        query_weight,
        query_bias,
        key_weight,
        value_weight,
        value_bias,
        output_weight,
        output_bias,
        attn_gain,
        attn_shift,
        inner_weight,
        inner_bias,
        outer_weight,
        outer_bias,
        ffn_gain,
        ffn_shift,
        out_grad,
        lm_mask,
        doc_segments,
    ):
        seg_dev, rows_dev, width = tokens.shape
        assert seg_dev == nseq
        rows = rows_dev * nseq
        assert rows < (1 << DIGITS) and ndp * nseq <= 256
        mem_rows = memory_init.shape[1]
        ff = inner_weight.shape[1]
        seq_index = lax.axis_index("seq")
        dp_index = lax.axis_index("dp")
        segs_total = ndp * seg_dev

        def to_segments(x):
            pieces = []
            for k in range(nseq):
                piece = lax.dynamic_index_in_dim(x, seq_index ^ k, axis=0, keepdims=False)
                pieces.append(swap_seq(piece, k) if k else piece)
            return pieces

        def to_rows(pieces, finish):
            out = None
            for k in range(nseq):
                piece = finish(pieces[k])
                if out is None:
                    out = jnp.zeros((nseq,) + piece.shape, piece.dtype)
                out = lax.dynamic_update_index_in_dim(out, piece, seq_index ^ k, axis=0)
            return out

        source = seq_index ^ jnp.arange(nseq, dtype=jnp.int32)
        position = source[:, None] * rows_dev + jnp.arange(rows_dev, dtype=jnp.int32)[None, :]
        is_mem = (position < mem_rows).reshape(rows)
        raw = jnp.concatenate(to_segments(tokens), axis=0)

        here = seq_index * rows_dev + jnp.arange(rows_dev, dtype=jnp.int32)
        valid = jnp.where((here < mem_rows)[None, :], 0, lm_mask)
        counts_here = jnp.sum(valid, axis=1)
        masked = jnp.where(valid[..., None] != 0, out_grad, jnp.zeros_like(out_grad))
        assert rows_dev <= 256
        count_rows = jnp.broadcast_to(counts_here.astype(bf16)[:, None, None], (seg_dev, EXTRA, width))
        cot_pieces = to_segments(jnp.concatenate([masked, count_rows], axis=1))

        seg_global = dp_index * seg_dev + seq_index
        starts = jnp.cumsum(doc_segments) - doc_segments
        is_first = jnp.any(starts == seg_global)
        me = jnp.stack([dp_index, seq_index, is_first.astype(jnp.int32)]).astype(jnp.int32)
        select = (is_first & is_mem)[:, None]
        table = jnp.concatenate([memory_init.T, jnp.zeros((rows_dev - mem_rows, width), bf16)], axis=0)
        table = jnp.concatenate([table] * nseq, axis=0)
        flat = jnp.where(select, table, raw)

        queries = (dot(flat, query_weight, 1, 0) + query_bias.astype(f32)).astype(bf16)
        keys = dot(flat, key_weight, 1, 0).astype(bf16)
        values = (dot(flat, value_weight, 1, 0) + value_bias.astype(f32)).astype(bf16)
        context, probs = attention_forward(queries, keys, values, 1, rows)
        zero = jnp.zeros_like(output_bias)
        vecs = jnp.stack(
            [output_bias, attn_gain, attn_shift, outer_bias, ffn_gain, ffn_shift, zero, zero]
        ).astype(f32)
        (hat1, inv1, n1t, active, slope), out_pieces, (d_resid2, d_outer, small2) = ffn_forward(
            flat,
            context,
            output_weight,
            vecs,
            inner_weight,
            inner_bias.astype(f32)[None],
            outer_weight,
            cot_pieces,
            rows_dev,
        )
        out_pieces = [swap_seq(p, k) if k else p for k, p in enumerate(out_pieces)]
        layer_out = to_rows(out_pieces, lambda p: p)

        aligned = (width // ndp) % 16 == 0 and (ff // (ndp * nseq)) % 16 == 0 and ff // nseq == BLOCK
        if aligned:
            keep, send = ffn_outer_grad(plan, me, active, d_outer)
        else:
            grad = dot(active, d_outer, 0, 0).astype(bf16)
            keep, send = place_pieces(plan, me, grad.reshape(ndp, nseq, -1, width))
        d_outer, keep, send = lax.optimization_barrier((d_outer, keep, send))
        outer = start_chunk(keep, send)
        if aligned:
            keep, send, d_resid1, d_attn, d_context, d_inner_bias, small1 = ffn_backward(
                plan, me, slope, d_outer, outer_weight, inner_weight, n1t, d_resid2, hat1, inv1, vecs[1:2], output_weight
            )
        else:
            d_inner = (dot(d_outer, outer_weight, 1, 1) * slope.astype(f32)).astype(bf16)
            d_inner_bias = jnp.broadcast_to(jnp.sum(d_inner.astype(f32), axis=0), (8, ff))
            grad = dot(n1t, d_inner, 1, 0).astype(bf16)
            grad = grad.reshape(ndp, width // ndp, nseq, ff // nseq).transpose(0, 2, 1, 3)
            keep, send = place_pieces(plan, me, grad)
            d_normed = dot(d_inner, inner_weight, 1, 1) + d_resid2
            d_resid1 = normalize_back(hat1, inv1[:, 0:1], d_normed * vecs[1:2])
            d_attn = d_resid1.astype(bf16)
            d_context = dot(d_attn, output_weight, 1, 1).astype(bf16)
            small1 = rows_of(d_normed * hat1, d_normed, d_attn.astype(f32))
        inner = start_chunk(keep, send)
        outer = step_chunk(outer, 0)
        d_queries, d_keys, d_values = attention_backward(
            queries, keys, values, context, d_context, probs, 1, rows
        )
        outer = step_chunk(outer, 1)
        inner = step_chunk(inner, 0)
        cut_pieces, small = inputs_backward(
            me,
            (d_queries, d_keys, d_values),
            (query_weight, key_weight, value_weight),
            d_resid1,
            small1,
            small2,
            d_inner_bias,
            rows_dev,
            nseq,
            mem_rows,
        )
        cut_pieces = [swap_seq(p, k) if k else p for k, p in enumerate(cut_pieces)]
        ib_rows = ff // width
        attn_grads = (d_queries, d_keys, d_values, d_attn)
        if aligned:
            keep, send = attn_weight_grads(plan, me, flat, context, attn_grads, small)
        else:
            blocks = []
            for s, d in enumerate(attn_grads):
                left = context if s == 3 else flat
                blocks.append(dot(left, d, 0, 0).astype(bf16).reshape(ndp, -1, width))
            blocks = jnp.stack(blocks, axis=1)
            below = jnp.broadcast_to(small.astype(bf16)[None], (ndp,) + small.shape)
            keep, send = place_pieces(plan, me, jnp.concatenate([blocks, below], axis=2))
        attn = start_chunk(keep, send)
        outer = step_chunk(outer, 2)
        inner = step_chunk(inner, 1)
        for step in range(3, plan.steps):
            outer = step_chunk(outer, step)
        for step in range(2, plan.steps):
            inner = step_chunk(inner, step)
        ffn_pieces = gather_seq(jnp.concatenate([total_of(outer)[0], total_of(inner)[0]], axis=0).astype(bf16))
        for step in range(plan.steps):
            attn = step_chunk(attn, step)
        attn_pieces = gather_seq(total_of(attn)[0].astype(bf16))

        def in_order(pieces):
            stack = jnp.stack(pieces)
            return [lax.dynamic_index_in_dim(stack, seq_index ^ s, 0, keepdims=False) for s in range(nseq)]

        part = width // ndp
        attn_parts = in_order(attn_pieces)
        ffn_parts = in_order(ffn_pieces)
        weights = (2.0 ** jnp.arange(DIGITS)).astype(f32)
        total = jnp.sum(attn_parts[1][part + ib_rows, :DIGITS].astype(f32) * weights)
        factor = total / segs_total
        finish = lambda x: x.astype(f32) * factor

        tokens_grad = to_rows(cut_pieces, finish)

        outer_rows = ff // (ndp * nseq)
        g_outer = finish(jnp.concatenate([p[:outer_rows] for p in ffn_parts], axis=0))
        g_inner = finish(jnp.concatenate([p[outer_rows:] for p in ffn_parts], axis=1))
        g_query, g_key, g_value, g_output = [finish(p[:part]) for p in attn_parts[:4]]
        mine = lambda x: lax.dynamic_slice_in_dim(finish(x), dp_index * part, part, axis=1)
        vec_rows = mine(attn_parts[0][part : part + 8])
        g_memory = mine(attn_parts[2][part : part + mem_rows]).T
        inner_part = ff // ndp
        g_inner_bias = lax.dynamic_slice_in_dim(
            finish(attn_parts[1][part : part + ib_rows]).reshape(-1), dp_index * inner_part, inner_part, axis=0
        )
        g_query_bias, g_value_bias, g_gain1, g_shift1, g_output_bias, g_gain2, g_shift2, g_outer_bias = vec_rows
        return (
            layer_out,
            tokens_grad,
            g_query,
            g_query_bias,
            g_key,
            g_value,
            g_value_bias,
            g_output,
            g_output_bias,
            g_gain1,
            g_shift1,
            g_inner,
            g_inner_bias,
            g_outer,
            g_outer_bias,
            g_gain2,
            g_shift2,
            g_memory,
        )

    return per_device


def solution(mesh):
    rows = P("dp", "seq", None)
    in_specs = (rows,) + (P(),) * 16 + (rows, P("dp", "seq"), P())
    out_specs = (
        rows,
        rows,
        P("dp", None),
        P("dp"),
        P("dp", None),
        P("dp", None),
        P("dp"),
        P("dp", None),
        P("dp"),
        P("dp"),
        P("dp"),
        P("dp", None),
        P("dp"),
        P("dp", None),
        P("dp"),
        P("dp"),
        P("dp"),
        P("dp", None),
    )
    return jax.shard_map(
        make_per_device(mesh), mesh=mesh, in_specs=in_specs, out_specs=out_specs, check_vma=False
    )
```

```python
import jax
import jax.numpy as jnp
from jax import lax
from jax.experimental import pallas as pl
from jax.experimental.pallas import tpu as pltpu
from jax.sharding import PartitionSpec as P


HEAD_DIM = 64
EPS = 1e-06
LOG2E = 1.4426950408889634
BLOCK = 768
EXTRA = 16
f32 = jnp.float32
bf16 = jnp.bfloat16


def dot(a, b, ca, cb):
    return lax.dot_general(a, b, (((ca,), (cb,)), ((), ())), preferred_element_type=f32)


def attn_fwd_kernel(q_ref, k_ref, v_ref, ctx_ref, p_ref):
    q = q_ref[...]
    k = k_ref[...]
    v = v_ref[...]
    lanes = lax.broadcasted_iota(jnp.int32, (1, 2 * HEAD_DIM), 1)
    ctx = None
    for h in range(2):
        mask = (lanes // HEAD_DIM) == h
        kh = jnp.where(mask, k, jnp.zeros_like(k))
        vh = jnp.where(mask, v, jnp.zeros_like(v))
        s = dot(q, kh, 1, 1) * (HEAD_DIM ** (-0.5) * LOG2E)
        e = jnp.exp2(s - jnp.max(s, axis=-1, keepdims=True))
        p = (e * (1.0 / jnp.sum(e, axis=-1, keepdims=True))).astype(bf16)
        p_ref[h] = p
        c = dot(p, vh, 1, 0)
        ctx = c if ctx is None else ctx + c
    ctx_ref[...] = ctx.astype(bf16)


def attn_bwd_kernel(q_ref, k_ref, v_ref, ctx_ref, dctx_ref, p_ref, dq_ref, dk_ref, dv_ref):
    q = q_ref[...]
    k = k_ref[...]
    v = v_ref[...]
    dctx = dctx_ref[...]
    prod = dctx.astype(f32) * ctx_ref[...].astype(f32)
    lanes = lax.broadcasted_iota(jnp.int32, (1, 2 * HEAD_DIM), 1)
    scale = HEAD_DIM ** (-0.5)
    dq = None
    dk = None
    dv = None
    for h in range(2):
        mask = (lanes // HEAD_DIM) == h
        zero = jnp.zeros_like(k)
        vh = jnp.where(mask, v, zero)
        kh = jnp.where(mask, k, zero)
        qh = jnp.where(mask, q, zero)
        dh = jnp.where(mask, dctx, zero)
        delta = jnp.sum(jnp.where(mask, prod, 0.0), axis=-1, keepdims=True)
        p = p_ref[h]
        dp = dot(dctx, vh, 1, 1)
        ds = (p.astype(f32) * (dp - delta)).astype(bf16)
        dqh = dot(ds, kh, 1, 0)
        dkh = dot(ds, qh, 0, 0)
        dvh = dot(p, dh, 0, 0)
        dq = dqh if dq is None else dq + dqh
        dk = dkh if dk is None else dk + dkh
        dv = dvh if dv is None else dv + dvh
    dq_ref[...] = (dq * scale).astype(bf16)
    dk_ref[...] = (dk * scale).astype(bf16)
    dv_ref[...] = dv.astype(bf16)


def attention_forward(q, k, v, segs, rows):
    block = 2 * HEAD_DIM
    pairs = q.shape[1] // block
    spec = pl.BlockSpec((rows, block), lambda s, h: (s, h))
    pspec = pl.BlockSpec((2, rows, rows), lambda s, h: (s * pairs + h, 0, 0))
    return pl.pallas_call(
        attn_fwd_kernel,
        grid=(segs, pairs),
        in_specs=[spec, spec, spec],
        out_specs=[spec, pspec],
        out_shape=[
            jax.ShapeDtypeStruct(q.shape, bf16),
            jax.ShapeDtypeStruct((segs * 2 * pairs, rows, rows), bf16),
        ],
        name="attn_fwd",
    )(q, k, v)


def attention_backward(q, k, v, ctx, dctx, p, segs, rows):
    block = 2 * HEAD_DIM
    pairs = q.shape[1] // block
    spec = pl.BlockSpec((rows, block), lambda s, h: (s, h))
    pspec = pl.BlockSpec((2, rows, rows), lambda s, h: (s * pairs + h, 0, 0))
    shape = jax.ShapeDtypeStruct(q.shape, bf16)
    return pl.pallas_call(
        attn_bwd_kernel,
        grid=(segs, pairs),
        in_specs=[spec] * 5 + [pspec],
        out_specs=[spec] * 3,
        out_shape=[shape] * 3,
        name="attn_bwd",
    )(q, k, v, ctx, dctx, p)


def upper_tail(x):
    z = jnp.abs(x) * (0.5 ** 0.5)
    t = 1.0 / (1.0 + 0.5 * z)
    poly = 0.17087277
    for c in (
        -0.82215223,
        1.48851587,
        -1.13520398,
        0.27886807,
        -0.18628806,
        0.09678418,
        0.37409196,
        1.00002368,
        -1.26551223,
    ):
        poly = poly * t + c
    bell = jnp.exp(-0.5 * x * x)
    half = 0.5 * t * bell * jnp.exp(poly)
    return jnp.where(x >= 0, 1.0 - half, half), bell


def normalize(values):
    center = values - jnp.mean(values, axis=-1, keepdims=True)
    inv = lax.rsqrt(jnp.mean(center * center, axis=-1, keepdims=True) + EPS)
    return center * inv, inv


def normalize_back(hat, inv, g):
    a = jnp.mean(g, axis=-1, keepdims=True)
    b = jnp.mean(g * hat, axis=-1, keepdims=True)
    return inv * (g - a - hat * b)


def rows_of(*vectors):
    lines = [jnp.sum(v, axis=0, keepdims=True) for v in vectors]
    pad = 8 - len(lines)
    return jnp.concatenate(lines + [jnp.zeros((pad, lines[0].shape[1]), f32)], axis=0)


def ffn_forward(flat, ctx, wout, vecs, wi, ib, wo, cot_pieces, rows_dev):
    n, width = flat.shape
    inner = wi.shape[1]
    count = len(cot_pieces)

    def kernel(flat_ref, ctx_ref, wout_ref, vec_ref, wi_ref, ib_ref, wo_ref, *refs):
        cot_refs = refs[:count]
        hat1_ref, inv1_ref, n1t_ref, active_ref, slope_ref = refs[count : count + 5]
        out_refs = refs[count + 5 : 2 * count + 5]
        dres_ref, douter_ref, small_ref, low, acc = refs[2 * count + 5 :]
        j = pl.program_id(0)

        @pl.when(j == 0)
        def _():
            resid = flat_ref[...].astype(f32) + dot(ctx_ref[...], wout_ref[...], 1, 0) + vec_ref[0:1]
            hat, inv = normalize(resid)
            hat1_ref[...] = hat
            inv1_ref[...] = jnp.broadcast_to(inv, inv1_ref.shape)
            normed = hat * vec_ref[1:2] + vec_ref[2:3]
            low[...] = normed.astype(bf16)
            n1t_ref[...] = normed.astype(bf16).T
            acc[...] = normed + vec_ref[3:4]

        inner = dot(low[...], wi_ref[...], 1, 0) + ib_ref[...]
        cdf, bell = upper_tail(inner)
        active = (inner * cdf).astype(bf16)
        active_ref[...] = active
        slope_ref[...] = (cdf + inner * bell * 0.3989422804014327).astype(bf16)
        acc[...] += dot(active, wo_ref[...], 1, 0)

        @pl.when(j == pl.num_programs(0) - 1)
        def _():
            valid_rows = cot_refs[0][rows_dev : rows_dev + EXTRA].astype(f32)[0:1]
            for r in cot_refs[1:]:
                valid_rows = valid_rows + r[rows_dev : rows_dev + EXTRA].astype(f32)[0:1]
            scale = 1.0 / jnp.maximum(valid_rows, 1.0)
            lines = [valid_rows * 0.0] * 3
            for k in range(count):
                part = slice(k * rows_dev, (k + 1) * rows_dev)
                hat, inv = normalize(acc[part])
                out_refs[k][...] = (hat * vec_ref[4:5] + vec_ref[5:6]).astype(bf16)
                cot = cot_refs[k][0:rows_dev].astype(f32) * scale
                dres = normalize_back(hat, inv, cot * vec_ref[4:5])
                dres_ref[part] = dres
                low_d = dres.astype(bf16)
                douter_ref[part] = low_d
                for i, v in enumerate((cot * hat, cot, low_d.astype(f32))):
                    lines[i] = lines[i] + jnp.sum(v, axis=0, keepdims=True)
            for i, v in enumerate(lines):
                small_ref[i : i + 1] = v

    full = lambda a: pl.BlockSpec(a.shape, lambda j: (0,) * a.ndim)
    whole = lambda shape: pl.BlockSpec(shape, lambda j: (0,) * len(shape))
    cols = pl.BlockSpec((n, BLOCK), lambda j: (0, j))
    outs = [
        (whole, (n, width), f32),
        (whole, (n, 128), f32),
        (whole, (width, n), bf16),
        (None, (n, inner), bf16),
        (None, (n, inner), bf16),
    ]
    outs += [(whole, (rows_dev, width), bf16)] * count
    outs += [(whole, (n, width), f32), (whole, (n, width), bf16), (whole, (8, width), f32)]
    got = pl.pallas_call(
        kernel,
        grid=(inner // BLOCK,),
        in_specs=[
            full(flat),
            full(ctx),
            full(wout),
            full(vecs),
            pl.BlockSpec((width, BLOCK), lambda j: (0, j)),
            pl.BlockSpec((1, BLOCK), lambda j: (0, j)),
            pl.BlockSpec((BLOCK, width), lambda j: (j, 0)),
        ]
        + [full(c) for c in cot_pieces],
        out_specs=[spec(shape) if spec else cols for spec, shape, _ in outs],
        out_shape=[jax.ShapeDtypeStruct(shape, kind) for _, shape, kind in outs],
        scratch_shapes=[pltpu.VMEM((n, width), bf16), pltpu.VMEM((n, width), f32)],
        name="ffn_fwd",
    )(flat, ctx, wout, vecs, wi, ib, wo, *cot_pieces)
    return got[:5], got[5 : 5 + count], got[5 + count :]


def inputs_backward(me, grads, weights, d_resid1, small1, small2, d_inner_bias, rows_dev, nseq, mem_rows):
    _, width = d_resid1.shape
    ib_rows = d_inner_bias.shape[1] // width

    def kernel(me_ref, dq_ref, dk_ref, dv_ref, wq_ref, wk_ref, wv_ref, dres_ref, s1_ref, s2_ref, ib_ref, *outs):
        pieces, small_ref = outs[:nseq], outs[nseq]
        seq_me = me_ref[1]
        first = me_ref[2]
        small_ref[...] = jnp.zeros_like(small_ref)
        d = dres_ref[...]
        for g, w in ((dq_ref, wq_ref), (dk_ref, wk_ref), (dv_ref, wv_ref)):
            d = d + dot(g[...], w[...], 1, 1)
        row = lax.broadcasted_iota(jnp.int32, (rows_dev, 1), 0)
        memory = jnp.zeros((EXTRA, width), f32)
        for k in range(nseq):
            part = d[k * rows_dev : (k + 1) * rows_dev]
            is_mem = jnp.logical_and(row < mem_rows, jnp.logical_and(seq_me == k, first != 0))
            pieces[k][...] = jnp.where(is_mem, 0.0, part).astype(bf16)
            memory = memory + jnp.where(is_mem[:EXTRA], part[:EXTRA], 0.0)
        small_ref[0, 0:1] = jnp.sum(dq_ref[...].astype(f32), axis=0, keepdims=True)
        small_ref[0, 1:2] = jnp.sum(dv_ref[...].astype(f32), axis=0, keepdims=True)
        small_ref[0, 2:5] = s1_ref[0:3]
        small_ref[0, 5:8] = s2_ref[0:3]
        for r in range(ib_rows):
            small_ref[1, r : r + 1] = ib_ref[0:1, r * width : (r + 1) * width]
        small_ref[2] = memory

    vmem = pl.BlockSpec(memory_space=pltpu.VMEM)
    got = pl.pallas_call(
        kernel,
        in_specs=[pl.BlockSpec(memory_space=pltpu.SMEM)] + [vmem] * 10,
        out_specs=[vmem] * (nseq + 1),
        out_shape=[jax.ShapeDtypeStruct((rows_dev, width), bf16)] * nseq
        + [jax.ShapeDtypeStruct((nseq, EXTRA, width), f32)],
        name="inputs_bwd",
    )(me, *grads, *weights, d_resid1, small1, small2, d_inner_bias)
    return got[:nseq], got[nseq]


class Plan:
    def __init__(self, mesh):
        self.ndp, self.nseq = mesh.shape["dp"], mesh.shape["seq"]
        bits = [("seq", b) for b in range(self.nseq.bit_length() - 1)]
        dp_bits = [("dp", b) for b in range(self.ndp.bit_length() - 1)]
        assert 2 ** len(bits) == self.nseq and 2 ** len(dp_bits) == self.ndp
        rest = bits[2:] + dp_bits[1:]
        self.first = bits[0]
        self.orders = [[bits[1], dp_bits[0]] + rest, [dp_bits[0], bits[1]] + rest]
        self.steps = len(self.orders[0])
        self.places = 1 << self.steps

    def flip(self, device, which):
        axis, b = which
        return device ^ ((1 << b) * (self.nseq if axis == "dp" else 1))

    def perm(self, step):
        devices = range(self.ndp * self.nseq)
        if step < 0:
            return [(d, self.flip(d, self.first)) for d in devices]
        return [(d, self.flip(d, self.orders[d & 1][step])) for d in devices]

    def place(self, dp_diff, seq_diff, half):
        value = {"dp": dp_diff, "seq": seq_diff}
        places = []
        for order in self.orders:
            p = 0
            for axis, b in order:
                p = p * 2 + ((value[axis] >> b) & 1)
            places.append(p)
        return jnp.where(half == 0, places[0], places[1])


def scatter_pieces(plan, me_ref, result, pieces, keep_ref, send_ref, rows, offset=0):
    dp_me = me_ref[0]
    seq_me = me_ref[1]
    for i, (dp, seq) in enumerate(pieces):
        tile = result[i * rows : (i + 1) * rows].astype(bf16)
        half = seq & 1
        at = plan.place(dp ^ dp_me, seq ^ seq_me, half)
        stay = half == (seq_me & 1)

        @pl.when(stay)
        def _(tile=tile, at=at):
            keep_ref[at, offset : offset + rows] = tile

        @pl.when(jnp.logical_not(stay))
        def _(tile=tile, at=at):
            send_ref[at, offset : offset + rows] = tile


def ffn_outer_grad(plan, me, active, d_outer):
    n, inner = active.shape
    width = d_outer.shape[1]
    rows = inner // (plan.ndp * plan.nseq)
    per = BLOCK // rows

    def kernel(me_ref, active_ref, d_ref, keep_ref, send_ref):
        j = pl.program_id(0)
        result = dot(active_ref[...], d_ref[...], 0, 0)
        pieces = [((j * per + i) // plan.nseq, (j * per + i) % plan.nseq) for i in range(per)]
        scatter_pieces(plan, me_ref, result, pieces, keep_ref, send_ref, rows)

    shape = jax.ShapeDtypeStruct((plan.places, rows, width), bf16)
    spec = pl.BlockSpec(shape.shape, lambda j, m: (0, 0, 0))
    return pl.pallas_call(
        kernel,
        grid_spec=pltpu.PrefetchScalarGridSpec(
            num_scalar_prefetch=1,
            grid=(inner // BLOCK,),
            in_specs=[
                pl.BlockSpec((n, BLOCK), lambda j, m: (0, j)),
                pl.BlockSpec((n, width), lambda j, m: (0, 0)),
            ],
            out_specs=[spec, spec],
        ),
        out_shape=[shape, shape],
        name="outer_grad",
    )(me, active, d_outer)


def ffn_backward(slope, d_outer, wo, wi, d_resid2, hat1, inv1, gain1, wout):
    n, inner = slope.shape
    width = d_outer.shape[1]

    def kernel(
        slope_ref, douter_ref, wo_ref, wi_ref, dres2_ref, hat1_ref, inv1_ref, gain_ref, wout_ref,
        dinner_ref, dres1_ref, dattn_ref, dctx_ref, ib_ref, small_ref, acc,
    ):
        j = pl.program_id(0)
        d_active = dot(douter_ref[...], wo_ref[...], 1, 1)
        d_inner = (d_active * slope_ref[...].astype(f32)).astype(bf16)
        dinner_ref[...] = d_inner
        ib_ref[...] = jnp.broadcast_to(jnp.sum(d_inner.astype(f32), axis=0, keepdims=True), ib_ref.shape)
        back = dot(d_inner, wi_ref[...], 1, 1)

        @pl.when(j == 0)
        def _():
            acc[...] = dres2_ref[...] + back

        @pl.when(j > 0)
        def _():
            acc[...] += back

        @pl.when(j == pl.num_programs(0) - 1)
        def _():
            d_normed = acc[...]
            hat = hat1_ref[...]
            dres = normalize_back(hat, inv1_ref[:, 0:1], d_normed * gain_ref[...])
            dres1_ref[...] = dres
            low = dres.astype(bf16)
            dattn_ref[...] = low
            dctx_ref[...] = dot(low, wout_ref[...], 1, 1).astype(bf16)
            small_ref[...] = rows_of(d_normed * hat, d_normed, low.astype(f32))

    full = lambda a: pl.BlockSpec(a.shape, lambda j: (0,) * a.ndim)
    whole = lambda shape: pl.BlockSpec(shape, lambda j: (0,) * len(shape))
    cols = pl.BlockSpec((n, BLOCK), lambda j: (0, j))
    return pl.pallas_call(
        kernel,
        grid=(inner // BLOCK,),
        in_specs=[
            cols,
            full(d_outer),
            pl.BlockSpec((BLOCK, width), lambda j: (j, 0)),
            pl.BlockSpec((width, BLOCK), lambda j: (0, j)),
            full(d_resid2),
            full(hat1),
            full(inv1),
            full(gain1),
            full(wout),
        ],
        out_specs=[
            cols,
            whole((n, width)),
            whole((n, width)),
            whole((n, width)),
            pl.BlockSpec((8, BLOCK), lambda j: (0, j)),
            whole((8, width)),
        ],
        scratch_shapes=[pltpu.VMEM((n, width), f32)],
        out_shape=[
            jax.ShapeDtypeStruct((n, inner), bf16),
            jax.ShapeDtypeStruct((n, width), f32),
            jax.ShapeDtypeStruct((n, width), bf16),
            jax.ShapeDtypeStruct((n, width), bf16),
            jax.ShapeDtypeStruct((8, inner), f32),
            jax.ShapeDtypeStruct((8, width), f32),
        ],
        name="ffn_bwd",
    )(slope, d_outer, wo, wi, d_resid2, hat1, inv1, gain1, wout)


def ffn_inner_grad(plan, me, n1t, d_inner):
    width, n = n1t.shape
    inner = d_inner.shape[1]
    rows = width // plan.ndp
    cols = inner // plan.nseq

    def kernel(me_ref, n1t_ref, d_ref, keep_ref, send_ref):
        j = pl.program_id(0)
        result = dot(n1t_ref[...], d_ref[...], 1, 0)
        scatter_pieces(plan, me_ref, result, [(i, j) for i in range(plan.ndp)], keep_ref, send_ref, rows)

    shape = jax.ShapeDtypeStruct((plan.places, rows, cols), bf16)
    spec = pl.BlockSpec(shape.shape, lambda j, m: (0, 0, 0))
    return pl.pallas_call(
        kernel,
        grid_spec=pltpu.PrefetchScalarGridSpec(
            num_scalar_prefetch=1,
            grid=(plan.nseq,),
            in_specs=[
                pl.BlockSpec((width, n), lambda j, m: (0, 0)),
                pl.BlockSpec((n, cols), lambda j, m: (0, j)),
            ],
            out_specs=[spec, spec],
        ),
        out_shape=[shape, shape],
        name="inner_grad",
    )(me, n1t, d_inner)


def finish_tokens(me, factor, pieces):
    count = len(pieces)

    def kernel(me_ref, factor_ref, *refs):
        out_ref = refs[count]
        for k in range(count):
            out_ref[me_ref[1] ^ k] = refs[k][...].astype(f32) * factor_ref[0]

    smem = pl.BlockSpec(memory_space=pltpu.SMEM)
    vmem = pl.BlockSpec(memory_space=pltpu.VMEM)
    return pl.pallas_call(
        kernel,
        in_specs=[smem, smem] + [vmem] * count,
        out_specs=vmem,
        out_shape=jax.ShapeDtypeStruct((count,) + pieces[0].shape, f32),
        name="finish_tok",
    )(me, factor, *pieces)


def finish_weights(me, factor, near, far, split):
    width = near.shape[2]
    count = 4
    shapes = []
    for start, rows, axis in split:
        if axis is None:
            shapes += [(rows, width)] * count
        else:
            shapes.append((count * rows, width) if axis == 0 else (rows, count * width))

    def kernel(me_ref, factor_ref, near_ref, far_ref, *outs):
        for s in range(count):
            diff = me_ref[1] ^ s
            at = diff >> 1
            o = 0
            for start, rows, axis in split:
                part = slice(start, start + rows)
                value = jnp.where((diff & 1) == 0, near_ref[at, part], far_ref[at, part])
                value = value.astype(f32) * factor_ref[0]
                if axis is None:
                    outs[o + s][...] = value
                    o += count
                elif axis == 0:
                    outs[o][s * rows : (s + 1) * rows] = value
                    o += 1
                else:
                    outs[o][:, s * width : (s + 1) * width] = value
                    o += 1

    smem = pl.BlockSpec(memory_space=pltpu.SMEM)
    vmem = pl.BlockSpec(memory_space=pltpu.VMEM)
    return pl.pallas_call(
        kernel,
        in_specs=[smem, smem, vmem, vmem],
        out_specs=[vmem] * len(shapes),
        out_shape=[jax.ShapeDtypeStruct(shape, f32) for shape in shapes],
    )(me, factor, near, far)


def attn_weight_grads(plan, me, flat, ctx, grads, small):
    n, width = flat.shape
    rows = width // plan.ndp

    def kernel(me_ref, flat_ref, ctx_ref, d0_ref, d1_ref, d2_ref, d3_ref, small_ref, keep_ref, send_ref, flat_t, ctx_t):
        flat_t[...] = flat_ref[...].T
        ctx_t[...] = ctx_ref[...].T
        for s, d_ref in enumerate((d0_ref, d1_ref, d2_ref, d3_ref)):
            left = ctx_t if s == 3 else flat_t
            result = dot(left[...], d_ref[...], 1, 0)
            pieces = [(i, s) for i in range(plan.ndp)]
            scatter_pieces(plan, me_ref, result, pieces, keep_ref, send_ref, rows)
            below = jnp.concatenate([small_ref[s].astype(bf16)] * plan.ndp, axis=0)
            scatter_pieces(plan, me_ref, below, pieces, keep_ref, send_ref, EXTRA, rows)

    shape = jax.ShapeDtypeStruct((plan.places, rows + EXTRA, width), bf16)
    return pl.pallas_call(
        kernel,
        in_specs=[pl.BlockSpec(memory_space=pltpu.SMEM)] + [pl.BlockSpec(memory_space=pltpu.VMEM)] * 7,
        out_specs=[pl.BlockSpec(memory_space=pltpu.VMEM)] * 2,
        out_shape=[shape, shape],
        scratch_shapes=[pltpu.VMEM((width, n), bf16), pltpu.VMEM((width, n), bf16)],
        name="attn_grad",
    )(me, flat, ctx, *grads, small)


def place_pieces(plan, me, blocks):
    dp = jnp.repeat(jnp.arange(plan.ndp), plan.nseq)
    seq = jnp.tile(jnp.arange(plan.nseq), plan.ndp)
    half = seq & 1
    place = plan.place(dp ^ me[0], seq ^ me[1], half)
    away = half ^ (me[1] & 1)
    flat = blocks.reshape((plan.ndp * plan.nseq,) + blocks.shape[2:])
    order = jnp.zeros((2 * plan.places,), jnp.int32).at[away * plan.places + place].set(jnp.arange(dp.shape[0]))
    both = jnp.take(flat, order, axis=0)
    return both[: plan.places], both[plan.places :]


def make_per_device(mesh):
    plan = Plan(mesh)
    ndp, nseq = plan.ndp, plan.nseq
    devices = ("dp", "seq")

    def total_of(terms):
        total = terms[0].astype(f32)
        for t in terms[1:]:
            total = total + t.astype(f32)
        return total

    def start_chunk(keep, send):
        return [keep, lax.ppermute(send, devices, plan.perm(-1))]

    def step_chunk(terms, step):
        half = terms[0].shape[0] // 2
        send = total_of([t[half:] for t in terms]).astype(bf16)
        got = lax.ppermute(send, devices, plan.perm(step))
        return [t[:half] for t in terms] + [got]

    def swap_seq(x, k):
        return lax.ppermute(x, "seq", [(i, i ^ k) for i in range(nseq)])

    def gather_seq(x):
        assert nseq == 4
        near = jnp.stack([x, swap_seq(x, 2)])
        return near, swap_seq(near, 1)

    def per_device(
        tokens,
        memory_init,
        query_weight,
        query_bias,
        key_weight,
        value_weight,
        value_bias,
        output_weight,
        output_bias,
        attn_gain,
        attn_shift,
        inner_weight,
        inner_bias,
        outer_weight,
        outer_bias,
        ffn_gain,
        ffn_shift,
        out_grad,
        lm_mask,
        doc_segments,
    ):
        seg_dev, rows_dev, width = tokens.shape
        assert seg_dev == nseq
        rows = rows_dev * nseq
        mem_rows = memory_init.shape[1]
        ff = inner_weight.shape[1]
        seq_index = lax.axis_index("seq")
        dp_index = lax.axis_index("dp")
        segs_total = ndp * seg_dev

        def to_segments(x):
            pieces = []
            for k in range(nseq):
                piece = lax.dynamic_index_in_dim(x, seq_index ^ k, axis=0, keepdims=False)
                pieces.append(swap_seq(piece, k) if k else piece)
            return pieces

        def to_rows(pieces, finish):
            out = None
            for k in range(nseq):
                piece = finish(pieces[k])
                if out is None:
                    out = jnp.zeros((nseq,) + piece.shape, piece.dtype)
                out = lax.dynamic_update_index_in_dim(out, piece, seq_index ^ k, axis=0)
            return out

        source = seq_index ^ jnp.arange(nseq, dtype=jnp.int32)
        position = source[:, None] * rows_dev + jnp.arange(rows_dev, dtype=jnp.int32)[None, :]
        is_mem = (position < mem_rows).reshape(rows)
        raw = jnp.concatenate(to_segments(tokens), axis=0)

        here = seq_index * rows_dev + jnp.arange(rows_dev, dtype=jnp.int32)
        valid = jnp.where((here < mem_rows)[None, :], 0, lm_mask)
        counts_here = jnp.sum(valid, axis=1)
        masked = jnp.where(valid[..., None] != 0, out_grad, jnp.zeros_like(out_grad))
        assert rows_dev <= 256
        assert seg_dev + 8 <= EXTRA
        low_counts = counts_here.astype(bf16)
        below = jnp.broadcast_to(jnp.pad(low_counts, (8, EXTRA - 8 - seg_dev))[None, :], (seg_dev, EXTRA))
        below = jnp.where(jnp.arange(EXTRA)[None, :] < 8, low_counts[:, None], below)
        count_rows = jnp.broadcast_to(below[:, :, None], (seg_dev, EXTRA, width))
        cot_pieces = to_segments(jnp.concatenate([masked, count_rows], axis=1))

        group = sum(jnp.sum(p[rows_dev + 8 : rows_dev + 8 + seg_dev, :128].astype(f32), axis=0) for p in cot_pieces)
        total = jnp.broadcast_to(group[None], (8, 128))
        for b in range(ndp.bit_length() - 1):
            total = total + lax.ppermute(total, "dp", [(i, i ^ (1 << b)) for i in range(ndp)])
        factor = total[0, 0] / segs_total

        seg_global = dp_index * seg_dev + seq_index
        starts = jnp.cumsum(doc_segments) - doc_segments
        is_first = jnp.any(starts == seg_global)
        me = jnp.stack([dp_index, seq_index, is_first.astype(jnp.int32)]).astype(jnp.int32)
        select = (is_first & is_mem)[:, None]
        table = jnp.concatenate([memory_init.T, jnp.zeros((rows_dev - mem_rows, width), bf16)], axis=0)
        table = jnp.concatenate([table] * nseq, axis=0)
        flat = jnp.where(select, table, raw)

        queries = (dot(flat, query_weight, 1, 0) + query_bias.astype(f32)).astype(bf16)
        keys = dot(flat, key_weight, 1, 0).astype(bf16)
        values = (dot(flat, value_weight, 1, 0) + value_bias.astype(f32)).astype(bf16)
        context, probs = attention_forward(queries, keys, values, 1, rows)
        zero = jnp.zeros_like(output_bias)
        vecs = jnp.stack(
            [output_bias, attn_gain, attn_shift, outer_bias, ffn_gain, ffn_shift, zero, zero]
        ).astype(f32)
        (hat1, inv1, n1t, active, slope), out_pieces, (d_resid2, d_outer, small2) = ffn_forward(
            flat,
            context,
            output_weight,
            vecs,
            inner_weight,
            inner_bias.astype(f32)[None],
            outer_weight,
            cot_pieces,
            rows_dev,
        )
        out_pieces = [swap_seq(p, k) if k else p for k, p in enumerate(out_pieces)]
        layer_out = to_rows(out_pieces, lambda p: p)

        aligned = (width // ndp) % 16 == 0 and (ff // (ndp * nseq)) % 16 == 0 and ff // nseq == BLOCK
        if aligned:
            keep, send = ffn_outer_grad(plan, me, active, d_outer)
        else:
            grad = dot(active, d_outer, 0, 0).astype(bf16)
            keep, send = place_pieces(plan, me, grad.reshape(ndp, nseq, -1, width))
        d_outer, keep, send = lax.optimization_barrier((d_outer, keep, send))
        outer = start_chunk(keep, send)
        d_inner, d_resid1, d_attn, d_context, d_inner_bias, small1 = ffn_backward(
            slope, d_outer, outer_weight, inner_weight, d_resid2, hat1, inv1, vecs[1:2], output_weight
        )
        outer = step_chunk(outer, 0)
        d_queries, d_keys, d_values = attention_backward(
            queries, keys, values, context, d_context, probs, 1, rows
        )
        d_queries, d_inner = lax.optimization_barrier((d_queries, d_inner))
        outer = step_chunk(outer, 1)
        if aligned:
            keep, send = ffn_inner_grad(plan, me, n1t, d_inner)
        else:
            grad = dot(n1t, d_inner, 1, 0).astype(bf16)
            grad = grad.reshape(ndp, width // ndp, nseq, ff // nseq).transpose(0, 2, 1, 3)
            keep, send = place_pieces(plan, me, grad)
        d_queries, keep, send = lax.optimization_barrier((d_queries, keep, send))
        inner = start_chunk(keep, send)
        outer = step_chunk(outer, 2)
        cut_pieces, small = inputs_backward(
            me,
            (d_queries, d_keys, d_values),
            (query_weight, key_weight, value_weight),
            d_resid1,
            small1,
            small2,
            d_inner_bias,
            rows_dev,
            nseq,
            mem_rows,
        )
        cut_pieces = [swap_seq(p, k) if k else p for k, p in enumerate(cut_pieces)]
        ib_rows = ff // width
        attn_grads = (d_queries, d_keys, d_values, d_attn)
        if aligned:
            keep, send = attn_weight_grads(plan, me, flat, context, attn_grads, small)
        else:
            blocks = []
            for s, d in enumerate(attn_grads):
                left = context if s == 3 else flat
                blocks.append(dot(left, d, 0, 0).astype(bf16).reshape(ndp, -1, width))
            blocks = jnp.stack(blocks, axis=1)
            below = jnp.broadcast_to(small.astype(bf16)[None], (ndp,) + small.shape)
            keep, send = place_pieces(plan, me, jnp.concatenate([blocks, below], axis=2))
        attn = start_chunk(keep, send)
        inner = step_chunk(inner, 0)
        for step in range(3, plan.steps):
            outer = step_chunk(outer, step)
        for step in range(1, plan.steps):
            inner = step_chunk(inner, step)
        for step in range(plan.steps):
            attn = step_chunk(attn, step)
        ffn_near, ffn_far = gather_seq(jnp.concatenate([total_of(outer)[0], total_of(inner)[0]], axis=0).astype(bf16))
        attn_near, attn_far = gather_seq(total_of(attn)[0].astype(bf16))

        part = width // ndp
        outer_rows = ff // (ndp * nseq)
        scale = factor.reshape(1)
        if aligned:
            tokens_grad = finish_tokens(me, scale, cut_pieces)
            g_outer, g_inner = finish_weights(me, scale, ffn_near, ffn_far, [(0, outer_rows, 0), (outer_rows, part, 1)])
            got = finish_weights(me, scale, attn_near, attn_far, [(0, part, None), (part, EXTRA, None)])
            g_query, g_key, g_value, g_output = got[:4]
            small_parts = got[4:]
        else:
            finish = lambda x: x.astype(f32) * factor
            tokens_grad = to_rows(cut_pieces, finish)

            def in_order(near, far):
                stack = jnp.stack([near[0], far[0], near[1], far[1]])
                return [finish(lax.dynamic_index_in_dim(stack, seq_index ^ k, 0, keepdims=False)) for k in range(nseq)]

            ffn_parts = in_order(ffn_near, ffn_far)
            g_outer = jnp.concatenate([p[:outer_rows] for p in ffn_parts], axis=0)
            g_inner = jnp.concatenate([p[outer_rows:] for p in ffn_parts], axis=1)
            attn_parts = in_order(attn_near, attn_far)
            g_query, g_key, g_value, g_output = [p[:part] for p in attn_parts]
            small_parts = [p[part:] for p in attn_parts]
        mine = lambda x: lax.dynamic_slice_in_dim(x, dp_index * part, part, axis=1)
        vec_rows = mine(small_parts[0][:8])
        g_memory = mine(small_parts[2][:mem_rows]).T
        inner_part = ff // ndp
        g_inner_bias = lax.dynamic_slice_in_dim(
            small_parts[1][:ib_rows].reshape(-1), dp_index * inner_part, inner_part, axis=0
        )
        g_query_bias, g_value_bias, g_gain1, g_shift1, g_output_bias, g_gain2, g_shift2, g_outer_bias = vec_rows
        return (
            layer_out,
            tokens_grad,
            g_query,
            g_query_bias,
            g_key,
            g_value,
            g_value_bias,
            g_output,
            g_output_bias,
            g_gain1,
            g_shift1,
            g_inner,
            g_inner_bias,
            g_outer,
            g_outer_bias,
            g_gain2,
            g_shift2,
            g_memory,
        )

    return per_device


def solution(mesh):
    rows = P("dp", "seq", None)
    in_specs = (rows,) + (P(),) * 16 + (rows, P("dp", "seq"), P())
    out_specs = (
        rows,
        rows,
        P("dp", None),
        P("dp"),
        P("dp", None),
        P("dp", None),
        P("dp"),
        P("dp", None),
        P("dp"),
        P("dp"),
        P("dp"),
        P("dp", None),
        P("dp"),
        P("dp", None),
        P("dp"),
        P("dp"),
        P("dp"),
        P("dp", None),
    )
    return jax.shard_map(
        make_per_device(mesh), mesh=mesh, in_specs=in_specs, out_specs=out_specs, check_vma=False
    )
```

```python
import jax
import jax.numpy as jnp
from jax import lax
from jax.experimental import pallas as pl
from jax.experimental.pallas import tpu as pltpu
from jax.sharding import PartitionSpec as P


HEAD_DIM = 64
EPS = 1e-06
LOG2E = 1.4426950408889634
BLOCK = 768
DIGITS = 16
EXTRA = 16
f32 = jnp.float32
bf16 = jnp.bfloat16


def dot(a, b, ca, cb):
    return lax.dot_general(a, b, (((ca,), (cb,)), ((), ())), preferred_element_type=f32)


def attn_fwd_kernel(q_ref, k_ref, v_ref, ctx_ref, p_ref):
    q = q_ref[...]
    k = k_ref[...]
    v = v_ref[...]
    lanes = lax.broadcasted_iota(jnp.int32, (1, 2 * HEAD_DIM), 1)
    ctx = None
    for h in range(2):
        mask = (lanes // HEAD_DIM) == h
        kh = jnp.where(mask, k, jnp.zeros_like(k))
        vh = jnp.where(mask, v, jnp.zeros_like(v))
        s = dot(q, kh, 1, 1) * (HEAD_DIM ** (-0.5) * LOG2E)
        e = jnp.exp2(s - jnp.max(s, axis=-1, keepdims=True))
        p = (e * (1.0 / jnp.sum(e, axis=-1, keepdims=True))).astype(bf16)
        p_ref[h] = p
        c = dot(p, vh, 1, 0)
        ctx = c if ctx is None else ctx + c
    ctx_ref[...] = ctx.astype(bf16)


def attn_bwd_kernel(q_ref, k_ref, v_ref, ctx_ref, dctx_ref, p_ref, dq_ref, dk_ref, dv_ref):
    q = q_ref[...]
    k = k_ref[...]
    v = v_ref[...]
    dctx = dctx_ref[...]
    prod = dctx.astype(f32) * ctx_ref[...].astype(f32)
    lanes = lax.broadcasted_iota(jnp.int32, (1, 2 * HEAD_DIM), 1)
    scale = HEAD_DIM ** (-0.5)
    dq = None
    dk = None
    dv = None
    for h in range(2):
        mask = (lanes // HEAD_DIM) == h
        zero = jnp.zeros_like(k)
        vh = jnp.where(mask, v, zero)
        kh = jnp.where(mask, k, zero)
        qh = jnp.where(mask, q, zero)
        dh = jnp.where(mask, dctx, zero)
        delta = jnp.sum(jnp.where(mask, prod, 0.0), axis=-1, keepdims=True)
        p = p_ref[h]
        dp = dot(dctx, vh, 1, 1)
        ds = (p.astype(f32) * (dp - delta)).astype(bf16)
        dqh = dot(ds, kh, 1, 0)
        dkh = dot(ds, qh, 0, 0)
        dvh = dot(p, dh, 0, 0)
        dq = dqh if dq is None else dq + dqh
        dk = dkh if dk is None else dk + dkh
        dv = dvh if dv is None else dv + dvh
    dq_ref[...] = (dq * scale).astype(bf16)
    dk_ref[...] = (dk * scale).astype(bf16)
    dv_ref[...] = dv.astype(bf16)


def attention_forward(q, k, v, segs, rows):
    block = 2 * HEAD_DIM
    pairs = q.shape[1] // block
    spec = pl.BlockSpec((rows, block), lambda s, h: (s, h))
    pspec = pl.BlockSpec((2, rows, rows), lambda s, h: (s * pairs + h, 0, 0))
    return pl.pallas_call(
        attn_fwd_kernel,
        grid=(segs, pairs),
        in_specs=[spec, spec, spec],
        out_specs=[spec, pspec],
        out_shape=[
            jax.ShapeDtypeStruct(q.shape, bf16),
            jax.ShapeDtypeStruct((segs * 2 * pairs, rows, rows), bf16),
        ],
        name="attn_fwd",
    )(q, k, v)


def attention_backward(q, k, v, ctx, dctx, p, segs, rows):
    block = 2 * HEAD_DIM
    pairs = q.shape[1] // block
    spec = pl.BlockSpec((rows, block), lambda s, h: (s, h))
    pspec = pl.BlockSpec((2, rows, rows), lambda s, h: (s * pairs + h, 0, 0))
    shape = jax.ShapeDtypeStruct(q.shape, bf16)
    return pl.pallas_call(
        attn_bwd_kernel,
        grid=(segs, pairs),
        in_specs=[spec] * 5 + [pspec],
        out_specs=[spec] * 3,
        out_shape=[shape] * 3,
        name="attn_bwd",
    )(q, k, v, ctx, dctx, p)


def upper_tail(x):
    z = jnp.abs(x) * (0.5 ** 0.5)
    t = 1.0 / (1.0 + 0.5 * z)
    poly = 0.17087277
    for c in (
        -0.82215223,
        1.48851587,
        -1.13520398,
        0.27886807,
        -0.18628806,
        0.09678418,
        0.37409196,
        1.00002368,
        -1.26551223,
    ):
        poly = poly * t + c
    bell = jnp.exp(-0.5 * x * x)
    half = 0.5 * t * bell * jnp.exp(poly)
    return jnp.where(x >= 0, 1.0 - half, half), bell


def normalize(values):
    center = values - jnp.mean(values, axis=-1, keepdims=True)
    inv = lax.rsqrt(jnp.mean(center * center, axis=-1, keepdims=True) + EPS)
    return center * inv, inv


def normalize_back(hat, inv, g):
    a = jnp.mean(g, axis=-1, keepdims=True)
    b = jnp.mean(g * hat, axis=-1, keepdims=True)
    return inv * (g - a - hat * b)


def rows_of(*vectors):
    lines = [jnp.sum(v, axis=0, keepdims=True) for v in vectors]
    pad = 8 - len(lines)
    return jnp.concatenate(lines + [jnp.zeros((pad, lines[0].shape[1]), f32)], axis=0)


def ffn_forward(flat, ctx, wout, vecs, wi, ib, wo, cot_pieces, rows_dev):
    n, width = flat.shape
    inner = wi.shape[1]
    count = len(cot_pieces)

    def kernel(flat_ref, ctx_ref, wout_ref, vec_ref, wi_ref, ib_ref, wo_ref, *refs):
        cot_refs = refs[:count]
        hat1_ref, inv1_ref, n1t_ref, active_ref, slope_ref = refs[count : count + 5]
        out_refs = refs[count + 5 : 2 * count + 5]
        dres_ref, douter_ref, small_ref, low, acc = refs[2 * count + 5 :]
        j = pl.program_id(0)

        @pl.when(j == 0)
        def _():
            resid = flat_ref[...].astype(f32) + dot(ctx_ref[...], wout_ref[...], 1, 0) + vec_ref[0:1]
            hat, inv = normalize(resid)
            hat1_ref[...] = hat
            inv1_ref[...] = jnp.broadcast_to(inv, inv1_ref.shape)
            normed = hat * vec_ref[1:2] + vec_ref[2:3]
            low[...] = normed.astype(bf16)
            n1t_ref[...] = normed.astype(bf16).T
            acc[...] = normed + vec_ref[3:4]

        inner = dot(low[...], wi_ref[...], 1, 0) + ib_ref[...]
        cdf, bell = upper_tail(inner)
        active = (inner * cdf).astype(bf16)
        active_ref[...] = active
        slope_ref[...] = (cdf + inner * bell * 0.3989422804014327).astype(bf16)
        acc[...] += dot(active, wo_ref[...], 1, 0)

        @pl.when(j == pl.num_programs(0) - 1)
        def _():
            valid_rows = cot_refs[0][rows_dev : rows_dev + EXTRA].astype(f32)[0:1]
            for r in cot_refs[1:]:
                valid_rows = valid_rows + r[rows_dev : rows_dev + EXTRA].astype(f32)[0:1]
            scale = 1.0 / jnp.maximum(valid_rows, 1.0)
            lines = [valid_rows * 0.0] * 3
            for k in range(count):
                part = slice(k * rows_dev, (k + 1) * rows_dev)
                hat, inv = normalize(acc[part])
                out_refs[k][...] = (hat * vec_ref[4:5] + vec_ref[5:6]).astype(bf16)
                cot = cot_refs[k][0:rows_dev].astype(f32) * scale
                dres = normalize_back(hat, inv, cot * vec_ref[4:5])
                dres_ref[part] = dres
                low_d = dres.astype(bf16)
                douter_ref[part] = low_d
                for i, v in enumerate((cot * hat, cot, low_d.astype(f32))):
                    lines[i] = lines[i] + jnp.sum(v, axis=0, keepdims=True)
            for i, v in enumerate(lines + [valid_rows]):
                small_ref[i : i + 1] = v

    full = lambda a: pl.BlockSpec(a.shape, lambda j: (0,) * a.ndim)
    whole = lambda shape: pl.BlockSpec(shape, lambda j: (0,) * len(shape))
    cols = pl.BlockSpec((n, BLOCK), lambda j: (0, j))
    outs = [
        (whole, (n, width), f32),
        (whole, (n, 128), f32),
        (whole, (width, n), bf16),
        (None, (n, inner), bf16),
        (None, (n, inner), bf16),
    ]
    outs += [(whole, (rows_dev, width), bf16)] * count
    outs += [(whole, (n, width), f32), (whole, (n, width), bf16), (whole, (8, width), f32)]
    got = pl.pallas_call(
        kernel,
        grid=(inner // BLOCK,),
        in_specs=[
            full(flat),
            full(ctx),
            full(wout),
            full(vecs),
            pl.BlockSpec((width, BLOCK), lambda j: (0, j)),
            pl.BlockSpec((1, BLOCK), lambda j: (0, j)),
            pl.BlockSpec((BLOCK, width), lambda j: (j, 0)),
        ]
        + [full(c) for c in cot_pieces],
        out_specs=[spec(shape) if spec else cols for spec, shape, _ in outs],
        out_shape=[jax.ShapeDtypeStruct(shape, kind) for _, shape, kind in outs],
        scratch_shapes=[pltpu.VMEM((n, width), bf16), pltpu.VMEM((n, width), f32)],
        name="ffn_fwd",
    )(flat, ctx, wout, vecs, wi, ib, wo, *cot_pieces)
    return got[:5], got[5 : 5 + count], got[5 + count :]


def inputs_backward(me, grads, weights, d_resid1, small1, small2, d_inner_bias, rows_dev, nseq, mem_rows):
    _, width = d_resid1.shape
    ib_rows = d_inner_bias.shape[1] // width

    def kernel(me_ref, dq_ref, dk_ref, dv_ref, wq_ref, wk_ref, wv_ref, dres_ref, s1_ref, s2_ref, ib_ref, *outs):
        pieces, small_ref = outs[:nseq], outs[nseq]
        seq_me = me_ref[1]
        first = me_ref[2]
        small_ref[...] = jnp.zeros_like(small_ref)
        d = dres_ref[...]
        for g, w in ((dq_ref, wq_ref), (dk_ref, wk_ref), (dv_ref, wv_ref)):
            d = d + dot(g[...], w[...], 1, 1)
        row = lax.broadcasted_iota(jnp.int32, (rows_dev, 1), 0)
        memory = jnp.zeros((EXTRA, width), f32)
        for k in range(nseq):
            part = d[k * rows_dev : (k + 1) * rows_dev]
            is_mem = jnp.logical_and(row < mem_rows, jnp.logical_and(seq_me == k, first != 0))
            pieces[k][...] = jnp.where(is_mem, 0.0, part).astype(bf16)
            memory = memory + jnp.where(is_mem[:EXTRA], part[:EXTRA], 0.0)
        small_ref[0, 0:1] = jnp.sum(dq_ref[...].astype(f32), axis=0, keepdims=True)
        small_ref[0, 1:2] = jnp.sum(dv_ref[...].astype(f32), axis=0, keepdims=True)
        small_ref[0, 2:5] = s1_ref[0:3]
        small_ref[0, 5:8] = s2_ref[0:3]
        for r in range(ib_rows):
            small_ref[1, r : r + 1] = ib_ref[0:1, r * width : (r + 1) * width]
        small_ref[2] = memory

    vmem = pl.BlockSpec(memory_space=pltpu.VMEM)
    got = pl.pallas_call(
        kernel,
        in_specs=[pl.BlockSpec(memory_space=pltpu.SMEM)] + [vmem] * 10,
        out_specs=[vmem] * (nseq + 1),
        out_shape=[jax.ShapeDtypeStruct((rows_dev, width), bf16)] * nseq
        + [jax.ShapeDtypeStruct((nseq, EXTRA, width), f32)],
        name="inputs_bwd",
    )(me, *grads, *weights, d_resid1, small1, small2, d_inner_bias)
    return got[:nseq], got[nseq]


class Plan:
    def __init__(self, mesh):
        self.ndp, self.nseq = mesh.shape["dp"], mesh.shape["seq"]
        bits = [("seq", b) for b in range(self.nseq.bit_length() - 1)]
        dp_bits = [("dp", b) for b in range(self.ndp.bit_length() - 1)]
        assert 2 ** len(bits) == self.nseq and 2 ** len(dp_bits) == self.ndp
        rest = bits[2:] + dp_bits[1:]
        self.first = bits[0]
        self.orders = [[bits[1], dp_bits[0]] + rest, [dp_bits[0]] + rest + [bits[1]]]
        self.steps = len(self.orders[0])
        self.places = 1 << self.steps

    def flip(self, device, which):
        axis, b = which
        return device ^ ((1 << b) * (self.nseq if axis == "dp" else 1))

    def perm(self, step):
        devices = range(self.ndp * self.nseq)
        if step < 0:
            return [(d, self.flip(d, self.first)) for d in devices]
        return [(d, self.flip(d, self.orders[d & 1][step])) for d in devices]

    def place(self, dp_diff, seq_diff, half):
        value = {"dp": dp_diff, "seq": seq_diff}
        places = []
        for order in self.orders:
            p = 0
            for axis, b in order:
                p = p * 2 + ((value[axis] >> b) & 1)
            places.append(p)
        return jnp.where(half == 0, places[0], places[1])


def scatter_pieces(plan, me_ref, result, pieces, keep_ref, send_ref, rows, offset=0):
    dp_me = me_ref[0]
    seq_me = me_ref[1]
    for i, (dp, seq) in enumerate(pieces):
        tile = result[i * rows : (i + 1) * rows].astype(bf16)
        half = seq & 1
        at = plan.place(dp ^ dp_me, seq ^ seq_me, half)
        stay = half == (seq_me & 1)

        @pl.when(stay)
        def _(tile=tile, at=at):
            keep_ref[at, offset : offset + rows] = tile

        @pl.when(jnp.logical_not(stay))
        def _(tile=tile, at=at):
            send_ref[at, offset : offset + rows] = tile


def count_bits(count_row):
    lane = lax.broadcasted_iota(jnp.int32, count_row.shape, 1)
    return ((count_row.astype(jnp.int32) >> jnp.minimum(lane, DIGITS)) & 1).astype(f32)


def ffn_outer_grad(plan, me, active, d_outer, small2):
    n, inner = active.shape
    width = d_outer.shape[1]
    rows = inner // (plan.ndp * plan.nseq)
    per = BLOCK // rows

    def kernel(me_ref, active_ref, d_ref, small_ref, keep_ref, send_ref):
        j = pl.program_id(0)

        @pl.when(j == 0)
        def _():
            below = jnp.broadcast_to(count_bits(small_ref[3:4]), (EXTRA, width)).astype(bf16)
            for p in range(plan.places):
                keep_ref[p, rows:] = below
                send_ref[p, rows:] = below

        result = dot(active_ref[...], d_ref[...], 0, 0)
        pieces = [((j * per + i) // plan.nseq, (j * per + i) % plan.nseq) for i in range(per)]
        scatter_pieces(plan, me_ref, result, pieces, keep_ref, send_ref, rows)

    shape = jax.ShapeDtypeStruct((plan.places, rows + EXTRA, width), bf16)
    spec = pl.BlockSpec(shape.shape, lambda j, m: (0, 0, 0))
    return pl.pallas_call(
        kernel,
        grid_spec=pltpu.PrefetchScalarGridSpec(
            num_scalar_prefetch=1,
            grid=(inner // BLOCK,),
            in_specs=[
                pl.BlockSpec((n, BLOCK), lambda j, m: (0, j)),
                pl.BlockSpec((n, width), lambda j, m: (0, 0)),
                pl.BlockSpec(small2.shape, lambda j, m: (0, 0)),
            ],
            out_specs=[spec, spec],
        ),
        out_shape=[shape, shape],
        name="outer_grad",
    )(me, active, d_outer, small2)


def ffn_backward(d_inner, wi, d_resid2, hat1, inv1, gain1, wout):
    n, inner = d_inner.shape
    width = d_resid2.shape[1]

    def kernel(
        dinner_ref, wi_ref, dres2_ref, hat1_ref, inv1_ref, gain_ref, wout_ref,
        dres1_ref, dattn_ref, dctx_ref, small_ref, acc,
    ):
        j = pl.program_id(0)
        back = dot(dinner_ref[...], wi_ref[...], 1, 1)

        @pl.when(j == 0)
        def _():
            acc[...] = dres2_ref[...] + back

        @pl.when(j > 0)
        def _():
            acc[...] += back

        @pl.when(j == pl.num_programs(0) - 1)
        def _():
            d_normed = acc[...]
            hat = hat1_ref[...]
            dres = normalize_back(hat, inv1_ref[:, 0:1], d_normed * gain_ref[...])
            dres1_ref[...] = dres
            low = dres.astype(bf16)
            dattn_ref[...] = low
            dctx_ref[...] = dot(low, wout_ref[...], 1, 1).astype(bf16)
            small_ref[...] = rows_of(d_normed * hat, d_normed, low.astype(f32))

    full = lambda a: pl.BlockSpec(a.shape, lambda j: (0,) * a.ndim)
    whole = lambda shape: pl.BlockSpec(shape, lambda j: (0,) * len(shape))
    return pl.pallas_call(
        kernel,
        grid=(inner // BLOCK,),
        in_specs=[
            pl.BlockSpec((n, BLOCK), lambda j: (0, j)),
            pl.BlockSpec((width, BLOCK), lambda j: (0, j)),
            full(d_resid2),
            full(hat1),
            full(inv1),
            full(gain1),
            full(wout),
        ],
        out_specs=[whole((n, width)), whole((n, width)), whole((n, width)), whole((8, width))],
        scratch_shapes=[pltpu.VMEM((n, width), f32)],
        out_shape=[
            jax.ShapeDtypeStruct((n, width), f32),
            jax.ShapeDtypeStruct((n, width), bf16),
            jax.ShapeDtypeStruct((n, width), bf16),
            jax.ShapeDtypeStruct((8, width), f32),
        ],
        name="ffn_bwd",
    )(d_inner, wi, d_resid2, hat1, inv1, gain1, wout)


def ffn_inner_grad(plan, me, n1t, slope, d_outer, wo):
    width, n = n1t.shape
    inner = slope.shape[1]
    rows = width // plan.ndp
    cols = inner // plan.nseq

    def kernel(me_ref, n1t_ref, slope_ref, douter_ref, wo_ref, keep_ref, send_ref, dinner_ref, ib_ref):
        j = pl.program_id(0)
        d_active = dot(douter_ref[...], wo_ref[...], 1, 1)
        d_inner = (d_active * slope_ref[...].astype(f32)).astype(bf16)
        dinner_ref[...] = d_inner
        ib_ref[...] = jnp.broadcast_to(jnp.sum(d_inner.astype(f32), axis=0, keepdims=True), ib_ref.shape)
        result = dot(n1t_ref[...], d_inner, 1, 0)
        scatter_pieces(plan, me_ref, result, [(i, j) for i in range(plan.ndp)], keep_ref, send_ref, rows)

    shape = jax.ShapeDtypeStruct((plan.places, rows, cols), bf16)
    spec = pl.BlockSpec(shape.shape, lambda j, m: (0, 0, 0))
    block = pl.BlockSpec((n, cols), lambda j, m: (0, j))
    return pl.pallas_call(
        kernel,
        grid_spec=pltpu.PrefetchScalarGridSpec(
            num_scalar_prefetch=1,
            grid=(plan.nseq,),
            in_specs=[
                pl.BlockSpec((width, n), lambda j, m: (0, 0)),
                block,
                pl.BlockSpec(d_outer.shape, lambda j, m: (0, 0)),
                pl.BlockSpec((cols, width), lambda j, m: (j, 0)),
            ],
            out_specs=[spec, spec, block, pl.BlockSpec((8, cols), lambda j, m: (0, j))],
        ),
        out_shape=[
            shape,
            shape,
            jax.ShapeDtypeStruct((n, inner), bf16),
            jax.ShapeDtypeStruct((8, inner), f32),
        ],
        name="inner_grad",
    )(me, n1t, slope, d_outer, wo)


def finish_tokens(me, factor, pieces):
    count = len(pieces)

    def kernel(me_ref, factor_ref, *refs):
        out_ref = refs[count]
        for k in range(count):
            out_ref[me_ref[1] ^ k] = refs[k][...].astype(f32) * factor_ref[0]

    smem = pl.BlockSpec(memory_space=pltpu.SMEM)
    vmem = pl.BlockSpec(memory_space=pltpu.VMEM)
    return pl.pallas_call(
        kernel,
        in_specs=[smem, smem] + [vmem] * count,
        out_specs=vmem,
        out_shape=jax.ShapeDtypeStruct((count,) + pieces[0].shape, f32),
        name="finish_tok",
    )(me, factor, *pieces)


def finish_weights(me, factor, near, far, split):
    width = near.shape[2]
    count = 4
    shapes = []
    for start, rows, axis in split:
        if axis is None:
            shapes += [(rows, width)] * count
        else:
            shapes.append((count * rows, width) if axis == 0 else (rows, count * width))

    def kernel(me_ref, factor_ref, near_ref, far_ref, *outs):
        for s in range(count):
            diff = me_ref[1] ^ s
            at = diff >> 1
            o = 0
            for start, rows, axis in split:
                part = slice(start, start + rows)
                value = jnp.where((diff & 1) == 0, near_ref[at, part], far_ref[at, part])
                value = value.astype(f32) * factor_ref[0]
                if axis is None:
                    outs[o + s][...] = value
                    o += count
                elif axis == 0:
                    outs[o][s * rows : (s + 1) * rows] = value
                    o += 1
                else:
                    outs[o][:, s * width : (s + 1) * width] = value
                    o += 1

    smem = pl.BlockSpec(memory_space=pltpu.SMEM)
    vmem = pl.BlockSpec(memory_space=pltpu.VMEM)
    return pl.pallas_call(
        kernel,
        in_specs=[smem, smem, vmem, vmem],
        out_specs=[vmem] * len(shapes),
        out_shape=[jax.ShapeDtypeStruct(shape, f32) for shape in shapes],
    )(me, factor, near, far)


def attn_weight_grads(plan, me, flat, ctx, grads, small):
    n, width = flat.shape
    rows = width // plan.ndp

    def kernel(me_ref, flat_ref, ctx_ref, d0_ref, d1_ref, d2_ref, d3_ref, small_ref, keep_ref, send_ref, flat_t, ctx_t):
        flat_t[...] = flat_ref[...].T
        ctx_t[...] = ctx_ref[...].T
        for s, d_ref in enumerate((d0_ref, d1_ref, d2_ref, d3_ref)):
            left = ctx_t if s == 3 else flat_t
            result = dot(left[...], d_ref[...], 1, 0)
            pieces = [(i, s) for i in range(plan.ndp)]
            scatter_pieces(plan, me_ref, result, pieces, keep_ref, send_ref, rows)
            below = jnp.concatenate([small_ref[s].astype(bf16)] * plan.ndp, axis=0)
            scatter_pieces(plan, me_ref, below, pieces, keep_ref, send_ref, EXTRA, rows)

    shape = jax.ShapeDtypeStruct((plan.places, rows + EXTRA, width), bf16)
    return pl.pallas_call(
        kernel,
        in_specs=[pl.BlockSpec(memory_space=pltpu.SMEM)] + [pl.BlockSpec(memory_space=pltpu.VMEM)] * 7,
        out_specs=[pl.BlockSpec(memory_space=pltpu.VMEM)] * 2,
        out_shape=[shape, shape],
        scratch_shapes=[pltpu.VMEM((width, n), bf16), pltpu.VMEM((width, n), bf16)],
        name="attn_grad",
    )(me, flat, ctx, *grads, small)


def place_pieces(plan, me, blocks):
    dp = jnp.repeat(jnp.arange(plan.ndp), plan.nseq)
    seq = jnp.tile(jnp.arange(plan.nseq), plan.ndp)
    half = seq & 1
    place = plan.place(dp ^ me[0], seq ^ me[1], half)
    away = half ^ (me[1] & 1)
    flat = blocks.reshape((plan.ndp * plan.nseq,) + blocks.shape[2:])
    order = jnp.zeros((2 * plan.places,), jnp.int32).at[away * plan.places + place].set(jnp.arange(dp.shape[0]))
    both = jnp.take(flat, order, axis=0)
    return both[: plan.places], both[plan.places :]


def make_per_device(mesh):
    plan = Plan(mesh)
    ndp, nseq = plan.ndp, plan.nseq
    devices = ("dp", "seq")

    def total_of(terms):
        total = terms[0].astype(f32)
        for t in terms[1:]:
            total = total + t.astype(f32)
        return total

    def start_chunk(keep, send):
        return [keep, lax.ppermute(send, devices, plan.perm(-1))]

    def step_chunk(terms, step):
        half = terms[0].shape[0] // 2
        send = total_of([t[half:] for t in terms]).astype(bf16)
        got = lax.ppermute(send, devices, plan.perm(step))
        return [t[:half] for t in terms] + [got]

    def swap_seq(x, k):
        return lax.ppermute(x, "seq", [(i, i ^ k) for i in range(nseq)])

    def gather_seq(x):
        assert nseq == 4
        near = jnp.stack([x, swap_seq(x, 2)])
        return near, swap_seq(near, 1)

    def per_device(
        tokens,
        memory_init,
        query_weight,
        query_bias,
        key_weight,
        value_weight,
        value_bias,
        output_weight,
        output_bias,
        attn_gain,
        attn_shift,
        inner_weight,
        inner_bias,
        outer_weight,
        outer_bias,
        ffn_gain,
        ffn_shift,
        out_grad,
        lm_mask,
        doc_segments,
    ):
        seg_dev, rows_dev, width = tokens.shape
        assert rows_dev * nseq < (1 << DIGITS) and ndp * nseq <= 256
        assert seg_dev == nseq
        rows = rows_dev * nseq
        mem_rows = memory_init.shape[1]
        ff = inner_weight.shape[1]
        seq_index = lax.axis_index("seq")
        dp_index = lax.axis_index("dp")
        segs_total = ndp * seg_dev

        def to_segments(x):
            pieces = []
            for k in range(nseq):
                piece = lax.dynamic_index_in_dim(x, seq_index ^ k, axis=0, keepdims=False)
                pieces.append(swap_seq(piece, k) if k else piece)
            return pieces

        def to_rows(pieces, finish):
            out = None
            for k in range(nseq):
                piece = finish(pieces[k])
                if out is None:
                    out = jnp.zeros((nseq,) + piece.shape, piece.dtype)
                out = lax.dynamic_update_index_in_dim(out, piece, seq_index ^ k, axis=0)
            return out

        source = seq_index ^ jnp.arange(nseq, dtype=jnp.int32)
        position = source[:, None] * rows_dev + jnp.arange(rows_dev, dtype=jnp.int32)[None, :]
        is_mem = (position < mem_rows).reshape(rows)
        raw = jnp.concatenate(to_segments(tokens), axis=0)

        here = seq_index * rows_dev + jnp.arange(rows_dev, dtype=jnp.int32)
        valid = jnp.where((here < mem_rows)[None, :], 0, lm_mask)
        counts_here = jnp.sum(valid, axis=1)
        masked = jnp.where(valid[..., None] != 0, out_grad, jnp.zeros_like(out_grad))
        assert rows_dev <= 256
        count_rows = jnp.broadcast_to(counts_here.astype(bf16)[:, None, None], (seg_dev, EXTRA, width))
        cot_pieces = to_segments(jnp.concatenate([masked, count_rows], axis=1))

        seg_global = dp_index * seg_dev + seq_index
        starts = jnp.cumsum(doc_segments) - doc_segments
        is_first = jnp.any(starts == seg_global)
        me = jnp.stack([dp_index, seq_index, is_first.astype(jnp.int32)]).astype(jnp.int32)
        select = (is_first & is_mem)[:, None]
        table = jnp.concatenate([memory_init.T, jnp.zeros((rows_dev - mem_rows, width), bf16)], axis=0)
        table = jnp.concatenate([table] * nseq, axis=0)
        flat = jnp.where(select, table, raw)

        queries = (dot(flat, query_weight, 1, 0) + query_bias.astype(f32)).astype(bf16)
        keys = dot(flat, key_weight, 1, 0).astype(bf16)
        values = (dot(flat, value_weight, 1, 0) + value_bias.astype(f32)).astype(bf16)
        context, probs = attention_forward(queries, keys, values, 1, rows)
        zero = jnp.zeros_like(output_bias)
        vecs = jnp.stack(
            [output_bias, attn_gain, attn_shift, outer_bias, ffn_gain, ffn_shift, zero, zero]
        ).astype(f32)
        (hat1, inv1, n1t, active, slope), out_pieces, (d_resid2, d_outer, small2) = ffn_forward(
            flat,
            context,
            output_weight,
            vecs,
            inner_weight,
            inner_bias.astype(f32)[None],
            outer_weight,
            cot_pieces,
            rows_dev,
        )
        out_pieces = [swap_seq(p, k) if k else p for k, p in enumerate(out_pieces)]
        layer_out = to_rows(out_pieces, lambda p: p)

        aligned = (width // ndp) % 16 == 0 and (ff // (ndp * nseq)) % 16 == 0 and ff // nseq == BLOCK
        if aligned:
            keep, send = ffn_outer_grad(plan, me, active, d_outer, small2)
        else:
            grad = dot(active, d_outer, 0, 0).astype(bf16)
            below = jnp.broadcast_to(count_bits(small2[3:4]), (ndp, nseq, EXTRA, width)).astype(bf16)
            blocks = jnp.concatenate([grad.reshape(ndp, nseq, -1, width), below], axis=2)
            keep, send = place_pieces(plan, me, blocks)
        d_outer, keep, send = lax.optimization_barrier((d_outer, keep, send))
        outer = start_chunk(keep, send)
        if aligned:
            keep, send, d_inner, d_inner_bias = ffn_inner_grad(plan, me, n1t, slope, d_outer, outer_weight)
        else:
            d_inner = (dot(d_outer, outer_weight, 1, 1) * slope.astype(f32)).astype(bf16)
            d_inner_bias = jnp.broadcast_to(jnp.sum(d_inner.astype(f32), axis=0), (8, ff))
            grad = dot(n1t, d_inner, 1, 0).astype(bf16)
            grad = grad.reshape(ndp, width // ndp, nseq, ff // nseq).transpose(0, 2, 1, 3)
            keep, send = place_pieces(plan, me, grad)
        inner = start_chunk(keep, send)
        outer = step_chunk(outer, 0)
        d_resid1, d_attn, d_context, small1 = ffn_backward(
            d_inner, inner_weight, d_resid2, hat1, inv1, vecs[1:2], output_weight
        )
        inner = step_chunk(inner, 0)
        d_queries, d_keys, d_values = attention_backward(
            queries, keys, values, context, d_context, probs, 1, rows
        )
        outer = step_chunk(outer, 1)
        cut_pieces, small = inputs_backward(
            me,
            (d_queries, d_keys, d_values),
            (query_weight, key_weight, value_weight),
            d_resid1,
            small1,
            small2,
            d_inner_bias,
            rows_dev,
            nseq,
            mem_rows,
        )
        cut_pieces = [swap_seq(p, k) if k else p for k, p in enumerate(cut_pieces)]
        ib_rows = ff // width
        attn_grads = (d_queries, d_keys, d_values, d_attn)
        if aligned:
            keep, send = attn_weight_grads(plan, me, flat, context, attn_grads, small)
        else:
            blocks = []
            for s, d in enumerate(attn_grads):
                left = context if s == 3 else flat
                blocks.append(dot(left, d, 0, 0).astype(bf16).reshape(ndp, -1, width))
            blocks = jnp.stack(blocks, axis=1)
            below = jnp.broadcast_to(small.astype(bf16)[None], (ndp,) + small.shape)
            keep, send = place_pieces(plan, me, jnp.concatenate([blocks, below], axis=2))
        attn = start_chunk(keep, send)
        for step in range(2, plan.steps):
            outer = step_chunk(outer, step)
        for step in range(1, plan.steps):
            inner = step_chunk(inner, step)
        for step in range(plan.steps):
            attn = step_chunk(attn, step)
        outer_rows = ff // (ndp * nseq)
        outer = total_of(outer)[0]
        total = jnp.sum(outer[outer_rows, :DIGITS] * (2.0 ** jnp.arange(DIGITS)).astype(f32))
        factor = total / segs_total
        ffn_near, ffn_far = gather_seq(jnp.concatenate([outer[:outer_rows], total_of(inner)[0]], axis=0).astype(bf16))
        attn_near, attn_far = gather_seq(total_of(attn)[0].astype(bf16))

        part = width // ndp
        scale = factor.reshape(1)
        if aligned:
            tokens_grad = finish_tokens(me, scale, cut_pieces)
            g_outer, g_inner = finish_weights(me, scale, ffn_near, ffn_far, [(0, outer_rows, 0), (outer_rows, part, 1)])
            got = finish_weights(me, scale, attn_near, attn_far, [(0, part, None), (part, EXTRA, None)])
            g_query, g_key, g_value, g_output = got[:4]
            small_parts = got[4:]
        else:
            finish = lambda x: x.astype(f32) * factor
            tokens_grad = to_rows(cut_pieces, finish)

            def in_order(near, far):
                stack = jnp.stack([near[0], far[0], near[1], far[1]])
                return [finish(lax.dynamic_index_in_dim(stack, seq_index ^ k, 0, keepdims=False)) for k in range(nseq)]

            ffn_parts = in_order(ffn_near, ffn_far)
            g_outer = jnp.concatenate([p[:outer_rows] for p in ffn_parts], axis=0)
            g_inner = jnp.concatenate([p[outer_rows:] for p in ffn_parts], axis=1)
            attn_parts = in_order(attn_near, attn_far)
            g_query, g_key, g_value, g_output = [p[:part] for p in attn_parts]
            small_parts = [p[part:] for p in attn_parts]
        mine = lambda x: lax.dynamic_slice_in_dim(x, dp_index * part, part, axis=1)
        vec_rows = mine(small_parts[0][:8])
        g_memory = mine(small_parts[2][:mem_rows]).T
        inner_part = ff // ndp
        g_inner_bias = lax.dynamic_slice_in_dim(
            small_parts[1][:ib_rows].reshape(-1), dp_index * inner_part, inner_part, axis=0
        )
        g_query_bias, g_value_bias, g_gain1, g_shift1, g_output_bias, g_gain2, g_shift2, g_outer_bias = vec_rows
        return (
            layer_out,
            tokens_grad,
            g_query,
            g_query_bias,
            g_key,
            g_value,
            g_value_bias,
            g_output,
            g_output_bias,
            g_gain1,
            g_shift1,
            g_inner,
            g_inner_bias,
            g_outer,
            g_outer_bias,
            g_gain2,
            g_shift2,
            g_memory,
        )

    return per_device


def solution(mesh):
    rows = P("dp", "seq", None)
    in_specs = (rows,) + (P(),) * 16 + (rows, P("dp", "seq"), P())
    out_specs = (
        rows,
        rows,
        P("dp", None),
        P("dp"),
        P("dp", None),
        P("dp", None),
        P("dp"),
        P("dp", None),
        P("dp"),
        P("dp"),
        P("dp"),
        P("dp", None),
        P("dp"),
        P("dp", None),
        P("dp"),
        P("dp"),
        P("dp"),
        P("dp", None),
    )
    return jax.shard_map(
        make_per_device(mesh), mesh=mesh, in_specs=in_specs, out_specs=out_specs, check_vma=False
    )
```

```python
import jax
import jax.numpy as jnp
from jax import lax
from jax.experimental import pallas as pl
from jax.experimental.pallas import tpu as pltpu
from jax.sharding import PartitionSpec as P


HEAD_DIM = 64
EPS = 1e-06
LOG2E = 1.4426950408889634
BLOCK = 768
PART = 256
DIGITS = 16
EXTRA = 8
f32 = jnp.float32
bf16 = jnp.bfloat16


def dot(a, b, ca, cb):
    return lax.dot_general(a, b, (((ca,), (cb,)), ((), ())), preferred_element_type=f32)


def attn_fwd_kernel(q_ref, k_ref, v_ref, ctx_ref, p_ref):
    q = q_ref[...]
    k = k_ref[...]
    v = v_ref[...]
    lanes = lax.broadcasted_iota(jnp.int32, (1, 2 * HEAD_DIM), 1)
    ctx = None
    for h in range(2):
        mask = (lanes // HEAD_DIM) == h
        kh = jnp.where(mask, k, jnp.zeros_like(k))
        vh = jnp.where(mask, v, jnp.zeros_like(v))
        s = dot(q, kh, 1, 1) * (HEAD_DIM ** (-0.5) * LOG2E)
        e = jnp.exp2(s - jnp.max(s, axis=-1, keepdims=True))
        p = (e * (1.0 / jnp.sum(e, axis=-1, keepdims=True))).astype(bf16)
        p_ref[h] = p
        c = dot(p, vh, 1, 0)
        ctx = c if ctx is None else ctx + c
    ctx_ref[...] = ctx.astype(bf16)


def attn_bwd_kernel(q_ref, k_ref, v_ref, ctx_ref, dctx_ref, p_ref, dq_ref, dk_ref, dv_ref):
    q = q_ref[...]
    k = k_ref[...]
    v = v_ref[...]
    dctx = dctx_ref[...]
    prod = dctx.astype(f32) * ctx_ref[...].astype(f32)
    lanes = lax.broadcasted_iota(jnp.int32, (1, 2 * HEAD_DIM), 1)
    scale = HEAD_DIM ** (-0.5)
    dq = None
    dk = None
    dv = None
    for h in range(2):
        mask = (lanes // HEAD_DIM) == h
        zero = jnp.zeros_like(k)
        vh = jnp.where(mask, v, zero)
        kh = jnp.where(mask, k, zero)
        qh = jnp.where(mask, q, zero)
        dh = jnp.where(mask, dctx, zero)
        delta = jnp.sum(jnp.where(mask, prod, 0.0), axis=-1, keepdims=True)
        p = p_ref[h]
        dp = dot(dctx, vh, 1, 1)
        ds = (p.astype(f32) * (dp - delta)).astype(bf16)
        dqh = dot(ds, kh, 1, 0)
        dkh = dot(ds, qh, 0, 0)
        dvh = dot(p, dh, 0, 0)
        dq = dqh if dq is None else dq + dqh
        dk = dkh if dk is None else dk + dkh
        dv = dvh if dv is None else dv + dvh
    dq_ref[...] = (dq * scale).astype(bf16)
    dk_ref[...] = (dk * scale).astype(bf16)
    dv_ref[...] = dv.astype(bf16)


def attention_forward(q, k, v, segs, rows):
    block = 2 * HEAD_DIM
    pairs = q.shape[1] // block
    spec = pl.BlockSpec((rows, block), lambda s, h: (s, h))
    pspec = pl.BlockSpec((2, rows, rows), lambda s, h: (s * pairs + h, 0, 0))
    return pl.pallas_call(
        attn_fwd_kernel,
        grid=(segs, pairs),
        in_specs=[spec, spec, spec],
        out_specs=[spec, pspec],
        out_shape=[
            jax.ShapeDtypeStruct(q.shape, bf16),
            jax.ShapeDtypeStruct((segs * 2 * pairs, rows, rows), bf16),
        ],
        name="attn_fwd",
    )(q, k, v)


def attention_backward(q, k, v, ctx, dctx, p, segs, rows):
    block = 2 * HEAD_DIM
    pairs = q.shape[1] // block
    spec = pl.BlockSpec((rows, block), lambda s, h: (s, h))
    pspec = pl.BlockSpec((2, rows, rows), lambda s, h: (s * pairs + h, 0, 0))
    shape = jax.ShapeDtypeStruct(q.shape, bf16)
    return pl.pallas_call(
        attn_bwd_kernel,
        grid=(segs, pairs),
        in_specs=[spec] * 5 + [pspec],
        out_specs=[spec] * 3,
        out_shape=[shape] * 3,
        name="attn_bwd",
    )(q, k, v, ctx, dctx, p)


def upper_tail(x):
    z = jnp.abs(x) * (0.5 ** 0.5)
    t = 1.0 / (1.0 + 0.5 * z)
    poly = 0.17087277
    for c in (
        -0.82215223,
        1.48851587,
        -1.13520398,
        0.27886807,
        -0.18628806,
        0.09678418,
        0.37409196,
        1.00002368,
        -1.26551223,
    ):
        poly = poly * t + c
    bell = jnp.exp(-0.5 * x * x)
    half = 0.5 * t * bell * jnp.exp(poly)
    return jnp.where(x >= 0, 1.0 - half, half), bell


def normalize(values):
    center = values - jnp.mean(values, axis=-1, keepdims=True)
    inv = lax.rsqrt(jnp.mean(center * center, axis=-1, keepdims=True) + EPS)
    return center * inv, inv


def normalize_back(hat, inv, g):
    a = jnp.mean(g, axis=-1, keepdims=True)
    b = jnp.mean(g * hat, axis=-1, keepdims=True)
    return inv * (g - a - hat * b)


def rows_of(*vectors):
    lines = [jnp.sum(v, axis=0, keepdims=True) for v in vectors]
    pad = 8 - len(lines)
    return jnp.concatenate(lines + [jnp.zeros((pad, lines[0].shape[1]), f32)], axis=0)


def ffn_forward(flat, ctx, wout, vecs, wi, ib, wo, cot_pieces, rows_dev):
    n, width = flat.shape
    inner = wi.shape[1]
    count = len(cot_pieces)

    def kernel(flat_ref, ctx_ref, wout_ref, vec_ref, wi_ref, ib_ref, wo_ref, *refs):
        cot_refs = refs[:count]
        hat1_ref, inv1_ref, n1t_ref, active_ref, slope_ref = refs[count : count + 5]
        out_refs = refs[count + 5 : 2 * count + 5]
        dres_ref, douter_ref, small_ref, low, acc = refs[2 * count + 5 :]
        j = pl.program_id(0)

        @pl.when(j == 0)
        def _():
            resid = flat_ref[...].astype(f32) + dot(ctx_ref[...], wout_ref[...], 1, 0) + vec_ref[0:1]
            hat, inv = normalize(resid)
            hat1_ref[...] = hat
            inv1_ref[...] = jnp.broadcast_to(inv, inv1_ref.shape)
            normed = hat * vec_ref[1:2] + vec_ref[2:3]
            low[...] = normed.astype(bf16)
            n1t_ref[...] = normed.astype(bf16).T
            acc[...] = normed + vec_ref[3:4]

        left = low[...]
        total = acc[...]
        for c in range(0, BLOCK, PART):
            part = slice(c, c + PART)
            inner = dot(left, wi_ref[:, part], 1, 0) + ib_ref[:, part]
            cdf, bell = upper_tail(inner)
            active = (inner * cdf).astype(bf16)
            active_ref[:, part] = active
            slope_ref[:, part] = (cdf + inner * bell * 0.3989422804014327).astype(bf16)
            total = total + dot(active, wo_ref[part], 1, 0)
        acc[...] = total

        @pl.when(j == pl.num_programs(0) - 1)
        def _():
            valid_rows = cot_refs[0][rows_dev : rows_dev + EXTRA].astype(f32)[0:1]
            for r in cot_refs[1:]:
                valid_rows = valid_rows + r[rows_dev : rows_dev + EXTRA].astype(f32)[0:1]
            scale = 1.0 / jnp.maximum(valid_rows, 1.0)
            lines = [valid_rows * 0.0] * 3
            for k in range(count):
                part = slice(k * rows_dev, (k + 1) * rows_dev)
                hat, inv = normalize(acc[part])
                out_refs[k][...] = (hat * vec_ref[4:5] + vec_ref[5:6]).astype(bf16)
                cot = cot_refs[k][0:rows_dev].astype(f32) * scale
                dres = normalize_back(hat, inv, cot * vec_ref[4:5])
                dres_ref[part] = dres
                low_d = dres.astype(bf16)
                douter_ref[part] = low_d
                for i, v in enumerate((cot * hat, cot, low_d.astype(f32))):
                    lines[i] = lines[i] + jnp.sum(v, axis=0, keepdims=True)
            for i, v in enumerate(lines + [valid_rows]):
                small_ref[i : i + 1] = v

    full = lambda a: pl.BlockSpec(a.shape, lambda j: (0,) * a.ndim)
    whole = lambda shape: pl.BlockSpec(shape, lambda j: (0,) * len(shape))
    cols = pl.BlockSpec((n, BLOCK), lambda j: (0, j))
    outs = [
        (whole, (n, width), f32),
        (whole, (n, 128), f32),
        (whole, (width, n), bf16),
        (None, (n, inner), bf16),
        (None, (n, inner), bf16),
    ]
    outs += [(whole, (rows_dev, width), bf16)] * count
    outs += [(whole, (n, width), f32), (whole, (n, width), bf16), (whole, (8, width), f32)]
    got = pl.pallas_call(
        kernel,
        grid=(inner // BLOCK,),
        in_specs=[
            full(flat),
            full(ctx),
            full(wout),
            full(vecs),
            pl.BlockSpec((width, BLOCK), lambda j: (0, j)),
            pl.BlockSpec((1, BLOCK), lambda j: (0, j)),
            pl.BlockSpec((BLOCK, width), lambda j: (j, 0)),
        ]
        + [full(c) for c in cot_pieces],
        out_specs=[spec(shape) if spec else cols for spec, shape, _ in outs],
        out_shape=[jax.ShapeDtypeStruct(shape, kind) for _, shape, kind in outs],
        scratch_shapes=[pltpu.VMEM((n, width), bf16), pltpu.VMEM((n, width), f32)],
        name="ffn_fwd",
    )(flat, ctx, wout, vecs, wi, ib, wo, *cot_pieces)
    return got[:5], got[5 : 5 + count], got[5 + count :]


def inputs_backward(me, grads, weights, d_resid1, small1, small2, d_inner_bias, rows_dev, nseq, mem_rows):
    _, width = d_resid1.shape
    ib_rows = d_inner_bias.shape[1] // width

    def kernel(me_ref, dq_ref, dk_ref, dv_ref, wq_ref, wk_ref, wv_ref, dres_ref, s1_ref, s2_ref, ib_ref, *outs):
        pieces, small_ref = outs[:nseq], outs[nseq]
        seq_me = me_ref[1]
        first = me_ref[2]
        small_ref[...] = jnp.zeros_like(small_ref)
        d = dres_ref[...]
        for g, w in ((dq_ref, wq_ref), (dk_ref, wk_ref), (dv_ref, wv_ref)):
            d = d + dot(g[...], w[...], 1, 1)
        row = lax.broadcasted_iota(jnp.int32, (rows_dev, 1), 0)
        memory = jnp.zeros((2 * EXTRA, width), f32)
        for k in range(nseq):
            part = d[k * rows_dev : (k + 1) * rows_dev]
            is_mem = jnp.logical_and(row < mem_rows, jnp.logical_and(seq_me == k, first != 0))
            pieces[k][...] = jnp.where(is_mem, 0.0, part).astype(bf16)
            memory = memory + jnp.where(is_mem[: 2 * EXTRA], part[: 2 * EXTRA], 0.0)
        small_ref[0, 0:1] = jnp.sum(dq_ref[...].astype(f32), axis=0, keepdims=True)
        small_ref[0, 1:2] = jnp.sum(dv_ref[...].astype(f32), axis=0, keepdims=True)
        small_ref[0, 2:5] = s1_ref[0:3]
        small_ref[0, 5:8] = s2_ref[0:3]
        for r in range(ib_rows):
            small_ref[1, r : r + 1] = ib_ref[0:1, r * width : (r + 1) * width]
        small_ref[2] = memory[:EXTRA]
        small_ref[3] = memory[EXTRA:]

    vmem = pl.BlockSpec(memory_space=pltpu.VMEM)
    got = pl.pallas_call(
        kernel,
        in_specs=[pl.BlockSpec(memory_space=pltpu.SMEM)] + [vmem] * 10,
        out_specs=[vmem] * (nseq + 1),
        out_shape=[jax.ShapeDtypeStruct((rows_dev, width), bf16)] * nseq
        + [jax.ShapeDtypeStruct((nseq, EXTRA, width), f32)],
        name="inputs_bwd",
    )(me, *grads, *weights, d_resid1, small1, small2, d_inner_bias)
    return got[:nseq], got[nseq]


class Plan:
    def __init__(self, mesh):
        self.ndp, self.nseq = mesh.shape["dp"], mesh.shape["seq"]
        bits = [("seq", b) for b in range(self.nseq.bit_length() - 1)]
        dp_bits = [("dp", b) for b in range(self.ndp.bit_length() - 1)]
        assert 2 ** len(bits) == self.nseq and 2 ** len(dp_bits) == self.ndp
        rest = bits[2:] + dp_bits[1:]
        self.first = bits[0]
        self.orders = [[bits[1], dp_bits[0]] + rest, [dp_bits[0]] + rest + [bits[1]]]
        self.steps = len(self.orders[0])
        self.places = 1 << self.steps

    def flip(self, device, which):
        axis, b = which
        return device ^ ((1 << b) * (self.nseq if axis == "dp" else 1))

    def perm(self, step):
        devices = range(self.ndp * self.nseq)
        if step < 0:
            return [(d, self.flip(d, self.first)) for d in devices]
        return [(d, self.flip(d, self.orders[d & 1][step])) for d in devices]

    def place(self, dp_diff, seq_diff, half):
        value = {"dp": dp_diff, "seq": seq_diff}
        places = []
        for order in self.orders:
            p = 0
            for axis, b in order:
                p = p * 2 + ((value[axis] >> b) & 1)
            places.append(p)
        return jnp.where(half == 0, places[0], places[1])


def scatter_pieces(plan, me_ref, result, pieces, keep_ref, send_ref, rows, offset=0):
    dp_me = me_ref[0]
    seq_me = me_ref[1]
    for i, (dp, seq) in enumerate(pieces):
        tile = result[i * rows : (i + 1) * rows].astype(bf16)
        half = seq & 1
        at = plan.place(dp ^ dp_me, seq ^ seq_me, half)
        stay = half == (seq_me & 1)

        @pl.when(stay)
        def _(tile=tile, at=at):
            keep_ref[at, offset : offset + rows] = tile

        @pl.when(jnp.logical_not(stay))
        def _(tile=tile, at=at):
            send_ref[at, offset : offset + rows] = tile


def count_bits(count_row):
    lane = lax.broadcasted_iota(jnp.int32, count_row.shape, 1)
    return ((count_row.astype(jnp.int32) >> jnp.minimum(lane, DIGITS)) & 1).astype(f32)


def ffn_outer_grad(plan, me, active, d_outer, small2):
    n, inner = active.shape
    width = d_outer.shape[1]
    rows = inner // (plan.ndp * plan.nseq)
    per = BLOCK // rows

    def kernel(me_ref, active_ref, d_ref, small_ref, keep_ref, send_ref):
        j = pl.program_id(0)

        @pl.when(j == 0)
        def _():
            below = jnp.broadcast_to(count_bits(small_ref[3:4]), (EXTRA, width)).astype(bf16)
            for p in range(plan.places):
                keep_ref[p, rows:] = below
                send_ref[p, rows:] = below

        result = dot(active_ref[...], d_ref[...], 0, 0)
        pieces = [((j * per + i) // plan.nseq, (j * per + i) % plan.nseq) for i in range(per)]
        scatter_pieces(plan, me_ref, result, pieces, keep_ref, send_ref, rows)

    shape = jax.ShapeDtypeStruct((plan.places, rows + EXTRA, width), bf16)
    spec = pl.BlockSpec(shape.shape, lambda j, m: (0, 0, 0))
    return pl.pallas_call(
        kernel,
        grid_spec=pltpu.PrefetchScalarGridSpec(
            num_scalar_prefetch=1,
            grid=(inner // BLOCK,),
            in_specs=[
                pl.BlockSpec((n, BLOCK), lambda j, m: (0, j)),
                pl.BlockSpec((n, width), lambda j, m: (0, 0)),
                pl.BlockSpec(small2.shape, lambda j, m: (0, 0)),
            ],
            out_specs=[spec, spec],
        ),
        out_shape=[shape, shape],
        name="outer_grad",
    )(me, active, d_outer, small2)


def ffn_backward(d_inner, wi, d_resid2, hat1, inv1, gain1, wout):
    n, inner = d_inner.shape
    width = d_resid2.shape[1]

    def kernel(
        dinner_ref, wi_ref, dres2_ref, hat1_ref, inv1_ref, gain_ref, wout_ref,
        dres1_ref, dattn_ref, dctx_ref, small_ref, acc,
    ):
        j = pl.program_id(0)
        back = dot(dinner_ref[...], wi_ref[...], 1, 1)

        @pl.when(j == 0)
        def _():
            acc[...] = dres2_ref[...] + back

        @pl.when(j > 0)
        def _():
            acc[...] += back

        @pl.when(j == pl.num_programs(0) - 1)
        def _():
            d_normed = acc[...]
            hat = hat1_ref[...]
            dres = normalize_back(hat, inv1_ref[:, 0:1], d_normed * gain_ref[...])
            dres1_ref[...] = dres
            low = dres.astype(bf16)
            dattn_ref[...] = low
            dctx_ref[...] = dot(low, wout_ref[...], 1, 1).astype(bf16)
            small_ref[...] = rows_of(d_normed * hat, d_normed, low.astype(f32))

    full = lambda a: pl.BlockSpec(a.shape, lambda j: (0,) * a.ndim)
    whole = lambda shape: pl.BlockSpec(shape, lambda j: (0,) * len(shape))
    return pl.pallas_call(
        kernel,
        grid=(inner // BLOCK,),
        in_specs=[
            pl.BlockSpec((n, BLOCK), lambda j: (0, j)),
            pl.BlockSpec((width, BLOCK), lambda j: (0, j)),
            full(d_resid2),
            full(hat1),
            full(inv1),
            full(gain1),
            full(wout),
        ],
        out_specs=[whole((n, width)), whole((n, width)), whole((n, width)), whole((8, width))],
        scratch_shapes=[pltpu.VMEM((n, width), f32)],
        out_shape=[
            jax.ShapeDtypeStruct((n, width), f32),
            jax.ShapeDtypeStruct((n, width), bf16),
            jax.ShapeDtypeStruct((n, width), bf16),
            jax.ShapeDtypeStruct((8, width), f32),
        ],
        name="ffn_bwd",
    )(d_inner, wi, d_resid2, hat1, inv1, gain1, wout)


def ffn_inner_grad(plan, me, n1t, slope, d_outer, wo):
    width, n = n1t.shape
    inner = slope.shape[1]
    rows = width // plan.ndp
    cols = inner // plan.nseq

    def kernel(me_ref, n1t_ref, slope_ref, douter_ref, wo_ref, keep_ref, send_ref, dinner_ref, ib_ref):
        j = pl.program_id(0)
        d_active = dot(douter_ref[...], wo_ref[...], 1, 1)
        d_inner = (d_active * slope_ref[...].astype(f32)).astype(bf16)
        dinner_ref[...] = d_inner
        ib_ref[...] = jnp.broadcast_to(jnp.sum(d_inner.astype(f32), axis=0, keepdims=True), ib_ref.shape)
        result = dot(n1t_ref[...], d_inner, 1, 0)
        scatter_pieces(plan, me_ref, result, [(i, j) for i in range(plan.ndp)], keep_ref, send_ref, rows)

    shape = jax.ShapeDtypeStruct((plan.places, rows, cols), bf16)
    spec = pl.BlockSpec(shape.shape, lambda j, m: (0, 0, 0))
    block = pl.BlockSpec((n, cols), lambda j, m: (0, j))
    return pl.pallas_call(
        kernel,
        grid_spec=pltpu.PrefetchScalarGridSpec(
            num_scalar_prefetch=1,
            grid=(plan.nseq,),
            in_specs=[
                pl.BlockSpec((width, n), lambda j, m: (0, 0)),
                block,
                pl.BlockSpec(d_outer.shape, lambda j, m: (0, 0)),
                pl.BlockSpec((cols, width), lambda j, m: (j, 0)),
            ],
            out_specs=[spec, spec, block, pl.BlockSpec((8, cols), lambda j, m: (0, j))],
        ),
        out_shape=[
            shape,
            shape,
            jax.ShapeDtypeStruct((n, inner), bf16),
            jax.ShapeDtypeStruct((8, inner), f32),
        ],
        name="inner_grad",
    )(me, n1t, slope, d_outer, wo)


def finish_rows(me, factor, pieces, kind):
    count = len(pieces)

    def kernel(me_ref, factor_ref, *refs):
        out_ref = refs[count]
        for k in range(count):
            piece = refs[k][...]
            out_ref[me_ref[1] ^ k] = piece if piece.dtype == kind else piece.astype(f32) * factor_ref[0]

    smem = pl.BlockSpec(memory_space=pltpu.SMEM)
    vmem = pl.BlockSpec(memory_space=pltpu.VMEM)
    return pl.pallas_call(
        kernel,
        in_specs=[smem, smem] + [vmem] * count,
        out_specs=vmem,
        out_shape=jax.ShapeDtypeStruct((count,) + pieces[0].shape, kind),
    )(me, factor, *pieces)


def finish_weights(me, factor, near, far, split):
    width = near.shape[2]
    count = 4
    shapes = []
    for start, rows, axis in split:
        if axis is None:
            shapes += [(rows, width)] * count
        else:
            shapes.append((count * rows, width) if axis == 0 else (rows, count * width))

    def kernel(me_ref, factor_ref, near_ref, far_ref, *outs):
        for s in range(count):
            diff = me_ref[1] ^ s
            at = diff >> 1
            o = 0
            for start, rows, axis in split:
                part = slice(start, start + rows)
                value = jnp.where((diff & 1) == 0, near_ref[at, part], far_ref[at, part])
                value = value.astype(f32) * factor_ref[0]
                if axis is None:
                    outs[o + s][...] = value
                    o += count
                elif axis == 0:
                    outs[o][s * rows : (s + 1) * rows] = value
                    o += 1
                else:
                    outs[o][:, s * width : (s + 1) * width] = value
                    o += 1

    smem = pl.BlockSpec(memory_space=pltpu.SMEM)
    vmem = pl.BlockSpec(memory_space=pltpu.VMEM)
    return pl.pallas_call(
        kernel,
        in_specs=[smem, smem, vmem, vmem],
        out_specs=[vmem] * len(shapes),
        out_shape=[jax.ShapeDtypeStruct(shape, f32) for shape in shapes],
    )(me, factor, near, far)


def attn_weight_grads(plan, me, flat, ctx, grads, small):
    n, width = flat.shape
    rows = width // plan.ndp

    def kernel(me_ref, flat_ref, ctx_ref, d0_ref, d1_ref, d2_ref, d3_ref, small_ref, keep_ref, send_ref, flat_t, ctx_t):
        flat_t[...] = flat_ref[...].T
        ctx_t[...] = ctx_ref[...].T
        for s, d_ref in enumerate((d0_ref, d1_ref, d2_ref, d3_ref)):
            left = ctx_t if s == 3 else flat_t
            result = dot(left[...], d_ref[...], 1, 0)
            pieces = [(i, s) for i in range(plan.ndp)]
            scatter_pieces(plan, me_ref, result, pieces, keep_ref, send_ref, rows)
            below = jnp.concatenate([small_ref[s].astype(bf16)] * plan.ndp, axis=0)
            scatter_pieces(plan, me_ref, below, pieces, keep_ref, send_ref, EXTRA, rows)

    shape = jax.ShapeDtypeStruct((plan.places, rows + EXTRA, width), bf16)
    return pl.pallas_call(
        kernel,
        in_specs=[pl.BlockSpec(memory_space=pltpu.SMEM)] + [pl.BlockSpec(memory_space=pltpu.VMEM)] * 7,
        out_specs=[pl.BlockSpec(memory_space=pltpu.VMEM)] * 2,
        out_shape=[shape, shape],
        scratch_shapes=[pltpu.VMEM((width, n), bf16), pltpu.VMEM((width, n), bf16)],
        name="attn_grad",
    )(me, flat, ctx, *grads, small)


def place_pieces(plan, me, blocks):
    dp = jnp.repeat(jnp.arange(plan.ndp), plan.nseq)
    seq = jnp.tile(jnp.arange(plan.nseq), plan.ndp)
    half = seq & 1
    place = plan.place(dp ^ me[0], seq ^ me[1], half)
    away = half ^ (me[1] & 1)
    flat = blocks.reshape((plan.ndp * plan.nseq,) + blocks.shape[2:])
    order = jnp.zeros((2 * plan.places,), jnp.int32).at[away * plan.places + place].set(jnp.arange(dp.shape[0]))
    both = jnp.take(flat, order, axis=0)
    return both[: plan.places], both[plan.places :]


def make_per_device(mesh):
    plan = Plan(mesh)
    ndp, nseq = plan.ndp, plan.nseq
    devices = ("dp", "seq")
    sent = {}

    def total_of(terms):
        total = terms[0].astype(f32)
        for t in terms[1:]:
            total = total + t.astype(f32)
        return total

    def start_chunk(keep, send):
        return [keep, lax.ppermute(send, devices, plan.perm(-1))]

    def step_chunk(name, terms, step, after=None):
        half = terms[0].shape[0] // 2
        if after is not None:
            *terms, _ = lax.optimization_barrier((*terms, after))
        send = total_of([t[half:] for t in terms]).astype(bf16)
        sent[name] = send
        got = lax.ppermute(send, devices, plan.perm(step))
        return [t[:half] for t in terms] + [got]

    def swap_seq(x, k):
        return lax.ppermute(x, "seq", [(i, i ^ k) for i in range(nseq)])

    def gather_seq(x):
        assert nseq == 4
        near = jnp.stack([x, swap_seq(x, 2)])
        return near, swap_seq(near, 1)

    def per_device(
        tokens,
        memory_init,
        query_weight,
        query_bias,
        key_weight,
        value_weight,
        value_bias,
        output_weight,
        output_bias,
        attn_gain,
        attn_shift,
        inner_weight,
        inner_bias,
        outer_weight,
        outer_bias,
        ffn_gain,
        ffn_shift,
        out_grad,
        lm_mask,
        doc_segments,
    ):
        seg_dev, rows_dev, width = tokens.shape
        assert rows_dev * nseq < (1 << DIGITS) and ndp * nseq <= 256
        assert seg_dev == nseq
        rows = rows_dev * nseq
        mem_rows = memory_init.shape[1]
        ff = inner_weight.shape[1]
        seq_index = lax.axis_index("seq")
        dp_index = lax.axis_index("dp")
        segs_total = ndp * seg_dev

        def to_segments(x):
            pieces = [lax.dynamic_index_in_dim(x, seq_index ^ k, axis=0, keepdims=False) for k in range(nseq)]
            return [swap_seq(p, k) if k else p for k, p in enumerate(pieces)], pieces

        def to_rows(pieces, finish):
            out = None
            for k in range(nseq):
                piece = finish(pieces[k])
                if out is None:
                    out = jnp.zeros((nseq,) + piece.shape, piece.dtype)
                out = lax.dynamic_update_index_in_dim(out, piece, seq_index ^ k, axis=0)
            return out

        source = seq_index ^ jnp.arange(nseq, dtype=jnp.int32)
        position = source[:, None] * rows_dev + jnp.arange(rows_dev, dtype=jnp.int32)[None, :]
        is_mem = (position < mem_rows).reshape(rows)
        pieces, sliced = to_segments(tokens)
        raw = jnp.concatenate(pieces, axis=0)
        out_grad, lm_mask, *_ = lax.optimization_barrier((out_grad, lm_mask, *sliced))

        here = seq_index * rows_dev + jnp.arange(rows_dev, dtype=jnp.int32)
        valid = jnp.where((here < mem_rows)[None, :], 0, lm_mask)
        counts_here = jnp.sum(valid, axis=1)
        masked = jnp.where(valid[..., None] != 0, out_grad, jnp.zeros_like(out_grad))
        assert rows_dev <= 256
        count_rows = jnp.broadcast_to(counts_here.astype(bf16)[:, None, None], (seg_dev, EXTRA, width))
        cot_pieces, _ = to_segments(jnp.concatenate([masked, count_rows], axis=1))

        seg_global = dp_index * seg_dev + seq_index
        starts = jnp.cumsum(doc_segments) - doc_segments
        is_first = jnp.any(starts == seg_global)
        me = jnp.stack([dp_index, seq_index, is_first.astype(jnp.int32)]).astype(jnp.int32)
        select = (is_first & is_mem)[:, None]
        table = jnp.concatenate([memory_init.T, jnp.zeros((rows_dev - mem_rows, width), bf16)], axis=0)
        table = jnp.concatenate([table] * nseq, axis=0)
        flat = jnp.where(select, table, raw)

        queries = (dot(flat, query_weight, 1, 0) + query_bias.astype(f32)).astype(bf16)
        keys = dot(flat, key_weight, 1, 0).astype(bf16)
        values = (dot(flat, value_weight, 1, 0) + value_bias.astype(f32)).astype(bf16)
        context, probs = attention_forward(queries, keys, values, 1, rows)
        zero = jnp.zeros_like(output_bias)
        vecs = jnp.stack(
            [output_bias, attn_gain, attn_shift, outer_bias, ffn_gain, ffn_shift, zero, zero]
        ).astype(f32)
        (hat1, inv1, n1t, active, slope), out_pieces, (d_resid2, d_outer, small2) = ffn_forward(
            flat,
            context,
            output_weight,
            vecs,
            inner_weight,
            inner_bias.astype(f32)[None],
            outer_weight,
            cot_pieces,
            rows_dev,
        )
        out_pieces = [swap_seq(p, k) if k else p for k, p in enumerate(out_pieces)]
        layer_out = finish_rows(me, jnp.ones((1,), f32), out_pieces, bf16)

        aligned = (width // ndp) % 16 == 0 and (ff // (ndp * nseq)) % 16 == 0 and ff // nseq == BLOCK
        if aligned:
            keep, send = ffn_outer_grad(plan, me, active, d_outer, small2)
        else:
            grad = dot(active, d_outer, 0, 0).astype(bf16)
            below = jnp.broadcast_to(count_bits(small2[3:4]), (ndp, nseq, EXTRA, width)).astype(bf16)
            blocks = jnp.concatenate([grad.reshape(ndp, nseq, -1, width), below], axis=2)
            keep, send = place_pieces(plan, me, blocks)
        d_outer, keep, send = lax.optimization_barrier((d_outer, keep, send))
        outer = start_chunk(keep, send)
        if aligned:
            keep, send, d_inner, d_inner_bias = ffn_inner_grad(plan, me, n1t, slope, d_outer, outer_weight)
        else:
            d_inner = (dot(d_outer, outer_weight, 1, 1) * slope.astype(f32)).astype(bf16)
            d_inner_bias = jnp.broadcast_to(jnp.sum(d_inner.astype(f32), axis=0), (8, ff))
            grad = dot(n1t, d_inner, 1, 0).astype(bf16)
            grad = grad.reshape(ndp, width // ndp, nseq, ff // nseq).transpose(0, 2, 1, 3)
            keep, send = place_pieces(plan, me, grad)
        inner = start_chunk(keep, send)
        outer = step_chunk("o", outer, 0)
        d_resid1, d_attn, d_context, small1 = ffn_backward(
            d_inner, inner_weight, d_resid2, hat1, inv1, vecs[1:2], output_weight
        )
        inner = step_chunk("i", inner, 0)
        d_queries, d_keys, d_values = attention_backward(
            queries, keys, values, context, d_context, probs, 1, rows
        )
        outer = step_chunk("o", outer, 1)
        cut_pieces, small = inputs_backward(
            me,
            (d_queries, d_keys, d_values),
            (query_weight, key_weight, value_weight),
            d_resid1,
            small1,
            small2,
            d_inner_bias,
            rows_dev,
            nseq,
            mem_rows,
        )
        cut_pieces = [swap_seq(p, k) if k else p for k, p in enumerate(cut_pieces)]
        ib_rows = ff // width
        attn_grads = (d_queries, d_keys, d_values, d_attn)
        if aligned:
            keep, send = attn_weight_grads(plan, me, flat, context, attn_grads, small)
        else:
            blocks = []
            for s, d in enumerate(attn_grads):
                left = context if s == 3 else flat
                blocks.append(dot(left, d, 0, 0).astype(bf16).reshape(ndp, -1, width))
            blocks = jnp.stack(blocks, axis=1)
            below = jnp.broadcast_to(small.astype(bf16)[None], (ndp,) + small.shape)
            keep, send = place_pieces(plan, me, jnp.concatenate([blocks, below], axis=2))
        attn = start_chunk(keep, send)
        for step in range(2, plan.steps):
            outer = step_chunk("o", outer, step)
        inner = step_chunk("i", inner, 1)
        attn = step_chunk("t", attn, 0)
        inner = step_chunk("i", inner, 2, sent["t"])
        attn = step_chunk("t", attn, 1)
        for step in range(3, plan.steps):
            inner = step_chunk("i", inner, step, sent["t"])
        for step in range(2, plan.steps):
            attn = step_chunk("t", attn, step)
            if step == 2:
                after_third = sent["t"]
        outer_rows = ff // (ndp * nseq)
        outer = total_of(outer)[0]
        total = jnp.sum(outer[outer_rows, :DIGITS] * (2.0 ** jnp.arange(DIGITS)).astype(f32))
        factor = total / segs_total
        *inner, _ = lax.optimization_barrier((*inner, after_third))
        ffn_near, ffn_far = gather_seq(jnp.concatenate([outer[:outer_rows], total_of(inner)[0]], axis=0).astype(bf16))
        attn_near, attn_far = gather_seq(total_of(attn)[0].astype(bf16))

        part = width // ndp
        scale = factor.reshape(1)
        if aligned:
            tokens_grad = finish_rows(me, scale, cut_pieces, f32)
            g_outer, g_inner = finish_weights(me, scale, ffn_near, ffn_far, [(0, outer_rows, 0), (outer_rows, part, 1)])
            got = finish_weights(me, scale, attn_near, attn_far, [(0, part, None), (part, EXTRA, None)])
            g_query, g_key, g_value, g_output = got[:4]
            small_parts = got[4:]
        else:
            finish = lambda x: x.astype(f32) * factor
            tokens_grad = to_rows(cut_pieces, finish)

            def in_order(near, far):
                stack = jnp.stack([near[0], far[0], near[1], far[1]])
                return [finish(lax.dynamic_index_in_dim(stack, seq_index ^ k, 0, keepdims=False)) for k in range(nseq)]

            ffn_parts = in_order(ffn_near, ffn_far)
            g_outer = jnp.concatenate([p[:outer_rows] for p in ffn_parts], axis=0)
            g_inner = jnp.concatenate([p[outer_rows:] for p in ffn_parts], axis=1)
            attn_parts = in_order(attn_near, attn_far)
            g_query, g_key, g_value, g_output = [p[:part] for p in attn_parts]
            small_parts = [p[part:] for p in attn_parts]
        mine = lambda x: lax.dynamic_slice_in_dim(x, dp_index * part, part, axis=1)
        vec_rows = mine(small_parts[0][:8])
        g_memory = mine(jnp.concatenate([small_parts[2], small_parts[3]])[:mem_rows]).T
        inner_part = ff // ndp
        g_inner_bias = lax.dynamic_slice_in_dim(
            small_parts[1][:ib_rows].reshape(-1), dp_index * inner_part, inner_part, axis=0
        )
        g_query_bias, g_value_bias, g_gain1, g_shift1, g_output_bias, g_gain2, g_shift2, g_outer_bias = vec_rows
        return (
            layer_out,
            tokens_grad,
            g_query,
            g_query_bias,
            g_key,
            g_value,
            g_value_bias,
            g_output,
            g_output_bias,
            g_gain1,
            g_shift1,
            g_inner,
            g_inner_bias,
            g_outer,
            g_outer_bias,
            g_gain2,
            g_shift2,
            g_memory,
        )

    return per_device


def solution(mesh):
    rows = P("dp", "seq", None)
    in_specs = (rows,) + (P(),) * 16 + (rows, P("dp", "seq"), P())
    out_specs = (
        rows,
        rows,
        P("dp", None),
        P("dp"),
        P("dp", None),
        P("dp", None),
        P("dp"),
        P("dp", None),
        P("dp"),
        P("dp"),
        P("dp"),
        P("dp", None),
        P("dp"),
        P("dp", None),
        P("dp"),
        P("dp"),
        P("dp"),
        P("dp", None),
    )
    return jax.shard_map(
        make_per_device(mesh), mesh=mesh, in_specs=in_specs, out_specs=out_specs, check_vma=False
    )
```

```python
import jax
import jax.numpy as jnp
from jax import lax
from jax.experimental import pallas as pl
from jax.experimental.pallas import tpu as pltpu
from jax.sharding import PartitionSpec as P


HEAD_DIM = 64
EPS = 1e-06
LOG2E = 1.4426950408889634
BLOCK = 768
PART = 768
DIGITS = 16
EXTRA = 8
f32 = jnp.float32
bf16 = jnp.bfloat16


def dot(a, b, ca, cb):
    return lax.dot_general(a, b, (((ca,), (cb,)), ((), ())), preferred_element_type=f32)


def attn_fwd_kernel(q_ref, k_ref, v_ref, ctx_ref, p_ref):
    q = q_ref[...]
    k = k_ref[...]
    v = v_ref[...]
    lanes = lax.broadcasted_iota(jnp.int32, (1, 2 * HEAD_DIM), 1)
    ctx = None
    for h in range(2):
        mask = (lanes // HEAD_DIM) == h
        kh = jnp.where(mask, k, jnp.zeros_like(k))
        vh = jnp.where(mask, v, jnp.zeros_like(v))
        s = dot(q, kh, 1, 1) * (HEAD_DIM ** (-0.5) * LOG2E)
        e = jnp.exp2(s - jnp.max(s, axis=-1, keepdims=True))
        p = (e * (1.0 / jnp.sum(e, axis=-1, keepdims=True))).astype(bf16)
        p_ref[h] = p
        c = dot(p, vh, 1, 0)
        ctx = c if ctx is None else ctx + c
    ctx_ref[...] = ctx.astype(bf16)


def attn_bwd_kernel(q_ref, k_ref, v_ref, ctx_ref, dctx_ref, p_ref, dq_ref, dk_ref, dv_ref):
    q = q_ref[...]
    k = k_ref[...]
    v = v_ref[...]
    dctx = dctx_ref[...]
    prod = dctx.astype(f32) * ctx_ref[...].astype(f32)
    lanes = lax.broadcasted_iota(jnp.int32, (1, 2 * HEAD_DIM), 1)
    scale = HEAD_DIM ** (-0.5)
    dq = None
    dk = None
    dv = None
    for h in range(2):
        mask = (lanes // HEAD_DIM) == h
        zero = jnp.zeros_like(k)
        vh = jnp.where(mask, v, zero)
        kh = jnp.where(mask, k, zero)
        qh = jnp.where(mask, q, zero)
        dh = jnp.where(mask, dctx, zero)
        delta = jnp.sum(jnp.where(mask, prod, 0.0), axis=-1, keepdims=True)
        p = p_ref[h]
        dp = dot(dctx, vh, 1, 1)
        ds = (p.astype(f32) * (dp - delta)).astype(bf16)
        dqh = dot(ds, kh, 1, 0)
        dkh = dot(ds, qh, 0, 0)
        dvh = dot(p, dh, 0, 0)
        dq = dqh if dq is None else dq + dqh
        dk = dkh if dk is None else dk + dkh
        dv = dvh if dv is None else dv + dvh
    dq_ref[...] = (dq * scale).astype(bf16)
    dk_ref[...] = (dk * scale).astype(bf16)
    dv_ref[...] = dv.astype(bf16)


def attention_forward(q, k, v, segs, rows):
    block = 2 * HEAD_DIM
    pairs = q.shape[1] // block
    spec = pl.BlockSpec((rows, block), lambda s, h: (s, h))
    pspec = pl.BlockSpec((2, rows, rows), lambda s, h: (s * pairs + h, 0, 0))
    return pl.pallas_call(
        attn_fwd_kernel,
        grid=(segs, pairs),
        in_specs=[spec, spec, spec],
        out_specs=[spec, pspec],
        out_shape=[
            jax.ShapeDtypeStruct(q.shape, bf16),
            jax.ShapeDtypeStruct((segs * 2 * pairs, rows, rows), bf16),
        ],
        name="attn_fwd",
    )(q, k, v)


def attention_backward(q, k, v, ctx, dctx, p, segs, rows):
    block = 2 * HEAD_DIM
    pairs = q.shape[1] // block
    spec = pl.BlockSpec((rows, block), lambda s, h: (s, h))
    pspec = pl.BlockSpec((2, rows, rows), lambda s, h: (s * pairs + h, 0, 0))
    shape = jax.ShapeDtypeStruct(q.shape, bf16)
    return pl.pallas_call(
        attn_bwd_kernel,
        grid=(segs, pairs),
        in_specs=[spec] * 5 + [pspec],
        out_specs=[spec] * 3,
        out_shape=[shape] * 3,
        name="attn_bwd",
    )(q, k, v, ctx, dctx, p)


def upper_tail(x):
    z = jnp.abs(x) * (0.5 ** 0.5)
    t = 1.0 / (1.0 + 0.5 * z)
    poly = 0.17087277
    for c in (
        -0.82215223,
        1.48851587,
        -1.13520398,
        0.27886807,
        -0.18628806,
        0.09678418,
        0.37409196,
        1.00002368,
        -1.26551223,
    ):
        poly = poly * t + c
    bell = jnp.exp(-0.5 * x * x)
    half = 0.5 * t * bell * jnp.exp(poly)
    return jnp.where(x >= 0, 1.0 - half, half), bell


def normalize(values):
    center = values - jnp.mean(values, axis=-1, keepdims=True)
    inv = lax.rsqrt(jnp.mean(center * center, axis=-1, keepdims=True) + EPS)
    return center * inv, inv


def normalize_back(hat, inv, g):
    a = jnp.mean(g, axis=-1, keepdims=True)
    b = jnp.mean(g * hat, axis=-1, keepdims=True)
    return inv * (g - a - hat * b)


def rows_of(*vectors):
    lines = [jnp.sum(v, axis=0, keepdims=True) for v in vectors]
    pad = 8 - len(lines)
    return jnp.concatenate(lines + [jnp.zeros((pad, lines[0].shape[1]), f32)], axis=0)


def ffn_forward(flat, ctx, wout, vecs, wi, ib, wo, cot_pieces, rows_dev):
    n, width = flat.shape
    inner = wi.shape[1]
    count = len(cot_pieces)

    def kernel(flat_ref, ctx_ref, wout_ref, vec_ref, wi_ref, ib_ref, wo_ref, *refs):
        cot_refs = refs[:count]
        hat1_ref, inv1_ref, n1t_ref, active_ref, slope_ref = refs[count : count + 5]
        out_refs = refs[count + 5 : 2 * count + 5]
        dres_ref, douter_ref, small_ref, low, acc = refs[2 * count + 5 :]
        j = pl.program_id(0)

        @pl.when(j == 0)
        def _():
            resid = flat_ref[...].astype(f32) + dot(ctx_ref[...], wout_ref[...], 1, 0) + vec_ref[0:1]
            hat, inv = normalize(resid)
            hat1_ref[...] = hat
            inv1_ref[...] = jnp.broadcast_to(inv, inv1_ref.shape)
            normed = hat * vec_ref[1:2] + vec_ref[2:3]
            low[...] = normed.astype(bf16)
            n1t_ref[...] = normed.astype(bf16).T
            acc[...] = normed + vec_ref[3:4]

        left = low[...]
        total = acc[...]
        for c in range(0, BLOCK, PART):
            part = slice(c, c + PART)
            inner = dot(left, wi_ref[:, part], 1, 0) + ib_ref[:, part]
            cdf, bell = upper_tail(inner)
            active = (inner * cdf).astype(bf16)
            active_ref[:, part] = active
            slope_ref[:, part] = (cdf + inner * bell * 0.3989422804014327).astype(bf16)
            total = total + dot(active, wo_ref[part], 1, 0)
        acc[...] = total

        @pl.when(j == pl.num_programs(0) - 1)
        def _():
            valid_rows = cot_refs[0][rows_dev : rows_dev + EXTRA].astype(f32)[0:1]
            for r in cot_refs[1:]:
                valid_rows = valid_rows + r[rows_dev : rows_dev + EXTRA].astype(f32)[0:1]
            scale = 1.0 / jnp.maximum(valid_rows, 1.0)
            lines = [valid_rows * 0.0] * 3
            for k in range(count):
                part = slice(k * rows_dev, (k + 1) * rows_dev)
                hat, inv = normalize(acc[part])
                out_refs[k][...] = (hat * vec_ref[4:5] + vec_ref[5:6]).astype(bf16)
                cot = cot_refs[k][0:rows_dev].astype(f32) * scale
                dres = normalize_back(hat, inv, cot * vec_ref[4:5])
                dres_ref[part] = dres
                low_d = dres.astype(bf16)
                douter_ref[part] = low_d
                for i, v in enumerate((cot * hat, cot, low_d.astype(f32))):
                    lines[i] = lines[i] + jnp.sum(v, axis=0, keepdims=True)
            for i, v in enumerate(lines + [valid_rows]):
                small_ref[i : i + 1] = v

    full = lambda a: pl.BlockSpec(a.shape, lambda j: (0,) * a.ndim)
    whole = lambda shape: pl.BlockSpec(shape, lambda j: (0,) * len(shape))
    cols = pl.BlockSpec((n, BLOCK), lambda j: (0, j))
    outs = [
        (whole, (n, width), f32),
        (whole, (n, 128), f32),
        (whole, (width, n), bf16),
        (None, (n, inner), bf16),
        (None, (n, inner), bf16),
    ]
    outs += [(whole, (rows_dev, width), bf16)] * count
    outs += [(whole, (n, width), f32), (whole, (n, width), bf16), (whole, (8, width), f32)]
    got = pl.pallas_call(
        kernel,
        grid=(inner // BLOCK,),
        in_specs=[
            full(flat),
            full(ctx),
            full(wout),
            full(vecs),
            pl.BlockSpec((width, BLOCK), lambda j: (0, j)),
            pl.BlockSpec((1, BLOCK), lambda j: (0, j)),
            pl.BlockSpec((BLOCK, width), lambda j: (j, 0)),
        ]
        + [full(c) for c in cot_pieces],
        out_specs=[spec(shape) if spec else cols for spec, shape, _ in outs],
        out_shape=[jax.ShapeDtypeStruct(shape, kind) for _, shape, kind in outs],
        scratch_shapes=[pltpu.VMEM((n, width), bf16), pltpu.VMEM((n, width), f32)],
        name="ffn_fwd",
    )(flat, ctx, wout, vecs, wi, ib, wo, *cot_pieces)
    return got[:5], got[5 : 5 + count], got[5 + count :]


def inputs_backward(me, grads, weights, d_resid1, small1, small2, d_inner_bias, rows_dev, nseq, mem_rows):
    _, width = d_resid1.shape
    ib_rows = d_inner_bias.shape[1] // width

    def kernel(me_ref, dq_ref, dk_ref, dv_ref, wq_ref, wk_ref, wv_ref, dres_ref, s1_ref, s2_ref, ib_ref, *outs):
        pieces, small_ref = outs[:nseq], outs[nseq]
        seq_me = me_ref[1]
        first = me_ref[2]
        small_ref[...] = jnp.zeros_like(small_ref)
        d = dres_ref[...]
        for g, w in ((dq_ref, wq_ref), (dk_ref, wk_ref), (dv_ref, wv_ref)):
            d = d + dot(g[...], w[...], 1, 1)
        row = lax.broadcasted_iota(jnp.int32, (rows_dev, 1), 0)
        memory = jnp.zeros((2 * EXTRA, width), f32)
        for k in range(nseq):
            part = d[k * rows_dev : (k + 1) * rows_dev]
            is_mem = jnp.logical_and(row < mem_rows, jnp.logical_and(seq_me == k, first != 0))
            pieces[k][...] = jnp.where(is_mem, 0.0, part).astype(bf16)
            memory = memory + jnp.where(is_mem[: 2 * EXTRA], part[: 2 * EXTRA], 0.0)
        small_ref[0, 0:1] = jnp.sum(dq_ref[...].astype(f32), axis=0, keepdims=True)
        small_ref[0, 1:2] = jnp.sum(dv_ref[...].astype(f32), axis=0, keepdims=True)
        small_ref[0, 2:5] = s1_ref[0:3]
        small_ref[0, 5:8] = s2_ref[0:3]
        for r in range(ib_rows):
            small_ref[1, r : r + 1] = ib_ref[0:1, r * width : (r + 1) * width]
        small_ref[2] = memory[:EXTRA]
        small_ref[3] = memory[EXTRA:]

    vmem = pl.BlockSpec(memory_space=pltpu.VMEM)
    got = pl.pallas_call(
        kernel,
        in_specs=[pl.BlockSpec(memory_space=pltpu.SMEM)] + [vmem] * 10,
        out_specs=[vmem] * (nseq + 1),
        out_shape=[jax.ShapeDtypeStruct((rows_dev, width), bf16)] * nseq
        + [jax.ShapeDtypeStruct((nseq, EXTRA, width), f32)],
        name="inputs_bwd",
    )(me, *grads, *weights, d_resid1, small1, small2, d_inner_bias)
    return got[:nseq], got[nseq]


class Plan:
    def __init__(self, mesh):
        self.ndp, self.nseq = mesh.shape["dp"], mesh.shape["seq"]
        bits = [("seq", b) for b in range(self.nseq.bit_length() - 1)]
        dp_bits = [("dp", b) for b in range(self.ndp.bit_length() - 1)]
        assert 2 ** len(bits) == self.nseq and 2 ** len(dp_bits) == self.ndp
        rest = bits[2:] + dp_bits[1:]
        self.first = bits[0]
        self.orders = [[bits[1], dp_bits[0]] + rest, [dp_bits[0]] + rest + [bits[1]]]
        self.steps = len(self.orders[0])
        self.places = 1 << self.steps

    def flip(self, device, which):
        axis, b = which
        return device ^ ((1 << b) * (self.nseq if axis == "dp" else 1))

    def perm(self, step):
        devices = range(self.ndp * self.nseq)
        if step < 0:
            return [(d, self.flip(d, self.first)) for d in devices]
        return [(d, self.flip(d, self.orders[d & 1][step])) for d in devices]

    def place(self, dp_diff, seq_diff, half):
        value = {"dp": dp_diff, "seq": seq_diff}
        places = []
        for order in self.orders:
            p = 0
            for axis, b in order:
                p = p * 2 + ((value[axis] >> b) & 1)
            places.append(p)
        return jnp.where(half == 0, places[0], places[1])


def scatter_pieces(plan, me_ref, result, pieces, keep_ref, send_ref, rows, offset=0):
    dp_me = me_ref[0]
    seq_me = me_ref[1]
    for i, (dp, seq) in enumerate(pieces):
        tile = result[i * rows : (i + 1) * rows].astype(bf16)
        half = seq & 1
        at = plan.place(dp ^ dp_me, seq ^ seq_me, half)
        stay = half == (seq_me & 1)

        @pl.when(stay)
        def _(tile=tile, at=at):
            keep_ref[at, offset : offset + rows] = tile

        @pl.when(jnp.logical_not(stay))
        def _(tile=tile, at=at):
            send_ref[at, offset : offset + rows] = tile


def count_bits(count_row):
    lane = lax.broadcasted_iota(jnp.int32, count_row.shape, 1)
    return ((count_row.astype(jnp.int32) >> jnp.minimum(lane, DIGITS)) & 1).astype(f32)


def ffn_outer_grad(plan, me, active, d_outer, small2):
    n, inner = active.shape
    width = d_outer.shape[1]
    rows = inner // (plan.ndp * plan.nseq)
    per = BLOCK // rows

    def kernel(me_ref, active_ref, d_ref, small_ref, keep_ref, send_ref):
        j = pl.program_id(0)

        @pl.when(j == 0)
        def _():
            below = jnp.broadcast_to(count_bits(small_ref[3:4]), (EXTRA, width)).astype(bf16)
            for p in range(plan.places):
                keep_ref[p, rows:] = below
                send_ref[p, rows:] = below

        result = dot(active_ref[...], d_ref[...], 0, 0)
        pieces = [((j * per + i) // plan.nseq, (j * per + i) % plan.nseq) for i in range(per)]
        scatter_pieces(plan, me_ref, result, pieces, keep_ref, send_ref, rows)

    shape = jax.ShapeDtypeStruct((plan.places, rows + EXTRA, width), bf16)
    spec = pl.BlockSpec(shape.shape, lambda j, m: (0, 0, 0))
    return pl.pallas_call(
        kernel,
        grid_spec=pltpu.PrefetchScalarGridSpec(
            num_scalar_prefetch=1,
            grid=(inner // BLOCK,),
            in_specs=[
                pl.BlockSpec((n, BLOCK), lambda j, m: (0, j)),
                pl.BlockSpec((n, width), lambda j, m: (0, 0)),
                pl.BlockSpec(small2.shape, lambda j, m: (0, 0)),
            ],
            out_specs=[spec, spec],
        ),
        out_shape=[shape, shape],
        name="outer_grad",
    )(me, active, d_outer, small2)


def ffn_backward(plan, me, slope, d_outer, wo, wi, n1t, d_resid2, hat1, inv1, gain1, wout):
    n, inner = slope.shape
    width = d_outer.shape[1]
    rows = width // plan.ndp
    cols = inner // plan.nseq

    def kernel(
        me_ref, slope_ref, douter_ref, wo_ref, wi_ref, n1t_ref, dres2_ref, hat1_ref, inv1_ref, gain_ref, wout_ref,
        keep_ref, send_ref, dres1_ref, dattn_ref, dctx_ref, ib_ref, small_ref, acc,
    ):
        j = pl.program_id(0)
        d_active = dot(douter_ref[...], wo_ref[...], 1, 1)
        d_inner = (d_active * slope_ref[...].astype(f32)).astype(bf16)
        ib_ref[...] = jnp.broadcast_to(jnp.sum(d_inner.astype(f32), axis=0, keepdims=True), ib_ref.shape)
        result = dot(n1t_ref[...], d_inner, 1, 0)
        scatter_pieces(plan, me_ref, result, [(i, j) for i in range(plan.ndp)], keep_ref, send_ref, rows)
        back = dot(d_inner, wi_ref[...], 1, 1)

        @pl.when(j == 0)
        def _():
            acc[...] = dres2_ref[...] + back

        @pl.when(j > 0)
        def _():
            acc[...] += back

        @pl.when(j == pl.num_programs(0) - 1)
        def _():
            d_normed = acc[...]
            hat = hat1_ref[...]
            dres = normalize_back(hat, inv1_ref[:, 0:1], d_normed * gain_ref[...])
            dres1_ref[...] = dres
            low = dres.astype(bf16)
            dattn_ref[...] = low
            dctx_ref[...] = dot(low, wout_ref[...], 1, 1).astype(bf16)
            small_ref[...] = rows_of(d_normed * hat, d_normed, low.astype(f32))

    full = lambda a: pl.BlockSpec(a.shape, lambda j, m: (0,) * a.ndim)
    whole = lambda shape: pl.BlockSpec(shape, lambda j, m: (0,) * len(shape))
    chunk = jax.ShapeDtypeStruct((plan.places, rows, cols), bf16)
    return pl.pallas_call(
        kernel,
        grid_spec=pltpu.PrefetchScalarGridSpec(
            num_scalar_prefetch=1,
            grid=(plan.nseq,),
            in_specs=[
                pl.BlockSpec((n, cols), lambda j, m: (0, j)),
                full(d_outer),
                pl.BlockSpec((cols, width), lambda j, m: (j, 0)),
                pl.BlockSpec((width, cols), lambda j, m: (0, j)),
                full(n1t),
                full(d_resid2),
                full(hat1),
                full(inv1),
                full(gain1),
                full(wout),
            ],
            out_specs=[
                whole(chunk.shape),
                whole(chunk.shape),
                whole((n, width)),
                whole((n, width)),
                whole((n, width)),
                pl.BlockSpec((8, cols), lambda j, m: (0, j)),
                whole((8, width)),
            ],
            scratch_shapes=[pltpu.VMEM((n, width), f32)],
        ),
        out_shape=[
            chunk,
            chunk,
            jax.ShapeDtypeStruct((n, width), f32),
            jax.ShapeDtypeStruct((n, width), bf16),
            jax.ShapeDtypeStruct((n, width), bf16),
            jax.ShapeDtypeStruct((8, inner), f32),
            jax.ShapeDtypeStruct((8, width), f32),
        ],
        name="ffn_bwd",
    )(me, slope, d_outer, wo, wi, n1t, d_resid2, hat1, inv1, gain1, wout)


def finish_rows(me, factor, pieces, kind):
    count = len(pieces)

    def kernel(me_ref, factor_ref, *refs):
        out_ref = refs[count]
        for k in range(count):
            piece = refs[k][...]
            out_ref[me_ref[1] ^ k] = piece if piece.dtype == kind else piece.astype(f32) * factor_ref[0]

    smem = pl.BlockSpec(memory_space=pltpu.SMEM)
    vmem = pl.BlockSpec(memory_space=pltpu.VMEM)
    return pl.pallas_call(
        kernel,
        in_specs=[smem, smem] + [vmem] * count,
        out_specs=vmem,
        out_shape=jax.ShapeDtypeStruct((count,) + pieces[0].shape, kind),
    )(me, factor, *pieces)


def finish_weights(me, factor, near, far, split):
    width = near.shape[2]
    count = 4
    shapes = []
    for start, rows, axis in split:
        if axis is None:
            shapes += [(rows, width)] * count
        else:
            shapes.append((count * rows, width) if axis == 0 else (rows, count * width))

    def kernel(me_ref, factor_ref, near_ref, far_ref, *outs):
        for s in range(count):
            diff = me_ref[1] ^ s
            at = diff >> 1
            o = 0
            for start, rows, axis in split:
                part = slice(start, start + rows)
                value = jnp.where((diff & 1) == 0, near_ref[at, part], far_ref[at, part])
                value = value.astype(f32) * factor_ref[0]
                if axis is None:
                    outs[o + s][...] = value
                    o += count
                elif axis == 0:
                    outs[o][s * rows : (s + 1) * rows] = value
                    o += 1
                else:
                    outs[o][:, s * width : (s + 1) * width] = value
                    o += 1

    smem = pl.BlockSpec(memory_space=pltpu.SMEM)
    vmem = pl.BlockSpec(memory_space=pltpu.VMEM)
    return pl.pallas_call(
        kernel,
        in_specs=[smem, smem, vmem, vmem],
        out_specs=[vmem] * len(shapes),
        out_shape=[jax.ShapeDtypeStruct(shape, f32) for shape in shapes],
    )(me, factor, near, far)


def attn_weight_grads(plan, me, flat, ctx, grads, small):
    n, width = flat.shape
    rows = width // plan.ndp

    def kernel(me_ref, flat_ref, ctx_ref, d0_ref, d1_ref, d2_ref, d3_ref, small_ref, keep_ref, send_ref, flat_t, ctx_t):
        flat_t[...] = flat_ref[...].T
        ctx_t[...] = ctx_ref[...].T
        for s, d_ref in enumerate((d0_ref, d1_ref, d2_ref, d3_ref)):
            left = ctx_t if s == 3 else flat_t
            result = dot(left[...], d_ref[...], 1, 0)
            pieces = [(i, s) for i in range(plan.ndp)]
            scatter_pieces(plan, me_ref, result, pieces, keep_ref, send_ref, rows)
            below = jnp.concatenate([small_ref[s].astype(bf16)] * plan.ndp, axis=0)
            scatter_pieces(plan, me_ref, below, pieces, keep_ref, send_ref, EXTRA, rows)

    shape = jax.ShapeDtypeStruct((plan.places, rows + EXTRA, width), bf16)
    return pl.pallas_call(
        kernel,
        in_specs=[pl.BlockSpec(memory_space=pltpu.SMEM)] + [pl.BlockSpec(memory_space=pltpu.VMEM)] * 7,
        out_specs=[pl.BlockSpec(memory_space=pltpu.VMEM)] * 2,
        out_shape=[shape, shape],
        scratch_shapes=[pltpu.VMEM((width, n), bf16), pltpu.VMEM((width, n), bf16)],
        name="attn_grad",
    )(me, flat, ctx, *grads, small)


def place_pieces(plan, me, blocks):
    dp = jnp.repeat(jnp.arange(plan.ndp), plan.nseq)
    seq = jnp.tile(jnp.arange(plan.nseq), plan.ndp)
    half = seq & 1
    place = plan.place(dp ^ me[0], seq ^ me[1], half)
    away = half ^ (me[1] & 1)
    flat = blocks.reshape((plan.ndp * plan.nseq,) + blocks.shape[2:])
    order = jnp.zeros((2 * plan.places,), jnp.int32).at[away * plan.places + place].set(jnp.arange(dp.shape[0]))
    both = jnp.take(flat, order, axis=0)
    return both[: plan.places], both[plan.places :]


def make_per_device(mesh):
    plan = Plan(mesh)
    ndp, nseq = plan.ndp, plan.nseq
    devices = ("dp", "seq")

    def total_of(terms):
        total = terms[0].astype(f32)
        for t in terms[1:]:
            total = total + t.astype(f32)
        return total

    def start_chunk(keep, send):
        return [keep, lax.ppermute(send, devices, plan.perm(-1))]

    def step_chunk(terms, step):
        half = terms[0].shape[0] // 2
        send = total_of([t[half:] for t in terms]).astype(bf16)
        got = lax.ppermute(send, devices, plan.perm(step))
        return [t[:half] for t in terms] + [got]

    def swap_seq(x, k):
        return lax.ppermute(x, "seq", [(i, i ^ k) for i in range(nseq)])

    def gather_seq(x):
        assert nseq == 4
        near = jnp.stack([x, swap_seq(x, 2)])
        return near, swap_seq(near, 1)

    def per_device(
        tokens,
        memory_init,
        query_weight,
        query_bias,
        key_weight,
        value_weight,
        value_bias,
        output_weight,
        output_bias,
        attn_gain,
        attn_shift,
        inner_weight,
        inner_bias,
        outer_weight,
        outer_bias,
        ffn_gain,
        ffn_shift,
        out_grad,
        lm_mask,
        doc_segments,
    ):
        seg_dev, rows_dev, width = tokens.shape
        assert rows_dev * nseq < (1 << DIGITS) and ndp * nseq <= 256
        assert seg_dev == nseq
        rows = rows_dev * nseq
        mem_rows = memory_init.shape[1]
        ff = inner_weight.shape[1]
        seq_index = lax.axis_index("seq")
        dp_index = lax.axis_index("dp")
        segs_total = ndp * seg_dev

        def to_segments(x):
            pieces = [lax.dynamic_index_in_dim(x, seq_index ^ k, axis=0, keepdims=False) for k in range(nseq)]
            return [swap_seq(p, k) if k else p for k, p in enumerate(pieces)], pieces

        def to_rows(pieces, finish):
            out = None
            for k in range(nseq):
                piece = finish(pieces[k])
                if out is None:
                    out = jnp.zeros((nseq,) + piece.shape, piece.dtype)
                out = lax.dynamic_update_index_in_dim(out, piece, seq_index ^ k, axis=0)
            return out

        source = seq_index ^ jnp.arange(nseq, dtype=jnp.int32)
        position = source[:, None] * rows_dev + jnp.arange(rows_dev, dtype=jnp.int32)[None, :]
        is_mem = (position < mem_rows).reshape(rows)
        pieces, sliced = to_segments(tokens)
        raw = jnp.concatenate(pieces, axis=0)
        out_grad, lm_mask, *_ = lax.optimization_barrier((out_grad, lm_mask, *sliced))

        here = seq_index * rows_dev + jnp.arange(rows_dev, dtype=jnp.int32)
        valid = jnp.where((here < mem_rows)[None, :], 0, lm_mask)
        counts_here = jnp.sum(valid, axis=1)
        masked = jnp.where(valid[..., None] != 0, out_grad, jnp.zeros_like(out_grad))
        assert rows_dev <= 256
        count_rows = jnp.broadcast_to(counts_here.astype(bf16)[:, None, None], (seg_dev, EXTRA, width))
        cot_pieces, _ = to_segments(jnp.concatenate([masked, count_rows], axis=1))

        seg_global = dp_index * seg_dev + seq_index
        starts = jnp.cumsum(doc_segments) - doc_segments
        is_first = jnp.any(starts == seg_global)
        me = jnp.stack([dp_index, seq_index, is_first.astype(jnp.int32)]).astype(jnp.int32)
        select = (is_first & is_mem)[:, None]
        table = jnp.concatenate([memory_init.T, jnp.zeros((rows_dev - mem_rows, width), bf16)], axis=0)
        table = jnp.concatenate([table] * nseq, axis=0)
        flat = jnp.where(select, table, raw)

        queries = (dot(flat, query_weight, 1, 0) + query_bias.astype(f32)).astype(bf16)
        keys = dot(flat, key_weight, 1, 0).astype(bf16)
        values = (dot(flat, value_weight, 1, 0) + value_bias.astype(f32)).astype(bf16)
        context, probs = attention_forward(queries, keys, values, 1, rows)
        zero = jnp.zeros_like(output_bias)
        vecs = jnp.stack(
            [output_bias, attn_gain, attn_shift, outer_bias, ffn_gain, ffn_shift, zero, zero]
        ).astype(f32)
        (hat1, inv1, n1t, active, slope), out_pieces, (d_resid2, d_outer, small2) = ffn_forward(
            flat,
            context,
            output_weight,
            vecs,
            inner_weight,
            inner_bias.astype(f32)[None],
            outer_weight,
            cot_pieces,
            rows_dev,
        )
        out_pieces = [swap_seq(p, k) if k else p for k, p in enumerate(out_pieces)]
        layer_out = finish_rows(me, jnp.ones((1,), f32), out_pieces, bf16)

        aligned = (width // ndp) % 16 == 0 and (ff // (ndp * nseq)) % 16 == 0 and ff // nseq == BLOCK
        if aligned:
            keep, send = ffn_outer_grad(plan, me, active, d_outer, small2)
        else:
            grad = dot(active, d_outer, 0, 0).astype(bf16)
            below = jnp.broadcast_to(count_bits(small2[3:4]), (ndp, nseq, EXTRA, width)).astype(bf16)
            blocks = jnp.concatenate([grad.reshape(ndp, nseq, -1, width), below], axis=2)
            keep, send = place_pieces(plan, me, blocks)
        d_outer, keep, send = lax.optimization_barrier((d_outer, keep, send))
        outer = start_chunk(keep, send)
        if aligned:
            keep, send, d_resid1, d_attn, d_context, d_inner_bias, small1 = ffn_backward(
                plan, me, slope, d_outer, outer_weight, inner_weight, n1t, d_resid2, hat1, inv1, vecs[1:2], output_weight
            )
        else:
            d_inner = (dot(d_outer, outer_weight, 1, 1) * slope.astype(f32)).astype(bf16)
            d_inner_bias = jnp.broadcast_to(jnp.sum(d_inner.astype(f32), axis=0), (8, ff))
            grad = dot(n1t, d_inner, 1, 0).astype(bf16)
            grad = grad.reshape(ndp, width // ndp, nseq, ff // nseq).transpose(0, 2, 1, 3)
            keep, send = place_pieces(plan, me, grad)
            d_normed = dot(d_inner, inner_weight, 1, 1) + d_resid2
            d_resid1 = normalize_back(hat1, inv1[:, 0:1], d_normed * vecs[1:2])
            d_attn = d_resid1.astype(bf16)
            d_context = dot(d_attn, output_weight, 1, 1).astype(bf16)
            small1 = rows_of(d_normed * hat1, d_normed, d_attn.astype(f32))
        inner = start_chunk(keep, send)
        outer = step_chunk(outer, 0)
        d_queries, d_keys, d_values = attention_backward(
            queries, keys, values, context, d_context, probs, 1, rows
        )
        outer = step_chunk(outer, 1)
        inner = step_chunk(inner, 0)
        cut_pieces, small = inputs_backward(
            me,
            (d_queries, d_keys, d_values),
            (query_weight, key_weight, value_weight),
            d_resid1,
            small1,
            small2,
            d_inner_bias,
            rows_dev,
            nseq,
            mem_rows,
        )
        cut_pieces = [swap_seq(p, k) if k else p for k, p in enumerate(cut_pieces)]
        ib_rows = ff // width
        attn_grads = (d_queries, d_keys, d_values, d_attn)
        if aligned:
            keep, send = attn_weight_grads(plan, me, flat, context, attn_grads, small)
        else:
            blocks = []
            for s, d in enumerate(attn_grads):
                left = context if s == 3 else flat
                blocks.append(dot(left, d, 0, 0).astype(bf16).reshape(ndp, -1, width))
            blocks = jnp.stack(blocks, axis=1)
            below = jnp.broadcast_to(small.astype(bf16)[None], (ndp,) + small.shape)
            keep, send = place_pieces(plan, me, jnp.concatenate([blocks, below], axis=2))
        attn = start_chunk(keep, send)
        for step in range(2, plan.steps):
            outer = step_chunk(outer, step)
        for step in range(1, plan.steps):
            inner = step_chunk(inner, step)
        for step in range(plan.steps):
            attn = step_chunk(attn, step)
        outer_rows = ff // (ndp * nseq)
        outer = total_of(outer)[0]
        total = jnp.sum(outer[outer_rows, :DIGITS] * (2.0 ** jnp.arange(DIGITS)).astype(f32))
        factor = total / segs_total
        ffn_near, ffn_far = gather_seq(jnp.concatenate([outer[:outer_rows], total_of(inner)[0]], axis=0).astype(bf16))
        attn_near, attn_far = gather_seq(total_of(attn)[0].astype(bf16))

        part = width // ndp
        scale = factor.reshape(1)
        if aligned:
            tokens_grad = finish_rows(me, scale, cut_pieces, f32)
            g_outer, g_inner = finish_weights(me, scale, ffn_near, ffn_far, [(0, outer_rows, 0), (outer_rows, part, 1)])
            got = finish_weights(me, scale, attn_near, attn_far, [(0, part, None), (part, EXTRA, None)])
            g_query, g_key, g_value, g_output = got[:4]
            small_parts = got[4:]
        else:
            finish = lambda x: x.astype(f32) * factor
            tokens_grad = to_rows(cut_pieces, finish)

            def in_order(near, far):
                stack = jnp.stack([near[0], far[0], near[1], far[1]])
                return [finish(lax.dynamic_index_in_dim(stack, seq_index ^ k, 0, keepdims=False)) for k in range(nseq)]

            ffn_parts = in_order(ffn_near, ffn_far)
            g_outer = jnp.concatenate([p[:outer_rows] for p in ffn_parts], axis=0)
            g_inner = jnp.concatenate([p[outer_rows:] for p in ffn_parts], axis=1)
            attn_parts = in_order(attn_near, attn_far)
            g_query, g_key, g_value, g_output = [p[:part] for p in attn_parts]
            small_parts = [p[part:] for p in attn_parts]
        mine = lambda x: lax.dynamic_slice_in_dim(x, dp_index * part, part, axis=1)
        vec_rows = mine(small_parts[0][:8])
        g_memory = mine(jnp.concatenate([small_parts[2], small_parts[3]])[:mem_rows]).T
        inner_part = ff // ndp
        g_inner_bias = lax.dynamic_slice_in_dim(
            small_parts[1][:ib_rows].reshape(-1), dp_index * inner_part, inner_part, axis=0
        )
        g_query_bias, g_value_bias, g_gain1, g_shift1, g_output_bias, g_gain2, g_shift2, g_outer_bias = vec_rows
        return (
            layer_out,
            tokens_grad,
            g_query,
            g_query_bias,
            g_key,
            g_value,
            g_value_bias,
            g_output,
            g_output_bias,
            g_gain1,
            g_shift1,
            g_inner,
            g_inner_bias,
            g_outer,
            g_outer_bias,
            g_gain2,
            g_shift2,
            g_memory,
        )

    return per_device


def solution(mesh):
    rows = P("dp", "seq", None)
    in_specs = (rows,) + (P(),) * 16 + (rows, P("dp", "seq"), P())
    out_specs = (
        rows,
        rows,
        P("dp", None),
        P("dp"),
        P("dp", None),
        P("dp", None),
        P("dp"),
        P("dp", None),
        P("dp"),
        P("dp"),
        P("dp"),
        P("dp", None),
        P("dp"),
        P("dp", None),
        P("dp"),
        P("dp"),
        P("dp"),
        P("dp", None),
    )
    return jax.shard_map(
        make_per_device(mesh), mesh=mesh, in_specs=in_specs, out_specs=out_specs, check_vma=False
    )
```

```python
import jax
import jax.numpy as jnp
from jax import lax
from jax.experimental import pallas as pl
from jax.experimental.pallas import tpu as pltpu
from jax.sharding import PartitionSpec as P


HEAD_DIM = 64
EPS = 1e-06
LOG2E = 1.4426950408889634
BLOCK = 768
PART = 768
DIGITS = 16
EXTRA = 8
f32 = jnp.float32
bf16 = jnp.bfloat16


def dot(a, b, ca, cb):
    return lax.dot_general(a, b, (((ca,), (cb,)), ((), ())), preferred_element_type=f32)


def attn_fwd_kernel(q_ref, k_ref, v_ref, ctx_ref, p_ref):
    q = q_ref[...]
    k = k_ref[...]
    v = v_ref[...]
    lanes = lax.broadcasted_iota(jnp.int32, (1, 2 * HEAD_DIM), 1)
    ctx = None
    for h in range(2):
        mask = (lanes // HEAD_DIM) == h
        kh = jnp.where(mask, k, jnp.zeros_like(k))
        vh = jnp.where(mask, v, jnp.zeros_like(v))
        s = dot(q, kh, 1, 1) * (HEAD_DIM ** (-0.5) * LOG2E)
        e = jnp.exp2(s - jnp.max(s, axis=-1, keepdims=True))
        p = (e * (1.0 / jnp.sum(e, axis=-1, keepdims=True))).astype(bf16)
        p_ref[h] = p
        c = dot(p, vh, 1, 0)
        ctx = c if ctx is None else ctx + c
    ctx_ref[...] = ctx.astype(bf16)


def attn_bwd_kernel(q_ref, k_ref, v_ref, ctx_ref, dctx_ref, p_ref, dq_ref, dk_ref, dv_ref):
    q = q_ref[...]
    k = k_ref[...]
    v = v_ref[...]
    dctx = dctx_ref[...]
    prod = dctx.astype(f32) * ctx_ref[...].astype(f32)
    lanes = lax.broadcasted_iota(jnp.int32, (1, 2 * HEAD_DIM), 1)
    scale = HEAD_DIM ** (-0.5)
    dq = None
    dk = None
    dv = None
    for h in range(2):
        mask = (lanes // HEAD_DIM) == h
        zero = jnp.zeros_like(k)
        vh = jnp.where(mask, v, zero)
        kh = jnp.where(mask, k, zero)
        qh = jnp.where(mask, q, zero)
        dh = jnp.where(mask, dctx, zero)
        delta = jnp.sum(jnp.where(mask, prod, 0.0), axis=-1, keepdims=True)
        p = p_ref[h]
        dp = dot(dctx, vh, 1, 1)
        ds = (p.astype(f32) * (dp - delta)).astype(bf16)
        dqh = dot(ds, kh, 1, 0)
        dkh = dot(ds, qh, 0, 0)
        dvh = dot(p, dh, 0, 0)
        dq = dqh if dq is None else dq + dqh
        dk = dkh if dk is None else dk + dkh
        dv = dvh if dv is None else dv + dvh
    dq_ref[...] = (dq * scale).astype(bf16)
    dk_ref[...] = (dk * scale).astype(bf16)
    dv_ref[...] = dv.astype(bf16)


def attention_forward(q, k, v, segs, rows):
    block = 2 * HEAD_DIM
    pairs = q.shape[1] // block
    spec = pl.BlockSpec((rows, block), lambda s, h: (s, h))
    pspec = pl.BlockSpec((2, rows, rows), lambda s, h: (s * pairs + h, 0, 0))
    return pl.pallas_call(
        attn_fwd_kernel,
        grid=(segs, pairs),
        in_specs=[spec, spec, spec],
        out_specs=[spec, pspec],
        out_shape=[
            jax.ShapeDtypeStruct(q.shape, bf16),
            jax.ShapeDtypeStruct((segs * 2 * pairs, rows, rows), bf16),
        ],
        name="attn_fwd",
    )(q, k, v)


def attention_backward(q, k, v, ctx, dctx, p, segs, rows):
    block = 2 * HEAD_DIM
    pairs = q.shape[1] // block
    spec = pl.BlockSpec((rows, block), lambda s, h: (s, h))
    pspec = pl.BlockSpec((2, rows, rows), lambda s, h: (s * pairs + h, 0, 0))
    shape = jax.ShapeDtypeStruct(q.shape, bf16)
    return pl.pallas_call(
        attn_bwd_kernel,
        grid=(segs, pairs),
        in_specs=[spec] * 5 + [pspec],
        out_specs=[spec] * 3,
        out_shape=[shape] * 3,
        name="attn_bwd",
    )(q, k, v, ctx, dctx, p)


def upper_tail(x):
    z = jnp.abs(x) * (0.5 ** 0.5)
    t = 1.0 / (1.0 + 0.5 * z)
    poly = 0.17087277
    for c in (
        -0.82215223,
        1.48851587,
        -1.13520398,
        0.27886807,
        -0.18628806,
        0.09678418,
        0.37409196,
        1.00002368,
        -1.26551223,
    ):
        poly = poly * t + c
    bell = jnp.exp(-0.5 * x * x)
    half = 0.5 * t * bell * jnp.exp(poly)
    return jnp.where(x >= 0, 1.0 - half, half), bell


def normalize(values):
    center = values - jnp.mean(values, axis=-1, keepdims=True)
    inv = lax.rsqrt(jnp.mean(center * center, axis=-1, keepdims=True) + EPS)
    return center * inv, inv


def normalize_back(hat, inv, g):
    a = jnp.mean(g, axis=-1, keepdims=True)
    b = jnp.mean(g * hat, axis=-1, keepdims=True)
    return inv * (g - a - hat * b)


def rows_of(*vectors):
    lines = [jnp.sum(v, axis=0, keepdims=True) for v in vectors]
    pad = 8 - len(lines)
    return jnp.concatenate(lines + [jnp.zeros((pad, lines[0].shape[1]), f32)], axis=0)


def ffn_forward(flat, ctx, wout, vecs, wi, ib, wo, cot_pieces, rows_dev):
    n, width = flat.shape
    inner = wi.shape[1]
    count = len(cot_pieces)

    def kernel(flat_ref, ctx_ref, wout_ref, vec_ref, wi_ref, ib_ref, wo_ref, *refs):
        cot_refs = refs[:count]
        hat1_ref, inv1_ref, n1t_ref, active_ref, slope_ref = refs[count : count + 5]
        out_refs = refs[count + 5 : 2 * count + 5]
        dres_ref, douter_ref, small_ref, low, acc = refs[2 * count + 5 :]
        j = pl.program_id(0)

        @pl.when(j == 0)
        def _():
            resid = flat_ref[...].astype(f32) + dot(ctx_ref[...], wout_ref[...], 1, 0) + vec_ref[0:1]
            hat, inv = normalize(resid)
            hat1_ref[...] = hat
            inv1_ref[...] = jnp.broadcast_to(inv, inv1_ref.shape)
            normed = hat * vec_ref[1:2] + vec_ref[2:3]
            low[...] = normed.astype(bf16)
            n1t_ref[...] = normed.astype(bf16).T
            acc[...] = normed + vec_ref[3:4]

        left = low[...]
        total = acc[...]
        for c in range(0, BLOCK, PART):
            part = slice(c, c + PART)
            inner = dot(left, wi_ref[:, part], 1, 0) + ib_ref[:, part]
            cdf, bell = upper_tail(inner)
            active = (inner * cdf).astype(bf16)
            active_ref[:, part] = active
            slope_ref[:, part] = (cdf + inner * bell * 0.3989422804014327).astype(bf16)
            total = total + dot(active, wo_ref[part], 1, 0)
        acc[...] = total

        @pl.when(j == pl.num_programs(0) - 1)
        def _():
            valid_rows = cot_refs[0][rows_dev : rows_dev + EXTRA].astype(f32)[0:1]
            for r in cot_refs[1:]:
                valid_rows = valid_rows + r[rows_dev : rows_dev + EXTRA].astype(f32)[0:1]
            scale = 1.0 / jnp.maximum(valid_rows, 1.0)
            lines = [valid_rows * 0.0] * 3
            for k in range(count):
                part = slice(k * rows_dev, (k + 1) * rows_dev)
                hat, inv = normalize(acc[part])
                out_refs[k][...] = (hat * vec_ref[4:5] + vec_ref[5:6]).astype(bf16)
                cot = cot_refs[k][0:rows_dev].astype(f32) * scale
                dres = normalize_back(hat, inv, cot * vec_ref[4:5])
                dres_ref[part] = dres
                low_d = dres.astype(bf16)
                douter_ref[part] = low_d
                for i, v in enumerate((cot * hat, cot, low_d.astype(f32))):
                    lines[i] = lines[i] + jnp.sum(v, axis=0, keepdims=True)
            for i, v in enumerate(lines + [valid_rows]):
                small_ref[i : i + 1] = v

    full = lambda a: pl.BlockSpec(a.shape, lambda j: (0,) * a.ndim)
    whole = lambda shape: pl.BlockSpec(shape, lambda j: (0,) * len(shape))
    cols = pl.BlockSpec((n, BLOCK), lambda j: (0, j))
    outs = [
        (whole, (n, width), f32),
        (whole, (n, 128), f32),
        (whole, (width, n), bf16),
        (None, (n, inner), bf16),
        (None, (n, inner), bf16),
    ]
    outs += [(whole, (rows_dev, width), bf16)] * count
    outs += [(whole, (n, width), f32), (whole, (n, width), bf16), (whole, (8, width), f32)]
    got = pl.pallas_call(
        kernel,
        grid=(inner // BLOCK,),
        in_specs=[
            full(flat),
            full(ctx),
            full(wout),
            full(vecs),
            pl.BlockSpec((width, BLOCK), lambda j: (0, j)),
            pl.BlockSpec((1, BLOCK), lambda j: (0, j)),
            pl.BlockSpec((BLOCK, width), lambda j: (j, 0)),
        ]
        + [full(c) for c in cot_pieces],
        out_specs=[spec(shape) if spec else cols for spec, shape, _ in outs],
        out_shape=[jax.ShapeDtypeStruct(shape, kind) for _, shape, kind in outs],
        scratch_shapes=[pltpu.VMEM((n, width), bf16), pltpu.VMEM((n, width), f32)],
        name="ffn_fwd",
    )(flat, ctx, wout, vecs, wi, ib, wo, *cot_pieces)
    return got[:5], got[5 : 5 + count], got[5 + count :]


def inputs_backward(me, grads, weights, d_resid1, small1, small2, d_inner_bias, rows_dev, nseq, mem_rows):
    _, width = d_resid1.shape
    ib_rows = d_inner_bias.shape[1] // width

    def kernel(me_ref, dq_ref, dk_ref, dv_ref, wq_ref, wk_ref, wv_ref, dres_ref, s1_ref, s2_ref, ib_ref, *outs):
        pieces, small_ref = outs[:nseq], outs[nseq]
        seq_me = me_ref[1]
        first = me_ref[2]
        small_ref[...] = jnp.zeros_like(small_ref)
        d = dres_ref[...]
        for g, w in ((dq_ref, wq_ref), (dk_ref, wk_ref), (dv_ref, wv_ref)):
            d = d + dot(g[...], w[...], 1, 1)
        row = lax.broadcasted_iota(jnp.int32, (rows_dev, 1), 0)
        memory = jnp.zeros((2 * EXTRA, width), f32)
        for k in range(nseq):
            part = d[k * rows_dev : (k + 1) * rows_dev]
            is_mem = jnp.logical_and(row < mem_rows, jnp.logical_and(seq_me == k, first != 0))
            pieces[k][...] = jnp.where(is_mem, 0.0, part).astype(bf16)
            memory = memory + jnp.where(is_mem[: 2 * EXTRA], part[: 2 * EXTRA], 0.0)
        small_ref[0, 0:1] = jnp.sum(dq_ref[...].astype(f32), axis=0, keepdims=True)
        small_ref[0, 1:2] = jnp.sum(dv_ref[...].astype(f32), axis=0, keepdims=True)
        small_ref[0, 2:5] = s1_ref[0:3]
        small_ref[0, 5:8] = s2_ref[0:3]
        for r in range(ib_rows):
            small_ref[1, r : r + 1] = ib_ref[0:1, r * width : (r + 1) * width]
        small_ref[2] = memory[:EXTRA]
        small_ref[3] = memory[EXTRA:]

    vmem = pl.BlockSpec(memory_space=pltpu.VMEM)
    got = pl.pallas_call(
        kernel,
        in_specs=[pl.BlockSpec(memory_space=pltpu.SMEM)] + [vmem] * 10,
        out_specs=[vmem] * (nseq + 1),
        out_shape=[jax.ShapeDtypeStruct((rows_dev, width), bf16)] * nseq
        + [jax.ShapeDtypeStruct((nseq, EXTRA, width), f32)],
        name="inputs_bwd",
    )(me, *grads, *weights, d_resid1, small1, small2, d_inner_bias)
    return got[:nseq], got[nseq]


class Plan:
    def __init__(self, mesh):
        self.ndp, self.nseq = mesh.shape["dp"], mesh.shape["seq"]
        bits = [("seq", b) for b in range(self.nseq.bit_length() - 1)]
        dp_bits = [("dp", b) for b in range(self.ndp.bit_length() - 1)]
        assert 2 ** len(bits) == self.nseq and 2 ** len(dp_bits) == self.ndp
        rest = bits[2:] + dp_bits[1:]
        self.first = bits[0]
        self.orders = [[bits[1], dp_bits[0]] + rest, [dp_bits[0]] + rest + [bits[1]]]
        self.steps = len(self.orders[0])
        self.places = 1 << self.steps

    def flip(self, device, which):
        axis, b = which
        return device ^ ((1 << b) * (self.nseq if axis == "dp" else 1))

    def perm(self, step):
        devices = range(self.ndp * self.nseq)
        if step < 0:
            return [(d, self.flip(d, self.first)) for d in devices]
        return [(d, self.flip(d, self.orders[d & 1][step])) for d in devices]

    def place(self, dp_diff, seq_diff, half):
        value = {"dp": dp_diff, "seq": seq_diff}
        places = []
        for order in self.orders:
            p = 0
            for axis, b in order:
                p = p * 2 + ((value[axis] >> b) & 1)
            places.append(p)
        return jnp.where(half == 0, places[0], places[1])


def scatter_pieces(plan, me_ref, result, pieces, keep_ref, send_ref, rows, offset=0):
    dp_me = me_ref[0]
    seq_me = me_ref[1]
    for i, (dp, seq) in enumerate(pieces):
        tile = result[i * rows : (i + 1) * rows].astype(bf16)
        half = seq & 1
        at = plan.place(dp ^ dp_me, seq ^ seq_me, half)
        stay = half == (seq_me & 1)

        @pl.when(stay)
        def _(tile=tile, at=at):
            keep_ref[at, offset : offset + rows] = tile

        @pl.when(jnp.logical_not(stay))
        def _(tile=tile, at=at):
            send_ref[at, offset : offset + rows] = tile


def count_bits(count_row):
    lane = lax.broadcasted_iota(jnp.int32, count_row.shape, 1)
    return ((count_row.astype(jnp.int32) >> jnp.minimum(lane, DIGITS)) & 1).astype(f32)


def ffn_outer_grad(plan, me, active, d_outer, small2):
    n, inner = active.shape
    width = d_outer.shape[1]
    rows = inner // (plan.ndp * plan.nseq)
    per = BLOCK // rows

    def kernel(me_ref, active_ref, d_ref, small_ref, keep_ref, send_ref):
        j = pl.program_id(0)

        @pl.when(j == 0)
        def _():
            below = jnp.broadcast_to(count_bits(small_ref[3:4]), (EXTRA, width)).astype(bf16)
            for p in range(plan.places):
                keep_ref[p, rows:] = below
                send_ref[p, rows:] = below

        result = dot(active_ref[...], d_ref[...], 0, 0)
        pieces = [((j * per + i) // plan.nseq, (j * per + i) % plan.nseq) for i in range(per)]
        scatter_pieces(plan, me_ref, result, pieces, keep_ref, send_ref, rows)

    shape = jax.ShapeDtypeStruct((plan.places, rows + EXTRA, width), bf16)
    spec = pl.BlockSpec(shape.shape, lambda j, m: (0, 0, 0))
    return pl.pallas_call(
        kernel,
        grid_spec=pltpu.PrefetchScalarGridSpec(
            num_scalar_prefetch=1,
            grid=(inner // BLOCK,),
            in_specs=[
                pl.BlockSpec((n, BLOCK), lambda j, m: (0, j)),
                pl.BlockSpec((n, width), lambda j, m: (0, 0)),
                pl.BlockSpec(small2.shape, lambda j, m: (0, 0)),
            ],
            out_specs=[spec, spec],
        ),
        out_shape=[shape, shape],
        name="outer_grad",
    )(me, active, d_outer, small2)


def ffn_backward(plan, me, slope, d_outer, wo, wi, n1t, d_resid2, hat1, inv1, gain1, wout):
    n, inner = slope.shape
    width = d_outer.shape[1]
    rows = width // plan.ndp
    cols = inner // plan.nseq

    def kernel(
        me_ref, slope_ref, douter_ref, wo_ref, wi_ref, n1t_ref, dres2_ref, hat1_ref, inv1_ref, gain_ref, wout_ref,
        keep_ref, send_ref, dres1_ref, dattn_ref, dctx_ref, ib_ref, small_ref, acc,
    ):
        j = pl.program_id(0)
        d_active = dot(douter_ref[...], wo_ref[...], 1, 1)
        d_inner = (d_active * slope_ref[...].astype(f32)).astype(bf16)
        ib_ref[...] = jnp.broadcast_to(jnp.sum(d_inner.astype(f32), axis=0, keepdims=True), ib_ref.shape)
        result = dot(n1t_ref[...], d_inner, 1, 0)
        scatter_pieces(plan, me_ref, result, [(i, j) for i in range(plan.ndp)], keep_ref, send_ref, rows)
        back = dot(d_inner, wi_ref[...], 1, 1)

        @pl.when(j == 0)
        def _():
            acc[...] = dres2_ref[...] + back

        @pl.when(j > 0)
        def _():
            acc[...] += back

        @pl.when(j == pl.num_programs(0) - 1)
        def _():
            d_normed = acc[...]
            hat = hat1_ref[...]
            dres = normalize_back(hat, inv1_ref[:, 0:1], d_normed * gain_ref[...])
            dres1_ref[...] = dres
            low = dres.astype(bf16)
            dattn_ref[...] = low
            dctx_ref[...] = dot(low, wout_ref[...], 1, 1).astype(bf16)
            small_ref[...] = rows_of(d_normed * hat, d_normed, low.astype(f32))

    full = lambda a: pl.BlockSpec(a.shape, lambda j, m: (0,) * a.ndim)
    whole = lambda shape: pl.BlockSpec(shape, lambda j, m: (0,) * len(shape))
    chunk = jax.ShapeDtypeStruct((plan.places, rows, cols), bf16)
    return pl.pallas_call(
        kernel,
        grid_spec=pltpu.PrefetchScalarGridSpec(
            num_scalar_prefetch=1,
            grid=(plan.nseq,),
            in_specs=[
                pl.BlockSpec((n, cols), lambda j, m: (0, j)),
                full(d_outer),
                pl.BlockSpec((cols, width), lambda j, m: (j, 0)),
                pl.BlockSpec((width, cols), lambda j, m: (0, j)),
                full(n1t),
                full(d_resid2),
                full(hat1),
                full(inv1),
                full(gain1),
                full(wout),
            ],
            out_specs=[
                whole(chunk.shape),
                whole(chunk.shape),
                whole((n, width)),
                whole((n, width)),
                whole((n, width)),
                pl.BlockSpec((8, cols), lambda j, m: (0, j)),
                whole((8, width)),
            ],
            scratch_shapes=[pltpu.VMEM((n, width), f32)],
        ),
        out_shape=[
            chunk,
            chunk,
            jax.ShapeDtypeStruct((n, width), f32),
            jax.ShapeDtypeStruct((n, width), bf16),
            jax.ShapeDtypeStruct((n, width), bf16),
            jax.ShapeDtypeStruct((8, inner), f32),
            jax.ShapeDtypeStruct((8, width), f32),
        ],
        name="ffn_bwd",
    )(me, slope, d_outer, wo, wi, n1t, d_resid2, hat1, inv1, gain1, wout)


def finish_rows(me, factor, pieces, kind):
    count = len(pieces)

    def kernel(me_ref, factor_ref, *refs):
        out_ref = refs[count]
        for k in range(count):
            piece = refs[k][...]
            out_ref[me_ref[1] ^ k] = piece if piece.dtype == kind else piece.astype(f32) * factor_ref[0]

    smem = pl.BlockSpec(memory_space=pltpu.SMEM)
    vmem = pl.BlockSpec(memory_space=pltpu.VMEM)
    return pl.pallas_call(
        kernel,
        in_specs=[smem, smem] + [vmem] * count,
        out_specs=vmem,
        out_shape=jax.ShapeDtypeStruct((count,) + pieces[0].shape, kind),
    )(me, factor, *pieces)


def finish_weights(me, factor, near, far, split, ndp):
    width = near.shape[2]
    count = 4
    shapes = []
    for start, rows, axis in split:
        if axis is None:
            shapes += [(rows, width)] * count
        elif axis == "dp":
            shapes.append((count, rows, width // ndp))
        else:
            shapes.append((count * rows, width) if axis == 0 else (rows, count * width))

    def kernel(me_ref, factor_ref, near_ref, far_ref, *outs):
        if any(axis == "dp" for _, _, axis in split):
            shape = (width, width // ndp)
            column = lax.broadcasted_iota(jnp.int32, shape, 1) + me_ref[0] * (width // ndp)
            pick = (lax.broadcasted_iota(jnp.int32, shape, 0) == column).astype(f32).astype(bf16)
        for s in range(count):
            diff = me_ref[1] ^ s
            at = diff >> 1
            o = 0
            for start, rows, axis in split:
                part = slice(start, start + rows)
                value = jnp.where((diff & 1) == 0, near_ref[at, part], far_ref[at, part])
                if axis == "dp":
                    outs[o][s] = dot(value, pick, 1, 0) * factor_ref[0]
                    o += 1
                    continue
                value = value.astype(f32) * factor_ref[0]
                if axis is None:
                    outs[o + s][...] = value
                    o += count
                elif axis == 0:
                    outs[o][s * rows : (s + 1) * rows] = value
                    o += 1
                else:
                    outs[o][:, s * width : (s + 1) * width] = value
                    o += 1

    smem = pl.BlockSpec(memory_space=pltpu.SMEM)
    vmem = pl.BlockSpec(memory_space=pltpu.VMEM)
    return pl.pallas_call(
        kernel,
        in_specs=[smem, smem, vmem, vmem],
        out_specs=[vmem] * len(shapes),
        out_shape=[jax.ShapeDtypeStruct(shape, f32) for shape in shapes],
    )(me, factor, near, far)


def attn_weight_grads(plan, me, flat, ctx, grads, small):
    n, width = flat.shape
    rows = width // plan.ndp

    def kernel(me_ref, flat_ref, ctx_ref, d0_ref, d1_ref, d2_ref, d3_ref, small_ref, keep_ref, send_ref, flat_t, ctx_t):
        flat_t[...] = flat_ref[...].T
        ctx_t[...] = ctx_ref[...].T
        for s, d_ref in enumerate((d0_ref, d1_ref, d2_ref, d3_ref)):
            left = ctx_t if s == 3 else flat_t
            result = dot(left[...], d_ref[...], 1, 0)
            pieces = [(i, s) for i in range(plan.ndp)]
            scatter_pieces(plan, me_ref, result, pieces, keep_ref, send_ref, rows)
            below = jnp.concatenate([small_ref[s].astype(bf16)] * plan.ndp, axis=0)
            scatter_pieces(plan, me_ref, below, pieces, keep_ref, send_ref, EXTRA, rows)

    shape = jax.ShapeDtypeStruct((plan.places, rows + EXTRA, width), bf16)
    return pl.pallas_call(
        kernel,
        in_specs=[pl.BlockSpec(memory_space=pltpu.SMEM)] + [pl.BlockSpec(memory_space=pltpu.VMEM)] * 7,
        out_specs=[pl.BlockSpec(memory_space=pltpu.VMEM)] * 2,
        out_shape=[shape, shape],
        scratch_shapes=[pltpu.VMEM((width, n), bf16), pltpu.VMEM((width, n), bf16)],
        name="attn_grad",
    )(me, flat, ctx, *grads, small)


def place_pieces(plan, me, blocks):
    dp = jnp.repeat(jnp.arange(plan.ndp), plan.nseq)
    seq = jnp.tile(jnp.arange(plan.nseq), plan.ndp)
    half = seq & 1
    place = plan.place(dp ^ me[0], seq ^ me[1], half)
    away = half ^ (me[1] & 1)
    flat = blocks.reshape((plan.ndp * plan.nseq,) + blocks.shape[2:])
    order = jnp.zeros((2 * plan.places,), jnp.int32).at[away * plan.places + place].set(jnp.arange(dp.shape[0]))
    both = jnp.take(flat, order, axis=0)
    return both[: plan.places], both[plan.places :]


def make_per_device(mesh):
    plan = Plan(mesh)
    ndp, nseq = plan.ndp, plan.nseq
    devices = ("dp", "seq")

    def total_of(terms):
        total = terms[0].astype(f32)
        for t in terms[1:]:
            total = total + t.astype(f32)
        return total

    def start_chunk(keep, send):
        return [keep, lax.ppermute(send, devices, plan.perm(-1))]

    def step_chunk(terms, step):
        half = terms[0].shape[0] // 2
        send = total_of([t[half:] for t in terms]).astype(bf16)
        got = lax.ppermute(send, devices, plan.perm(step))
        return [t[:half] for t in terms] + [got]

    def swap_seq(x, k):
        return lax.ppermute(x, "seq", [(i, i ^ k) for i in range(nseq)])

    def gather_seq(x):
        assert nseq == 4
        near = jnp.stack([x, swap_seq(x, 2)])
        return near, swap_seq(near, 1)

    def per_device(
        tokens,
        memory_init,
        query_weight,
        query_bias,
        key_weight,
        value_weight,
        value_bias,
        output_weight,
        output_bias,
        attn_gain,
        attn_shift,
        inner_weight,
        inner_bias,
        outer_weight,
        outer_bias,
        ffn_gain,
        ffn_shift,
        out_grad,
        lm_mask,
        doc_segments,
    ):
        seg_dev, rows_dev, width = tokens.shape
        assert rows_dev * nseq < (1 << DIGITS) and ndp * nseq <= 256
        assert seg_dev == nseq
        rows = rows_dev * nseq
        mem_rows = memory_init.shape[1]
        ff = inner_weight.shape[1]
        seq_index = lax.axis_index("seq")
        dp_index = lax.axis_index("dp")
        segs_total = ndp * seg_dev

        def to_segments(x):
            pieces = [lax.dynamic_index_in_dim(x, seq_index ^ k, axis=0, keepdims=False) for k in range(nseq)]
            return [swap_seq(p, k) if k else p for k, p in enumerate(pieces)], pieces

        def to_rows(pieces, finish):
            out = None
            for k in range(nseq):
                piece = finish(pieces[k])
                if out is None:
                    out = jnp.zeros((nseq,) + piece.shape, piece.dtype)
                out = lax.dynamic_update_index_in_dim(out, piece, seq_index ^ k, axis=0)
            return out

        source = seq_index ^ jnp.arange(nseq, dtype=jnp.int32)
        position = source[:, None] * rows_dev + jnp.arange(rows_dev, dtype=jnp.int32)[None, :]
        is_mem = (position < mem_rows).reshape(rows)
        pieces, sliced = to_segments(tokens)
        raw = jnp.concatenate(pieces, axis=0)
        out_grad, lm_mask, *_ = lax.optimization_barrier((out_grad, lm_mask, *sliced))

        here = seq_index * rows_dev + jnp.arange(rows_dev, dtype=jnp.int32)
        valid = jnp.where((here < mem_rows)[None, :], 0, lm_mask)
        counts_here = jnp.sum(valid, axis=1)
        masked = jnp.where(valid[..., None] != 0, out_grad, jnp.zeros_like(out_grad))
        assert rows_dev <= 256
        count_rows = jnp.broadcast_to(counts_here.astype(bf16)[:, None, None], (seg_dev, EXTRA, width))
        cot_pieces, _ = to_segments(jnp.concatenate([masked, count_rows], axis=1))

        seg_global = dp_index * seg_dev + seq_index
        starts = jnp.cumsum(doc_segments) - doc_segments
        is_first = jnp.any(starts == seg_global)
        me = jnp.stack([dp_index, seq_index, is_first.astype(jnp.int32)]).astype(jnp.int32)
        select = (is_first & is_mem)[:, None]
        table = jnp.concatenate([memory_init.T, jnp.zeros((rows_dev - mem_rows, width), bf16)], axis=0)
        table = jnp.concatenate([table] * nseq, axis=0)
        flat = jnp.where(select, table, raw)

        queries = (dot(flat, query_weight, 1, 0) + query_bias.astype(f32)).astype(bf16)
        keys = dot(flat, key_weight, 1, 0).astype(bf16)
        values = (dot(flat, value_weight, 1, 0) + value_bias.astype(f32)).astype(bf16)
        context, probs = attention_forward(queries, keys, values, 1, rows)
        zero = jnp.zeros_like(output_bias)
        vecs = jnp.stack(
            [output_bias, attn_gain, attn_shift, outer_bias, ffn_gain, ffn_shift, zero, zero]
        ).astype(f32)
        (hat1, inv1, n1t, active, slope), out_pieces, (d_resid2, d_outer, small2) = ffn_forward(
            flat,
            context,
            output_weight,
            vecs,
            inner_weight,
            inner_bias.astype(f32)[None],
            outer_weight,
            cot_pieces,
            rows_dev,
        )
        out_pieces = [swap_seq(p, k) if k else p for k, p in enumerate(out_pieces)]
        layer_out = finish_rows(me, jnp.ones((1,), f32), out_pieces, bf16)

        aligned = (width // ndp) % 16 == 0 and (ff // (ndp * nseq)) % 16 == 0 and ff // nseq == BLOCK
        if aligned:
            keep, send = ffn_outer_grad(plan, me, active, d_outer, small2)
        else:
            grad = dot(active, d_outer, 0, 0).astype(bf16)
            below = jnp.broadcast_to(count_bits(small2[3:4]), (ndp, nseq, EXTRA, width)).astype(bf16)
            blocks = jnp.concatenate([grad.reshape(ndp, nseq, -1, width), below], axis=2)
            keep, send = place_pieces(plan, me, blocks)
        d_outer, keep, send = lax.optimization_barrier((d_outer, keep, send))
        outer = start_chunk(keep, send)
        if aligned:
            keep, send, d_resid1, d_attn, d_context, d_inner_bias, small1 = ffn_backward(
                plan, me, slope, d_outer, outer_weight, inner_weight, n1t, d_resid2, hat1, inv1, vecs[1:2], output_weight
            )
        else:
            d_inner = (dot(d_outer, outer_weight, 1, 1) * slope.astype(f32)).astype(bf16)
            d_inner_bias = jnp.broadcast_to(jnp.sum(d_inner.astype(f32), axis=0), (8, ff))
            grad = dot(n1t, d_inner, 1, 0).astype(bf16)
            grad = grad.reshape(ndp, width // ndp, nseq, ff // nseq).transpose(0, 2, 1, 3)
            keep, send = place_pieces(plan, me, grad)
            d_normed = dot(d_inner, inner_weight, 1, 1) + d_resid2
            d_resid1 = normalize_back(hat1, inv1[:, 0:1], d_normed * vecs[1:2])
            d_attn = d_resid1.astype(bf16)
            d_context = dot(d_attn, output_weight, 1, 1).astype(bf16)
            small1 = rows_of(d_normed * hat1, d_normed, d_attn.astype(f32))
        inner = start_chunk(keep, send)
        outer = step_chunk(outer, 0)
        d_queries, d_keys, d_values = attention_backward(
            queries, keys, values, context, d_context, probs, 1, rows
        )
        outer = step_chunk(outer, 1)
        inner = step_chunk(inner, 0)
        cut_pieces, small = inputs_backward(
            me,
            (d_queries, d_keys, d_values),
            (query_weight, key_weight, value_weight),
            d_resid1,
            small1,
            small2,
            d_inner_bias,
            rows_dev,
            nseq,
            mem_rows,
        )
        cut_pieces = [swap_seq(p, k) if k else p for k, p in enumerate(cut_pieces)]
        ib_rows = ff // width
        attn_grads = (d_queries, d_keys, d_values, d_attn)
        if aligned:
            keep, send = attn_weight_grads(plan, me, flat, context, attn_grads, small)
        else:
            blocks = []
            for s, d in enumerate(attn_grads):
                left = context if s == 3 else flat
                blocks.append(dot(left, d, 0, 0).astype(bf16).reshape(ndp, -1, width))
            blocks = jnp.stack(blocks, axis=1)
            below = jnp.broadcast_to(small.astype(bf16)[None], (ndp,) + small.shape)
            keep, send = place_pieces(plan, me, jnp.concatenate([blocks, below], axis=2))
        attn = start_chunk(keep, send)
        for step in range(2, plan.steps):
            outer = step_chunk(outer, step)
        for step in range(1, plan.steps):
            inner = step_chunk(inner, step)
        for step in range(plan.steps):
            attn = step_chunk(attn, step)
        outer_rows = ff // (ndp * nseq)
        outer = total_of(outer)[0]
        total = jnp.sum(outer[outer_rows, :DIGITS] * (2.0 ** jnp.arange(DIGITS)).astype(f32))
        factor = total / segs_total
        ffn_near, ffn_far = gather_seq(jnp.concatenate([outer[:outer_rows], total_of(inner)[0]], axis=0).astype(bf16))
        attn_near, attn_far = gather_seq(total_of(attn)[0].astype(bf16))

        part = width // ndp
        scale = factor.reshape(1)
        if aligned:
            tokens_grad = finish_rows(me, scale, cut_pieces, f32)
            g_outer, g_inner = finish_weights(
                me, scale, ffn_near, ffn_far, [(0, outer_rows, 0), (outer_rows, part, 1)], ndp
            )
            got = finish_weights(
                me, scale, attn_near, attn_far, [(0, part, None), (part, EXTRA, None), (part, EXTRA, "dp")], ndp
            )
            g_query, g_key, g_value, g_output = got[:4]
            small_parts = got[4:8]
            small_cols = got[8]
        else:
            finish = lambda x: x.astype(f32) * factor
            tokens_grad = to_rows(cut_pieces, finish)

            def in_order(near, far):
                stack = jnp.stack([near[0], far[0], near[1], far[1]])
                return [finish(lax.dynamic_index_in_dim(stack, seq_index ^ k, 0, keepdims=False)) for k in range(nseq)]

            ffn_parts = in_order(ffn_near, ffn_far)
            g_outer = jnp.concatenate([p[:outer_rows] for p in ffn_parts], axis=0)
            g_inner = jnp.concatenate([p[outer_rows:] for p in ffn_parts], axis=1)
            attn_parts = in_order(attn_near, attn_far)
            g_query, g_key, g_value, g_output = [p[:part] for p in attn_parts]
            small_parts = [p[part:] for p in attn_parts]
            small_cols = lax.dynamic_slice_in_dim(jnp.stack(small_parts), dp_index * part, part, axis=2)
        vec_rows = small_cols[0]
        g_memory = jnp.concatenate([small_cols[2], small_cols[3]])[:mem_rows].T
        inner_part = ff // ndp
        g_inner_bias = lax.dynamic_slice_in_dim(
            small_parts[1][:ib_rows].reshape(-1), dp_index * inner_part, inner_part, axis=0
        )
        g_query_bias, g_value_bias, g_gain1, g_shift1, g_output_bias, g_gain2, g_shift2, g_outer_bias = vec_rows
        return (
            layer_out,
            tokens_grad,
            g_query,
            g_query_bias,
            g_key,
            g_value,
            g_value_bias,
            g_output,
            g_output_bias,
            g_gain1,
            g_shift1,
            g_inner,
            g_inner_bias,
            g_outer,
            g_outer_bias,
            g_gain2,
            g_shift2,
            g_memory,
        )

    return per_device


def solution(mesh):
    rows = P("dp", "seq", None)
    in_specs = (rows,) + (P(),) * 16 + (rows, P("dp", "seq"), P())
    out_specs = (
        rows,
        rows,
        P("dp", None),
        P("dp"),
        P("dp", None),
        P("dp", None),
        P("dp"),
        P("dp", None),
        P("dp"),
        P("dp"),
        P("dp"),
        P("dp", None),
        P("dp"),
        P("dp", None),
        P("dp"),
        P("dp"),
        P("dp"),
        P("dp", None),
    )
    return jax.shard_map(
        make_per_device(mesh), mesh=mesh, in_specs=in_specs, out_specs=out_specs, check_vma=False
    )
```

```python
import jax
import jax.numpy as jnp
from jax import lax
from jax.experimental import pallas as pl
from jax.experimental.pallas import tpu as pltpu
from jax.sharding import PartitionSpec as P


HEAD_DIM = 64
EPS = 1e-06
LOG2E = 1.4426950408889634
BLOCK = 768
PART = 768
DIGITS = 16
EXTRA = 8
f32 = jnp.float32
bf16 = jnp.bfloat16


def dot(a, b, ca, cb):
    return lax.dot_general(a, b, (((ca,), (cb,)), ((), ())), preferred_element_type=f32)


def attn_fwd_kernel(q_ref, k_ref, v_ref, ctx_ref, p_ref):
    q = q_ref[...]
    k = k_ref[...]
    v = v_ref[...]
    lanes = lax.broadcasted_iota(jnp.int32, (1, 2 * HEAD_DIM), 1)
    ctx = None
    for h in range(2):
        mask = (lanes // HEAD_DIM) == h
        kh = jnp.where(mask, k, jnp.zeros_like(k))
        vh = jnp.where(mask, v, jnp.zeros_like(v))
        s = dot(q, kh, 1, 1) * (HEAD_DIM ** (-0.5) * LOG2E)
        e = jnp.exp2(s - jnp.max(s, axis=-1, keepdims=True))
        p = (e * (1.0 / jnp.sum(e, axis=-1, keepdims=True))).astype(bf16)
        p_ref[h] = p
        c = dot(p, vh, 1, 0)
        ctx = c if ctx is None else ctx + c
    ctx_ref[...] = ctx.astype(bf16)


def attn_bwd_kernel(q_ref, k_ref, v_ref, ctx_ref, dctx_ref, p_ref, dq_ref, dk_ref, dv_ref):
    q = q_ref[...]
    k = k_ref[...]
    v = v_ref[...]
    dctx = dctx_ref[...]
    prod = dctx.astype(f32) * ctx_ref[...].astype(f32)
    lanes = lax.broadcasted_iota(jnp.int32, (1, 2 * HEAD_DIM), 1)
    scale = HEAD_DIM ** (-0.5)
    dq = None
    dk = None
    dv = None
    for h in range(2):
        mask = (lanes // HEAD_DIM) == h
        zero = jnp.zeros_like(k)
        vh = jnp.where(mask, v, zero)
        kh = jnp.where(mask, k, zero)
        qh = jnp.where(mask, q, zero)
        dh = jnp.where(mask, dctx, zero)
        delta = jnp.sum(jnp.where(mask, prod, 0.0), axis=-1, keepdims=True)
        p = p_ref[h]
        dp = dot(dctx, vh, 1, 1)
        ds = (p.astype(f32) * (dp - delta)).astype(bf16)
        dqh = dot(ds, kh, 1, 0)
        dkh = dot(ds, qh, 0, 0)
        dvh = dot(p, dh, 0, 0)
        dq = dqh if dq is None else dq + dqh
        dk = dkh if dk is None else dk + dkh
        dv = dvh if dv is None else dv + dvh
    dq_ref[...] = (dq * scale).astype(bf16)
    dk_ref[...] = (dk * scale).astype(bf16)
    dv_ref[...] = dv.astype(bf16)


def attention_forward(q, k, v, segs, rows):
    block = 2 * HEAD_DIM
    pairs = q.shape[1] // block
    spec = pl.BlockSpec((rows, block), lambda s, h: (s, h))
    pspec = pl.BlockSpec((2, rows, rows), lambda s, h: (s * pairs + h, 0, 0))
    return pl.pallas_call(
        attn_fwd_kernel,
        grid=(segs, pairs),
        in_specs=[spec, spec, spec],
        out_specs=[spec, pspec],
        out_shape=[
            jax.ShapeDtypeStruct(q.shape, bf16),
            jax.ShapeDtypeStruct((segs * 2 * pairs, rows, rows), bf16),
        ],
        name="attn_fwd",
    )(q, k, v)


def attention_backward(q, k, v, ctx, dctx, p, segs, rows):
    block = 2 * HEAD_DIM
    pairs = q.shape[1] // block
    spec = pl.BlockSpec((rows, block), lambda s, h: (s, h))
    pspec = pl.BlockSpec((2, rows, rows), lambda s, h: (s * pairs + h, 0, 0))
    shape = jax.ShapeDtypeStruct(q.shape, bf16)
    return pl.pallas_call(
        attn_bwd_kernel,
        grid=(segs, pairs),
        in_specs=[spec] * 5 + [pspec],
        out_specs=[spec] * 3,
        out_shape=[shape] * 3,
        name="attn_bwd",
    )(q, k, v, ctx, dctx, p)


def upper_tail(x):
    z = jnp.abs(x) * (0.5 ** 0.5)
    t = 1.0 / (1.0 + 0.5 * z)
    poly = 0.17087277
    for c in (
        -0.82215223,
        1.48851587,
        -1.13520398,
        0.27886807,
        -0.18628806,
        0.09678418,
        0.37409196,
        1.00002368,
        -1.26551223,
    ):
        poly = poly * t + c
    bell = jnp.exp(-0.5 * x * x)
    half = 0.5 * t * bell * jnp.exp(poly)
    return jnp.where(x >= 0, 1.0 - half, half), bell


def normalize(values):
    center = values - jnp.mean(values, axis=-1, keepdims=True)
    inv = lax.rsqrt(jnp.mean(center * center, axis=-1, keepdims=True) + EPS)
    return center * inv, inv


def normalize_back(hat, inv, g):
    a = jnp.mean(g, axis=-1, keepdims=True)
    b = jnp.mean(g * hat, axis=-1, keepdims=True)
    return inv * (g - a - hat * b)


def rows_of(*vectors):
    lines = [jnp.sum(v, axis=0, keepdims=True) for v in vectors]
    pad = 8 - len(lines)
    return jnp.concatenate(lines + [jnp.zeros((pad, lines[0].shape[1]), f32)], axis=0)


def ffn_forward(flat, ctx, wout, vecs, wi, ib, wo, cot_pieces, rows_dev):
    n, width = flat.shape
    inner = wi.shape[1]
    count = len(cot_pieces)

    def kernel(flat_ref, ctx_ref, wout_ref, vec_ref, wi_ref, ib_ref, wo_ref, *refs):
        cot_refs = refs[:count]
        hat1_ref, inv1_ref, n1t_ref, active_ref, slope_ref = refs[count : count + 5]
        out_refs = refs[count + 5 : 2 * count + 5]
        dres_ref, douter_ref, small_ref, low, acc = refs[2 * count + 5 :]
        j = pl.program_id(0)

        @pl.when(j == 0)
        def _():
            resid = flat_ref[...].astype(f32) + dot(ctx_ref[...], wout_ref[...], 1, 0) + vec_ref[0:1]
            hat, inv = normalize(resid)
            hat1_ref[...] = hat
            inv1_ref[...] = jnp.broadcast_to(inv, inv1_ref.shape)
            normed = hat * vec_ref[1:2] + vec_ref[2:3]
            low[...] = normed.astype(bf16)
            n1t_ref[...] = normed.astype(bf16).T
            acc[...] = normed + vec_ref[3:4]

        left = low[...]
        total = acc[...]
        for c in range(0, BLOCK, PART):
            part = slice(c, c + PART)
            inner = dot(left, wi_ref[:, part], 1, 0) + ib_ref[:, part]
            cdf, bell = upper_tail(inner)
            active = (inner * cdf).astype(bf16)
            active_ref[:, part] = active
            slope_ref[:, part] = (cdf + inner * bell * 0.3989422804014327).astype(bf16)
            total = total + dot(active, wo_ref[part], 1, 0)
        acc[...] = total

        @pl.when(j == pl.num_programs(0) - 1)
        def _():
            valid_rows = cot_refs[0][rows_dev : rows_dev + EXTRA].astype(f32)[0:1]
            for r in cot_refs[1:]:
                valid_rows = valid_rows + r[rows_dev : rows_dev + EXTRA].astype(f32)[0:1]
            scale = 1.0 / jnp.maximum(valid_rows, 1.0)
            lines = [valid_rows * 0.0] * 3
            for k in range(count):
                part = slice(k * rows_dev, (k + 1) * rows_dev)
                hat, inv = normalize(acc[part])
                out_refs[k][...] = (hat * vec_ref[4:5] + vec_ref[5:6]).astype(bf16)
                cot = cot_refs[k][0:rows_dev].astype(f32) * scale
                dres = normalize_back(hat, inv, cot * vec_ref[4:5])
                dres_ref[part] = dres
                low_d = dres.astype(bf16)
                douter_ref[part] = low_d
                for i, v in enumerate((cot * hat, cot, low_d.astype(f32))):
                    lines[i] = lines[i] + jnp.sum(v, axis=0, keepdims=True)
            for i, v in enumerate(lines + [valid_rows]):
                small_ref[i : i + 1] = v

    full = lambda a: pl.BlockSpec(a.shape, lambda j: (0,) * a.ndim)
    whole = lambda shape: pl.BlockSpec(shape, lambda j: (0,) * len(shape))
    cols = pl.BlockSpec((n, BLOCK), lambda j: (0, j))
    outs = [
        (whole, (n, width), f32),
        (whole, (n, 128), f32),
        (whole, (width, n), bf16),
        (None, (n, inner), bf16),
        (None, (n, inner), bf16),
    ]
    outs += [(whole, (rows_dev, width), bf16)] * count
    outs += [(whole, (n, width), f32), (whole, (n, width), bf16), (whole, (8, width), f32)]
    got = pl.pallas_call(
        kernel,
        grid=(inner // BLOCK,),
        in_specs=[
            full(flat),
            full(ctx),
            full(wout),
            full(vecs),
            pl.BlockSpec((width, BLOCK), lambda j: (0, j)),
            pl.BlockSpec((1, BLOCK), lambda j: (0, j)),
            pl.BlockSpec((BLOCK, width), lambda j: (j, 0)),
        ]
        + [full(c) for c in cot_pieces],
        out_specs=[spec(shape) if spec else cols for spec, shape, _ in outs],
        out_shape=[jax.ShapeDtypeStruct(shape, kind) for _, shape, kind in outs],
        scratch_shapes=[pltpu.VMEM((n, width), bf16), pltpu.VMEM((n, width), f32)],
        name="ffn_fwd",
    )(flat, ctx, wout, vecs, wi, ib, wo, *cot_pieces)
    return got[:5], got[5 : 5 + count], got[5 + count :]


def inputs_backward(me, grads, weights, d_resid1, small1, small2, d_inner_bias, rows_dev, nseq, mem_rows):
    _, width = d_resid1.shape
    ib_rows = d_inner_bias.shape[1] // width

    def kernel(me_ref, dq_ref, dk_ref, dv_ref, wq_ref, wk_ref, wv_ref, dres_ref, s1_ref, s2_ref, ib_ref, *outs):
        pieces, small_ref = outs[:nseq], outs[nseq]
        seq_me = me_ref[1]
        first = me_ref[2]
        small_ref[...] = jnp.zeros_like(small_ref)
        d = dres_ref[...]
        for g, w in ((dq_ref, wq_ref), (dk_ref, wk_ref), (dv_ref, wv_ref)):
            d = d + dot(g[...], w[...], 1, 1)
        row = lax.broadcasted_iota(jnp.int32, (rows_dev, 1), 0)
        memory = jnp.zeros((2 * EXTRA, width), f32)
        for k in range(nseq):
            part = d[k * rows_dev : (k + 1) * rows_dev]
            is_mem = jnp.logical_and(row < mem_rows, jnp.logical_and(seq_me == k, first != 0))
            pieces[k][...] = jnp.where(is_mem, 0.0, part).astype(bf16)
            memory = memory + jnp.where(is_mem[: 2 * EXTRA], part[: 2 * EXTRA], 0.0)
        small_ref[0, 0:1] = jnp.sum(dq_ref[...].astype(f32), axis=0, keepdims=True)
        small_ref[0, 1:2] = jnp.sum(dv_ref[...].astype(f32), axis=0, keepdims=True)
        small_ref[0, 2:5] = s1_ref[0:3]
        small_ref[0, 5:8] = s2_ref[0:3]
        for r in range(ib_rows):
            small_ref[1, r : r + 1] = ib_ref[0:1, r * width : (r + 1) * width]
        small_ref[2] = memory[:EXTRA]
        small_ref[3] = memory[EXTRA:]

    vmem = pl.BlockSpec(memory_space=pltpu.VMEM)
    got = pl.pallas_call(
        kernel,
        in_specs=[pl.BlockSpec(memory_space=pltpu.SMEM)] + [vmem] * 10,
        out_specs=[vmem] * (nseq + 1),
        out_shape=[jax.ShapeDtypeStruct((rows_dev, width), bf16)] * nseq
        + [jax.ShapeDtypeStruct((nseq, EXTRA, width), f32)],
        name="inputs_bwd",
    )(me, *grads, *weights, d_resid1, small1, small2, d_inner_bias)
    return got[:nseq], got[nseq]


class Plan:
    def __init__(self, mesh):
        self.ndp, self.nseq = mesh.shape["dp"], mesh.shape["seq"]
        bits = [("seq", b) for b in range(self.nseq.bit_length() - 1)]
        dp_bits = [("dp", b) for b in range(self.ndp.bit_length() - 1)]
        assert 2 ** len(bits) == self.nseq and 2 ** len(dp_bits) == self.ndp
        rest = bits[2:] + dp_bits[1:]
        self.first = bits[0]
        self.orders = [[bits[1], dp_bits[0]] + rest, [dp_bits[0]] + rest + [bits[1]]]
        self.steps = len(self.orders[0])
        self.places = 1 << self.steps

    def flip(self, device, which):
        axis, b = which
        return device ^ ((1 << b) * (self.nseq if axis == "dp" else 1))

    def perm(self, step):
        devices = range(self.ndp * self.nseq)
        if step < 0:
            return [(d, self.flip(d, self.first)) for d in devices]
        return [(d, self.flip(d, self.orders[d & 1][step])) for d in devices]

    def place(self, dp_diff, seq_diff, half):
        value = {"dp": dp_diff, "seq": seq_diff}
        places = []
        for order in self.orders:
            p = 0
            for axis, b in order:
                p = p * 2 + ((value[axis] >> b) & 1)
            places.append(p)
        return jnp.where(half == 0, places[0], places[1])


def scatter_pieces(plan, me_ref, result, pieces, keep_ref, send_ref, rows, offset=0):
    dp_me = me_ref[0]
    seq_me = me_ref[1]
    for i, (dp, seq) in enumerate(pieces):
        tile = result[i * rows : (i + 1) * rows].astype(bf16)
        half = seq & 1
        at = plan.place(dp ^ dp_me, seq ^ seq_me, half)
        stay = half == (seq_me & 1)

        @pl.when(stay)
        def _(tile=tile, at=at):
            keep_ref[at, offset : offset + rows] = tile

        @pl.when(jnp.logical_not(stay))
        def _(tile=tile, at=at):
            send_ref[at, offset : offset + rows] = tile


def count_bits(count_row):
    lane = lax.broadcasted_iota(jnp.int32, count_row.shape, 1)
    return ((count_row.astype(jnp.int32) >> jnp.minimum(lane, DIGITS)) & 1).astype(f32)


def ffn_outer_grad(plan, me, active, d_outer, small2):
    n, inner = active.shape
    width = d_outer.shape[1]
    rows = inner // (plan.ndp * plan.nseq)
    per = BLOCK // rows

    def kernel(me_ref, active_ref, d_ref, small_ref, keep_ref, send_ref):
        j = pl.program_id(0)

        @pl.when(j == 0)
        def _():
            below = jnp.broadcast_to(count_bits(small_ref[3:4]), (EXTRA, width)).astype(bf16)
            for p in range(plan.places):
                keep_ref[p, rows:] = below
                send_ref[p, rows:] = below

        result = dot(active_ref[...], d_ref[...], 0, 0)
        pieces = [((j * per + i) // plan.nseq, (j * per + i) % plan.nseq) for i in range(per)]
        scatter_pieces(plan, me_ref, result, pieces, keep_ref, send_ref, rows)

    shape = jax.ShapeDtypeStruct((plan.places, rows + EXTRA, width), bf16)
    spec = pl.BlockSpec(shape.shape, lambda j, m: (0, 0, 0))
    return pl.pallas_call(
        kernel,
        grid_spec=pltpu.PrefetchScalarGridSpec(
            num_scalar_prefetch=1,
            grid=(inner // BLOCK,),
            in_specs=[
                pl.BlockSpec((n, BLOCK), lambda j, m: (0, j)),
                pl.BlockSpec((n, width), lambda j, m: (0, 0)),
                pl.BlockSpec(small2.shape, lambda j, m: (0, 0)),
            ],
            out_specs=[spec, spec],
        ),
        out_shape=[shape, shape],
        name="outer_grad",
    )(me, active, d_outer, small2)


def ffn_backward(plan, me, slope, d_outer, wo, wi, n1t, d_resid2, hat1, inv1, gain1, wout):
    n, inner = slope.shape
    width = d_outer.shape[1]
    rows = width // plan.ndp
    cols = inner // plan.nseq

    def kernel(
        me_ref, slope_ref, douter_ref, wo_ref, wi_ref, n1t_ref, dres2_ref, hat1_ref, inv1_ref, gain_ref, wout_ref,
        keep_ref, send_ref, dres1_ref, dattn_ref, dctx_ref, ib_ref, small_ref, acc,
    ):
        j = pl.program_id(0)
        d_active = dot(douter_ref[...], wo_ref[...], 1, 1)
        d_inner = (d_active * slope_ref[...].astype(f32)).astype(bf16)
        ib_ref[...] = jnp.broadcast_to(jnp.sum(d_inner.astype(f32), axis=0, keepdims=True), ib_ref.shape)
        result = dot(n1t_ref[...], d_inner, 1, 0)
        scatter_pieces(plan, me_ref, result, [(i, j) for i in range(plan.ndp)], keep_ref, send_ref, rows)
        back = dot(d_inner, wi_ref[...], 1, 1)

        @pl.when(j == 0)
        def _():
            acc[...] = dres2_ref[...] + back

        @pl.when(j > 0)
        def _():
            acc[...] += back

        @pl.when(j == pl.num_programs(0) - 1)
        def _():
            d_normed = acc[...]
            hat = hat1_ref[...]
            dres = normalize_back(hat, inv1_ref[:, 0:1], d_normed * gain_ref[...])
            dres1_ref[...] = dres
            low = dres.astype(bf16)
            dattn_ref[...] = low
            dctx_ref[...] = dot(low, wout_ref[...], 1, 1).astype(bf16)
            small_ref[...] = rows_of(d_normed * hat, d_normed, low.astype(f32))

    full = lambda a: pl.BlockSpec(a.shape, lambda j, m: (0,) * a.ndim)
    whole = lambda shape: pl.BlockSpec(shape, lambda j, m: (0,) * len(shape))
    chunk = jax.ShapeDtypeStruct((plan.places, rows, cols), bf16)
    return pl.pallas_call(
        kernel,
        grid_spec=pltpu.PrefetchScalarGridSpec(
            num_scalar_prefetch=1,
            grid=(plan.nseq,),
            in_specs=[
                pl.BlockSpec((n, cols), lambda j, m: (0, j)),
                full(d_outer),
                pl.BlockSpec((cols, width), lambda j, m: (j, 0)),
                pl.BlockSpec((width, cols), lambda j, m: (0, j)),
                full(n1t),
                full(d_resid2),
                full(hat1),
                full(inv1),
                full(gain1),
                full(wout),
            ],
            out_specs=[
                whole(chunk.shape),
                whole(chunk.shape),
                whole((n, width)),
                whole((n, width)),
                whole((n, width)),
                pl.BlockSpec((8, cols), lambda j, m: (0, j)),
                whole((8, width)),
            ],
            scratch_shapes=[pltpu.VMEM((n, width), f32)],
        ),
        out_shape=[
            chunk,
            chunk,
            jax.ShapeDtypeStruct((n, width), f32),
            jax.ShapeDtypeStruct((n, width), bf16),
            jax.ShapeDtypeStruct((n, width), bf16),
            jax.ShapeDtypeStruct((8, inner), f32),
            jax.ShapeDtypeStruct((8, width), f32),
        ],
        name="ffn_bwd",
    )(me, slope, d_outer, wo, wi, n1t, d_resid2, hat1, inv1, gain1, wout)


def finish_rows(me, factor, pieces, kind):
    count = len(pieces)

    def kernel(me_ref, factor_ref, *refs):
        out_ref = refs[count]
        for k in range(count):
            piece = refs[k][...]
            out_ref[me_ref[1] ^ k] = piece if piece.dtype == kind else piece.astype(f32) * factor_ref[0]

    smem = pl.BlockSpec(memory_space=pltpu.SMEM)
    vmem = pl.BlockSpec(memory_space=pltpu.VMEM)
    return pl.pallas_call(
        kernel,
        in_specs=[smem, smem] + [vmem] * count,
        out_specs=vmem,
        out_shape=jax.ShapeDtypeStruct((count,) + pieces[0].shape, kind),
    )(me, factor, *pieces)


def finish_weights(me, factor, near, far, split, ndp):
    width = near.shape[2]
    count = 4
    shapes = []
    for start, rows, axis in split:
        if axis is None:
            shapes += [(rows, width)] * count
        elif axis == "dp":
            shapes.append((count, rows, width // ndp))
        else:
            shapes.append((count * rows, width) if axis == 0 else (rows, count * width))

    def kernel(me_ref, factor_ref, near_ref, far_ref, *outs):
        if any(axis == "dp" for _, _, axis in split):
            shape = (width, width // ndp)
            column = lax.broadcasted_iota(jnp.int32, shape, 1) + me_ref[0] * (width // ndp)
            pick = (lax.broadcasted_iota(jnp.int32, shape, 0) == column).astype(f32).astype(bf16)
        for s in range(count):
            diff = me_ref[1] ^ s
            at = diff >> 1
            o = 0
            for start, rows, axis in split:
                part = slice(start, start + rows)
                value = jnp.where((diff & 1) == 0, near_ref[at, part], far_ref[at, part])
                if axis == "dp":
                    outs[o][s] = dot(value, pick, 1, 0) * factor_ref[0]
                    o += 1
                    continue
                value = value.astype(f32) * factor_ref[0]
                if axis is None:
                    outs[o + s][...] = value
                    o += count
                elif axis == 0:
                    outs[o][s * rows : (s + 1) * rows] = value
                    o += 1
                else:
                    outs[o][:, s * width : (s + 1) * width] = value
                    o += 1

    smem = pl.BlockSpec(memory_space=pltpu.SMEM)
    vmem = pl.BlockSpec(memory_space=pltpu.VMEM)
    return pl.pallas_call(
        kernel,
        in_specs=[smem, smem, vmem, vmem],
        out_specs=[vmem] * len(shapes),
        out_shape=[jax.ShapeDtypeStruct(shape, f32) for shape in shapes],
    )(me, factor, near, far)


def attn_weight_grads(plan, me, flat, ctx, grads, small):
    n, width = flat.shape
    rows = width // plan.ndp

    def kernel(me_ref, flat_ref, ctx_ref, d0_ref, d1_ref, d2_ref, d3_ref, small_ref, keep_ref, send_ref, flat_t, ctx_t):
        flat_t[...] = flat_ref[...].T
        ctx_t[...] = ctx_ref[...].T
        for s, d_ref in enumerate((d0_ref, d1_ref, d2_ref, d3_ref)):
            left = ctx_t if s == 3 else flat_t
            result = dot(left[...], d_ref[...], 1, 0)
            pieces = [(i, s) for i in range(plan.ndp)]
            scatter_pieces(plan, me_ref, result, pieces, keep_ref, send_ref, rows)
            below = jnp.concatenate([small_ref[s].astype(bf16)] * plan.ndp, axis=0)
            scatter_pieces(plan, me_ref, below, pieces, keep_ref, send_ref, EXTRA, rows)

    shape = jax.ShapeDtypeStruct((plan.places, rows + EXTRA, width), bf16)
    return pl.pallas_call(
        kernel,
        in_specs=[pl.BlockSpec(memory_space=pltpu.SMEM)] + [pl.BlockSpec(memory_space=pltpu.VMEM)] * 7,
        out_specs=[pl.BlockSpec(memory_space=pltpu.VMEM)] * 2,
        out_shape=[shape, shape],
        scratch_shapes=[pltpu.VMEM((width, n), bf16), pltpu.VMEM((width, n), bf16)],
        name="attn_grad",
    )(me, flat, ctx, *grads, small)


def place_pieces(plan, me, blocks):
    dp = jnp.repeat(jnp.arange(plan.ndp), plan.nseq)
    seq = jnp.tile(jnp.arange(plan.nseq), plan.ndp)
    half = seq & 1
    place = plan.place(dp ^ me[0], seq ^ me[1], half)
    away = half ^ (me[1] & 1)
    flat = blocks.reshape((plan.ndp * plan.nseq,) + blocks.shape[2:])
    order = jnp.zeros((2 * plan.places,), jnp.int32).at[away * plan.places + place].set(jnp.arange(dp.shape[0]))
    both = jnp.take(flat, order, axis=0)
    return both[: plan.places], both[plan.places :]


def make_per_device(mesh):
    plan = Plan(mesh)
    ndp, nseq = plan.ndp, plan.nseq
    devices = ("dp", "seq")
    sent = {}

    def total_of(terms):
        total = terms[0].astype(f32)
        for t in terms[1:]:
            total = total + t.astype(f32)
        return total

    def start_chunk(keep, send):
        return [keep, lax.ppermute(send, devices, plan.perm(-1))]

    def step_chunk(name, terms, step):
        half = terms[0].shape[0] // 2
        send = total_of([t[half:] for t in terms]).astype(bf16)
        sent.setdefault(name, []).append(send)
        got = lax.ppermute(send, devices, plan.perm(step))
        return [t[:half] for t in terms] + [got]

    def swap_seq(x, k):
        return lax.ppermute(x, "seq", [(i, i ^ k) for i in range(nseq)])

    def gather_seq(x):
        assert nseq == 4
        near = jnp.stack([x, swap_seq(x, 2)])
        return near, swap_seq(near, 1)

    def per_device(
        tokens,
        memory_init,
        query_weight,
        query_bias,
        key_weight,
        value_weight,
        value_bias,
        output_weight,
        output_bias,
        attn_gain,
        attn_shift,
        inner_weight,
        inner_bias,
        outer_weight,
        outer_bias,
        ffn_gain,
        ffn_shift,
        out_grad,
        lm_mask,
        doc_segments,
    ):
        sent.clear()
        seg_dev, rows_dev, width = tokens.shape
        assert rows_dev * nseq < (1 << DIGITS) and ndp * nseq <= 256
        assert seg_dev == nseq
        rows = rows_dev * nseq
        mem_rows = memory_init.shape[1]
        ff = inner_weight.shape[1]
        seq_index = lax.axis_index("seq")
        dp_index = lax.axis_index("dp")
        segs_total = ndp * seg_dev

        def to_segments(x):
            pieces = [lax.dynamic_index_in_dim(x, seq_index ^ k, axis=0, keepdims=False) for k in range(nseq)]
            return [swap_seq(p, k) if k else p for k, p in enumerate(pieces)], pieces

        def to_rows(pieces, finish):
            out = None
            for k in range(nseq):
                piece = finish(pieces[k])
                if out is None:
                    out = jnp.zeros((nseq,) + piece.shape, piece.dtype)
                out = lax.dynamic_update_index_in_dim(out, piece, seq_index ^ k, axis=0)
            return out

        source = seq_index ^ jnp.arange(nseq, dtype=jnp.int32)
        position = source[:, None] * rows_dev + jnp.arange(rows_dev, dtype=jnp.int32)[None, :]
        is_mem = (position < mem_rows).reshape(rows)
        pieces, sliced = to_segments(tokens)
        raw = jnp.concatenate(pieces, axis=0)
        out_grad, lm_mask, *_ = lax.optimization_barrier((out_grad, lm_mask, *sliced))

        here = seq_index * rows_dev + jnp.arange(rows_dev, dtype=jnp.int32)
        valid = jnp.where((here < mem_rows)[None, :], 0, lm_mask)
        counts_here = jnp.sum(valid, axis=1)
        masked = jnp.where(valid[..., None] != 0, out_grad, jnp.zeros_like(out_grad))
        assert rows_dev <= 256
        count_rows = jnp.broadcast_to(counts_here.astype(bf16)[:, None, None], (seg_dev, EXTRA, width))
        cot_pieces, _ = to_segments(jnp.concatenate([masked, count_rows], axis=1))

        seg_global = dp_index * seg_dev + seq_index
        starts = jnp.cumsum(doc_segments) - doc_segments
        is_first = jnp.any(starts == seg_global)
        me = jnp.stack([dp_index, seq_index, is_first.astype(jnp.int32)]).astype(jnp.int32)
        select = (is_first & is_mem)[:, None]
        table = jnp.concatenate([memory_init.T, jnp.zeros((rows_dev - mem_rows, width), bf16)], axis=0)
        table = jnp.concatenate([table] * nseq, axis=0)
        flat = jnp.where(select, table, raw)

        queries = (dot(flat, query_weight, 1, 0) + query_bias.astype(f32)).astype(bf16)
        keys = dot(flat, key_weight, 1, 0).astype(bf16)
        values = (dot(flat, value_weight, 1, 0) + value_bias.astype(f32)).astype(bf16)
        context, probs = attention_forward(queries, keys, values, 1, rows)
        zero = jnp.zeros_like(output_bias)
        vecs = jnp.stack(
            [output_bias, attn_gain, attn_shift, outer_bias, ffn_gain, ffn_shift, zero, zero]
        ).astype(f32)
        (hat1, inv1, n1t, active, slope), out_pieces, (d_resid2, d_outer, small2) = ffn_forward(
            flat,
            context,
            output_weight,
            vecs,
            inner_weight,
            inner_bias.astype(f32)[None],
            outer_weight,
            cot_pieces,
            rows_dev,
        )
        out_pieces = [swap_seq(p, k) if k else p for k, p in enumerate(out_pieces)]
        layer_out = finish_rows(me, jnp.ones((1,), f32), out_pieces, bf16)

        aligned = (width // ndp) % 16 == 0 and (ff // (ndp * nseq)) % 16 == 0 and ff // nseq == BLOCK
        if aligned:
            keep, send = ffn_outer_grad(plan, me, active, d_outer, small2)
        else:
            grad = dot(active, d_outer, 0, 0).astype(bf16)
            below = jnp.broadcast_to(count_bits(small2[3:4]), (ndp, nseq, EXTRA, width)).astype(bf16)
            blocks = jnp.concatenate([grad.reshape(ndp, nseq, -1, width), below], axis=2)
            keep, send = place_pieces(plan, me, blocks)
        d_outer, keep, send = lax.optimization_barrier((d_outer, keep, send))
        outer = start_chunk(keep, send)
        if aligned:
            keep, send, d_resid1, d_attn, d_context, d_inner_bias, small1 = ffn_backward(
                plan, me, slope, d_outer, outer_weight, inner_weight, n1t, d_resid2, hat1, inv1, vecs[1:2], output_weight
            )
        else:
            d_inner = (dot(d_outer, outer_weight, 1, 1) * slope.astype(f32)).astype(bf16)
            d_inner_bias = jnp.broadcast_to(jnp.sum(d_inner.astype(f32), axis=0), (8, ff))
            grad = dot(n1t, d_inner, 1, 0).astype(bf16)
            grad = grad.reshape(ndp, width // ndp, nseq, ff // nseq).transpose(0, 2, 1, 3)
            keep, send = place_pieces(plan, me, grad)
            d_normed = dot(d_inner, inner_weight, 1, 1) + d_resid2
            d_resid1 = normalize_back(hat1, inv1[:, 0:1], d_normed * vecs[1:2])
            d_attn = d_resid1.astype(bf16)
            d_context = dot(d_attn, output_weight, 1, 1).astype(bf16)
            small1 = rows_of(d_normed * hat1, d_normed, d_attn.astype(f32))
        inner = start_chunk(keep, send)
        outer = step_chunk("o", outer, 0)
        d_queries, d_keys, d_values = attention_backward(
            queries, keys, values, context, d_context, probs, 1, rows
        )
        outer = step_chunk("o", outer, 1)
        inner = step_chunk("i", inner, 0)
        cut_pieces, small = inputs_backward(
            me,
            (d_queries, d_keys, d_values),
            (query_weight, key_weight, value_weight),
            d_resid1,
            small1,
            small2,
            d_inner_bias,
            rows_dev,
            nseq,
            mem_rows,
        )
        cut_pieces = [swap_seq(p, k) if k else p for k, p in enumerate(cut_pieces)]
        ib_rows = ff // width
        attn_grads = (d_queries, d_keys, d_values, d_attn)
        if aligned:
            keep, send = attn_weight_grads(plan, me, flat, context, attn_grads, small)
        else:
            blocks = []
            for s, d in enumerate(attn_grads):
                left = context if s == 3 else flat
                blocks.append(dot(left, d, 0, 0).astype(bf16).reshape(ndp, -1, width))
            blocks = jnp.stack(blocks, axis=1)
            below = jnp.broadcast_to(small.astype(bf16)[None], (ndp,) + small.shape)
            keep, send = place_pieces(plan, me, jnp.concatenate([blocks, below], axis=2))
        attn = start_chunk(keep, send)
        for step in range(2, plan.steps):
            outer = step_chunk("o", outer, step)
        for step in range(1, plan.steps):
            inner = step_chunk("i", inner, step)
        for step in range(plan.steps):
            attn = step_chunk("t", attn, step)
        *outer, _ = lax.optimization_barrier((*outer, sent["t"][1]))
        *inner, _ = lax.optimization_barrier((*inner, sent["t"][2]))
        outer_rows = ff // (ndp * nseq)
        outer = total_of(outer)[0]
        total = jnp.sum(outer[outer_rows, :DIGITS] * (2.0 ** jnp.arange(DIGITS)).astype(f32))
        factor = total / segs_total
        ffn_near, ffn_far = gather_seq(jnp.concatenate([outer[:outer_rows], total_of(inner)[0]], axis=0).astype(bf16))
        attn_near, attn_far = gather_seq(total_of(attn)[0].astype(bf16))

        part = width // ndp
        scale = factor.reshape(1)
        if aligned:
            tokens_grad = finish_rows(me, scale, cut_pieces, f32)
            g_outer, g_inner = finish_weights(
                me, scale, ffn_near, ffn_far, [(0, outer_rows, 0), (outer_rows, part, 1)], ndp
            )
            got = finish_weights(
                me, scale, attn_near, attn_far, [(0, part, None), (part, EXTRA, None), (part, EXTRA, "dp")], ndp
            )
            g_query, g_key, g_value, g_output = got[:4]
            small_parts = got[4:8]
            small_cols = got[8]
        else:
            finish = lambda x: x.astype(f32) * factor
            tokens_grad = to_rows(cut_pieces, finish)

            def in_order(near, far):
                stack = jnp.stack([near[0], far[0], near[1], far[1]])
                return [finish(lax.dynamic_index_in_dim(stack, seq_index ^ k, 0, keepdims=False)) for k in range(nseq)]

            ffn_parts = in_order(ffn_near, ffn_far)
            g_outer = jnp.concatenate([p[:outer_rows] for p in ffn_parts], axis=0)
            g_inner = jnp.concatenate([p[outer_rows:] for p in ffn_parts], axis=1)
            attn_parts = in_order(attn_near, attn_far)
            g_query, g_key, g_value, g_output = [p[:part] for p in attn_parts]
            small_parts = [p[part:] for p in attn_parts]
            small_cols = lax.dynamic_slice_in_dim(jnp.stack(small_parts), dp_index * part, part, axis=2)
        vec_rows = small_cols[0]
        g_memory = jnp.concatenate([small_cols[2], small_cols[3]])[:mem_rows].T
        inner_part = ff // ndp
        g_inner_bias = lax.dynamic_slice_in_dim(
            small_parts[1][:ib_rows].reshape(-1), dp_index * inner_part, inner_part, axis=0
        )
        g_query_bias, g_value_bias, g_gain1, g_shift1, g_output_bias, g_gain2, g_shift2, g_outer_bias = vec_rows
        return (
            layer_out,
            tokens_grad,
            g_query,
            g_query_bias,
            g_key,
            g_value,
            g_value_bias,
            g_output,
            g_output_bias,
            g_gain1,
            g_shift1,
            g_inner,
            g_inner_bias,
            g_outer,
            g_outer_bias,
            g_gain2,
            g_shift2,
            g_memory,
        )

    return per_device


def solution(mesh):
    rows = P("dp", "seq", None)
    in_specs = (rows,) + (P(),) * 16 + (rows, P("dp", "seq"), P())
    out_specs = (
        rows,
        rows,
        P("dp", None),
        P("dp"),
        P("dp", None),
        P("dp", None),
        P("dp"),
        P("dp", None),
        P("dp"),
        P("dp"),
        P("dp"),
        P("dp", None),
        P("dp"),
        P("dp", None),
        P("dp"),
        P("dp"),
        P("dp"),
        P("dp", None),
    )
    return jax.shard_map(
        make_per_device(mesh), mesh=mesh, in_specs=in_specs, out_specs=out_specs, check_vma=False
    )
```
